32 devices in a mesh: seq: 8 (over z, core), fsdp: 4 (over y, x).
Axes of the slice: x: 2, y: 2, z: 4, core: 2. Of those that a mesh axis runs over, the one named last changes fastest.
Arguments:
- tokens: bfloat16 [4, 2048, 1024], P('fsdp', 'seq'), may hold values from -6 to 6
- seq_lengths: int32 [4, 4], P('fsdp'), may hold values from 1 to 1024, 2048 in all within a row
- seq_order: int32 [4, 2048], P('fsdp'), may hold values from 0 to 2047, each once within a row
- norm_one: bfloat16 [1024], P('fsdp'), may hold values from 0.5 to 1.5
- w_qkv: bfloat16 [1024, 3072], P('fsdp'), may hold values from -0.25 to 0.25
- w_out: bfloat16 [1024, 1024], P('fsdp'), may hold values from -0.75 to 0.75
- norm_two: bfloat16 [1024], P('fsdp'), may hold values from 0.5 to 1.5
- w_in: bfloat16 [1024, 5248], P('fsdp'), may hold values from -0.1875 to 0.1875
- w_down: bfloat16 [2624, 1024], P('fsdp'), may hold values from -0.15625 to 0.15625
- cotangent: bfloat16 [4, 2048, 1024], P('fsdp', 'seq'), may hold values from -6 to 6
Outputs:
- layer_out: bfloat16 [4, 2048, 1024], P('fsdp', 'seq')
- grad_tokens: bfloat16 [4, 2048, 1024], P('fsdp', 'seq')
- grad_norm_one: float32 [1024], P('fsdp')
- grad_w_qkv: float32 [1024, 3072], P('fsdp')
- grad_w_out: float32 [1024, 1024], P('fsdp')
- grad_norm_two: float32 [1024], P('fsdp')
- grad_w_in: float32 [1024, 5248], P('fsdp')
- grad_w_down: float32 [2624, 1024], P('fsdp')
The draws below stay inside these ranges and needn't reach their ends.
Inputs may be any that keep to these rules, and one draw needn't show every extreme that they name: `seq_lengths`: each row holds the lengths of the 4 sequences packed one after another in a group; they sum to 2048 and the longest has exactly 1024 tokens. `seq_order`: each row holds every number of 0 to 2047 once.
All inputs are finite; a program needn't handle non-finite values.
Results may differ from the reference program's by a relative error of at most 0.017.
The reference program's roundings to bfloat16 on the way count: a program that leaves them out, or rounds other values in their place, can miss the bound.
Values may be sent and summed in bfloat16 or wider, within the bound.
No kernel may reach another device: no remote copies, remote signals or barrier semaphores. Data moves between devices by JAX's collectives and lax.ppermute only.
A program may use at most 192 MiB of HBM per device.

```python
import math
import jax
import jax.numpy as jnp
import numpy as np
from jax import lax

D = 1024
H = 16
HD = 64
FF = 2624
NSEQ = 4
GROUP = 2048
MAXLEN = 1024
N_FSDP = 4


def block_levels(rng, shape, pieces, least, top_value):
    loudness, own = 1.0, jax.random.fold_in(rng, 6)
    for axis_at, parts in pieces:
        steps = jnp.exp(jax.random.uniform(jax.random.fold_in(own, axis_at), (parts,), jnp.float32, least / len(pieces), top_value / len(pieces)))
        loudness = loudness * jnp.repeat(steps, shape[axis_at] // parts).reshape([-1 if axis == axis_at else 1 for axis in range(len(shape))])
    return loudness


def length_profile(amount, total, most, slope):
    weights = [(1 << 20) // math.isqrt(standing ** slope) + 1 for standing in range(2, amount + 1)]
    surplus, counts = total - most - (amount - 1), [1] * (amount - 1)
    while surplus > 0:
        candidates = [i for i in range(amount - 1) if counts[i] < most]
        pool, left = sum([weights[i] for i in candidates]), surplus
        for i in candidates:
            extra = min(most - counts[i], max(1, left * weights[i] // pool), surplus)
            counts[i] = counts[i] + extra
            surplus = surplus - extra
    return np.array([most] + counts)


def ragged_sizes(key, amount, total, most, lean):
    if amount == 2:
        one = jax.random.randint(key, (), max(1, total - most), min(most, total - 1) + 1)
        return jnp.stack([one, total - one])
    lengths = jnp.asarray(length_profile(amount, total, most, lean), jnp.int32)
    twos = (amount - 1) // 2
    donor, receiver = lengths[1:1 + 2 * twos:2], lengths[2:2 + 2 * twos:2]
    margin = jnp.minimum(donor - 1, most - receiver)
    moved = jax.random.randint(jax.random.fold_in(key, 1), (twos,), 0, 1 << 20) % (margin + 1)
    lengths = lengths.at[1:1 + 2 * twos:2].set(donor - moved).at[2:2 + 2 * twos:2].set(receiver + moved)
    return lengths[jax.random.permutation(jax.random.fold_in(key, 2), amount)]


def noise(key, shape, scale, reach, split=(), kind=jnp.bfloat16):
    level = block_levels(key, shape, split, -0.22, 0.18) if split else 1.0
    values = jax.random.normal(key, shape, jnp.float32) * scale * level
    return jnp.minimum(jnp.maximum(values, -reach), reach).astype(kind)


def setup_inputs(seed: int = 0) -> dict:
    splits = jax.random.split(jax.random.key(seed), 11)
    tokens = noise(splits[0], (N_FSDP, GROUP, D), 1.0, 6.0, ((0, 4), (1, 8)))
    seq_lengths = jax.vmap(lambda own: ragged_sizes(own, NSEQ, GROUP, MAXLEN, 2))(jax.random.split(splits[1], N_FSDP)).reshape((N_FSDP, NSEQ)).astype(jnp.int32)
    seq_order = jax.vmap(lambda own: jax.random.permutation(own, GROUP))(jax.random.split(splits[2], N_FSDP)).reshape((N_FSDP, GROUP)).astype(jnp.int32)
    norm_one = jnp.clip(1.0 + 0.1 * jax.random.normal(splits[3], (D,), jnp.float32), 0.5, 1.5).astype(jnp.bfloat16)
    w_qkv = noise(splits[4], (D, 3 * D), (D // 2) ** -0.5, 0.25, ((0, 4),))
    w_out = noise(splits[5], (D, D), (D // 16) ** -0.5, 0.75, ((0, 4),))
    norm_two = jnp.clip(1.0 + 0.1 * jax.random.normal(splits[6], (D,), jnp.float32), 0.5, 1.5).astype(jnp.bfloat16)
    w_in = noise(splits[7], (D, 2 * FF), D ** -0.5, 0.1875, ((0, 4),))
    w_down = noise(splits[8], (FF, D), (FF // 2) ** -0.5, 0.15625, ((0, 4),))
    cotangent = noise(splits[9], (N_FSDP, GROUP, D), 1.0, 6.0, ((0, 4), (1, 8)))
    return {"tokens": tokens, "seq_lengths": seq_lengths, "seq_order": seq_order, "norm_one": norm_one, "w_qkv": w_qkv, "w_out": w_out, "norm_two": norm_two, "w_in": w_in, "w_down": w_down, "cotangent": cotangent}


@jax.custom_vjp
def low(v):
    return lax.optimization_barrier(v.astype(jnp.bfloat16)).astype(jnp.float32)

@jax.custom_vjp
def low_back(v):
    return v

def low_keep(v):
    return (low(v), None)

def low_pass(kept, grad):
    return (grad,)

def back_keep(v):
    return (v, None)

def back_low(kept, grad):
    return (low(grad),)
low.defvjp(low_keep, low_pass)
low_back.defvjp(back_keep, back_low)
HIGH_PREC = lax.Precision.HIGHEST
NORM_EPS = 1e-05
ROPE_BASE = 160000.0
MASKED = -1000000000.0

def norm_rows(values, gain):
    center = values - lax.optimization_barrier(jnp.mean(values, axis=-1, keepdims=True))
    spread = lax.optimization_barrier(jnp.mean(center * center, axis=-1, keepdims=True))
    return center * lax.rsqrt(spread + NORM_EPS) * gain

def rotate(values, places):
    full_width = values.shape[-1]
    half_width = full_width // 2
    index_half = jnp.arange(half_width, dtype=jnp.float32)
    inverse_freq = jnp.power(jnp.float32(ROPE_BASE), -2.0 * index_half / full_width)
    angles = places.astype(jnp.float32)[:, None] * inverse_freq[None, :]
    cosine = jnp.cos(angles)[:, None, :]
    sine = jnp.sin(angles)[:, None, :]
    first_half = values[..., :half_width]
    second_half = values[..., half_width:]
    return jnp.concatenate([first_half * cosine - second_half * sine, second_half * cosine + first_half * sine], axis=-1)

def seq_layout(lengths_row, row_count):
    ends = jnp.cumsum(lengths_row).astype(jnp.int32)
    indices = jnp.arange(row_count, dtype=jnp.int32)
    passed = (indices[:, None] >= ends[None, :]).astype(jnp.int32)
    segment = lax.optimization_barrier(jnp.sum(passed, axis=1)).astype(jnp.int32)
    starts = lax.optimization_barrier(jnp.sum(passed * lengths_row[None, :], axis=1)).astype(jnp.int32)
    return (segment, indices - starts)

def attend_block(query_blk, seg_blk, key_all, value_all, seg_all):
    score_scale = query_blk.shape[-1] ** (-0.5)
    raw = low_back(jnp.einsum('qhd,khd->hqk', query_blk, key_all, precision=HIGH_PREC))
    same_seq = seg_blk[None, :, None] == seg_all[None, None, :]
    scores = jnp.where(same_seq, raw * score_scale, MASKED)
    row_top = lax.optimization_barrier(jnp.max(scores, axis=-1, keepdims=True))
    shifted = jnp.exp(scores - row_top)
    probs = shifted / lax.optimization_barrier(jnp.sum(shifted, axis=-1, keepdims=True))
    return jnp.einsum('hqk,khd->qhd', low(probs), value_all, precision=HIGH_PREC)

def attend_group(qkv_rows, lengths_row, order_row):
    group_rows = qkv_rows.shape[0]
    packed = jnp.take(qkv_rows, order_row, axis=0).reshape(group_rows, 3, H, HD)
    segment, places = seq_layout(lengths_row, group_rows)
    query = low(rotate(packed[:, 0], places))
    key_all = low(rotate(packed[:, 1], places))
    value_all = packed[:, 2]
    block_rows = min(512, group_rows)
    block_count = group_rows // block_rows
    blocked = jax.checkpoint(attend_block)

    def one_block(paired):
        return blocked(paired[0], paired[1], key_all, value_all, segment)
    outputs = lax.map(one_block, (query.reshape(block_count, block_rows, H, HD), segment.reshape(block_count, block_rows)))
    attended = low_back(low(outputs.reshape(group_rows, H * HD)))
    inverse = jnp.zeros((group_rows,), jnp.int32).at[order_row].set(jnp.arange(group_rows, dtype=jnp.int32))
    return jnp.take(attended, inverse, axis=0)

def forward(token_rows, seq_lengths, seq_order, gain_one, weight_qkv, weight_out, gain_two, weight_in, weight_down):
    normed_one = low(norm_rows(token_rows, gain_one))
    qkv = low_back(low(jnp.einsum('gtd,de->gte', normed_one, weight_qkv, precision=HIGH_PREC)))

    def one_group(triple):
        return attend_group(triple[0], triple[1], triple[2])
    attended = lax.map(one_group, (qkv, seq_lengths, seq_order))
    branch = low_back(jnp.einsum('gtd,de->gte', attended, weight_out, precision=HIGH_PREC))
    middle = token_rows + branch
    normed_two = low(norm_rows(middle, gain_two))
    both_parts = low_back(jnp.einsum('gtd,de->gte', normed_two, weight_in, precision=HIGH_PREC))
    hidden = low(jax.nn.gelu(both_parts[..., :FF], approximate=False) * both_parts[..., FF:])
    return middle + low_back(jnp.einsum('gtf,fd->gtd', hidden, weight_down, precision=HIGH_PREC))

def reference(tokens, seq_lengths, seq_order, norm_one, w_qkv, w_out, norm_two, w_in, w_down, cotangent):

    def closed(token_rows, gain_one, weight_qkv, weight_out, gain_two, weight_in, weight_down):
        return forward(token_rows, seq_lengths, seq_order, gain_one, weight_qkv, weight_out, gain_two, weight_in, weight_down)
    primals = (tokens.astype(jnp.float32), norm_one.astype(jnp.float32), w_qkv.astype(jnp.float32), w_out.astype(jnp.float32), norm_two.astype(jnp.float32), w_in.astype(jnp.float32), w_down.astype(jnp.float32))
    result, pullback = jax.vjp(closed, *primals)
    grads = pullback(cotangent.astype(jnp.float32))
    return (result.astype(jnp.bfloat16), grads[0].astype(jnp.bfloat16), grads[1], grads[2], grads[3], grads[4], grads[5], grads[6])
```

```python
import functools
import math

import jax
import jax.numpy as jnp
from jax import lax
from jax.experimental import pallas as pl
from jax.experimental.pallas import tpu as pltpu
from jax.sharding import PartitionSpec as P

HD = 64
NORM_EPS = 1e-05
ROPE_BASE = 160000.0
BLOCK = 256
LOG2E = math.log2(math.e)
AXES = ("seq", "fsdp")
F32 = jnp.float32
BF16 = jnp.bfloat16
VMEM_LIMIT = 60 * 1024 * 1024


def core_swap(value, seq_count):
    return lax.ppermute(value, "seq", [(i, i ^ 1) for i in range(seq_count)])


def plane_bit(core, phase, levels):
    return (phase + core * (levels // 2)) % levels


def plane_mask(core, key, levels):
    mask = 0
    for phase in range(levels):
        if key >> phase & 1:
            mask |= 1 << plane_bit(core, phase, levels)
    return mask


def plane_swap(value, phase, seq_count, fsdp_count):
    levels = fsdp_count.bit_length() - 1
    pairs = []
    for s in range(seq_count):
        step = 1 << plane_bit(s & 1, phase, levels)
        for f in range(fsdp_count):
            pairs.append((s * fsdp_count + f, s * fsdp_count + (f ^ step)))
    return lax.ppermute(value, AXES, pairs)


def plane_gather(piece, seq_count, fsdp_count):
    pieces = [piece]
    for phase in range(fsdp_count.bit_length() - 1):
        pieces = pieces + [plane_swap(p, phase, seq_count, fsdp_count) for p in pieces]
    return pieces


def plane_reduce(blocks, seq_count, fsdp_count):
    blocks = list(blocks)
    for phase in reversed(range(fsdp_count.bit_length() - 1)):
        got = [
            plane_swap(blocks[(1 << phase) + key], phase, seq_count, fsdp_count)
            for key in range(1 << phase)
        ]
        blocks = [
            (blocks[key].astype(F32) + got[key].astype(F32)).astype(BF16)
            for key in range(1 << phase)
        ]
    return blocks[0]


def line_swap(value, level, seq_count):
    return lax.ppermute(value, "seq", [(i, i ^ (2 << level)) for i in range(seq_count)])


def line_levels(seq_count):
    return (seq_count // 2).bit_length() - 1


def line_reduce(block, place_z, seq_count):
    for level in range(line_levels(seq_count)):
        half = block.shape[0] // 2
        bit = (place_z >> level) & 1
        sent = lax.dynamic_slice_in_dim(block, (1 - bit) * half, half, 0)
        kept = lax.dynamic_slice_in_dim(block, bit * half, half, 0)
        got = line_swap(sent, level, seq_count)
        block = (kept.astype(F32) + got.astype(F32)).astype(BF16)
    return block


def ordered(bit, mine, other):
    first = jnp.where(bit == 0, mine, other)
    second = jnp.where(bit == 0, other, mine)
    return jnp.concatenate([first, second], axis=0)


def line_gather(block, place_z, seq_count):
    for level in reversed(range(line_levels(seq_count))):
        bit = (place_z >> level) & 1
        block = ordered(bit, block, line_swap(block, level, seq_count))
    return block


def any_spec():
    return pl.BlockSpec(memory_space=pl.ANY)


def vmem_spec():
    return pl.BlockSpec(memory_space=pltpu.VMEM)


def smem_spec():
    return pl.BlockSpec(memory_space=pltpu.SMEM)


def params():
    return pltpu.CompilerParams(vmem_limit_bytes=VMEM_LIMIT)


def cost(flops, moved):
    return pl.CostEstimate(flops=int(flops), bytes_accessed=int(moved), transcendentals=0)


def nt_dot(a, b):
    return lax.dot_general(a, b, (((1,), (1,)), ((), ())), preferred_element_type=F32)


def nn_dot(a, b):
    return jnp.dot(a, b, preferred_element_type=F32)


def row_copies(place_ref, own, mine, others, full, sems, rows):
    count = len(mine) + 1
    half = rows // 2
    core = place_ref[2 * count - 1]
    copies = [
        pltpu.make_async_copy(
            own, full.at[pl.ds(pl.multiple_of(place_ref[0] * rows, 16), rows), :], sems.at[0]
        )
    ]
    for which, (refs, side) in enumerate(((mine, core), (others, 1 - core))):
        for i, ref in enumerate(refs):
            at = 1 + which * (count - 1) + i
            base = pl.multiple_of(place_ref[at] * rows + side * half, 16)
            copies.append(
                pltpu.make_async_copy(ref, full.at[pl.ds(base, half), :], sems.at[at])
            )
    return copies


def column_copies(place_ref, own, mine, others, full, sems, rows):
    count = len(mine) + 1
    half = full.shape[1] // 2
    core = place_ref[2 * count - 1]
    copies = [
        pltpu.make_async_copy(
            own, full.at[pl.ds(pl.multiple_of(place_ref[0] * rows, 16), rows), :], sems.at[0]
        )
    ]
    for which, (refs, side) in enumerate(((mine, core), (others, 1 - core))):
        for i, ref in enumerate(refs):
            at = 1 + which * (count - 1) + i
            base = pl.multiple_of(place_ref[at] * rows, 16)
            left = pl.multiple_of(side * half, 128)
            copies.append(
                pltpu.make_async_copy(
                    ref, full.at[pl.ds(base, rows), pl.ds(left, half)], sems.at[at]
                )
            )
    return copies


def down_copies(place_ref, refs, full, sems, count, hidden):
    if len(refs) == 1:
        return [pltpu.make_async_copy(refs[0], full.at[pl.ds(0, hidden), :], sems.at[0])]
    return column_copies(
        place_ref, refs[0], refs[1 : 1 + count], refs[1 + count :], full, sems, hidden // (count + 1)
    )


def seg_rows(value, start, stop):
    return value[start:stop]


def attention_forward(
    seq_count, heads, group, low_ref, high_ref, x_ref, gain_ref, w_ref, order_ref, start_ref, end_ref,
    cos_ref, sin_ref, normed_ref, packed_ref, att_ref, out_ref, lse_ref, qkv_t, k_rows, o_rows,
):
    width = heads * HD
    rows = group // seq_count
    blocks = group // BLOCK

    def project(i, carry):
        x = x_ref[i].astype(F32)
        center = x - jnp.mean(x, axis=-1, keepdims=True)
        spread = jnp.mean(center * center, axis=-1, keepdims=True)
        normed = (center * lax.rsqrt(spread + NORM_EPS) * gain_ref[...]).astype(BF16)
        normed_ref[i] = normed
        qkv = nn_dot(normed, w_ref[...]).astype(BF16)
        qkv_t[i] = qkv.T
        return carry

    lax.fori_loop(0, seq_count, project, 0)

    def pack(i, carry):
        at = pl.ds(pl.multiple_of(i * BLOCK, BLOCK), BLOCK)
        order = order_ref[:, at]
        total = jnp.zeros((3 * width, BLOCK), F32)
        for s in range(seq_count):
            here = lax.broadcasted_iota(jnp.int32, (rows, BLOCK), 0) + s * rows
            hot = jnp.where(here == order, 1.0, 0.0).astype(BF16)
            total = total + nn_dot(qkv_t[s], hot)
        cos = cos_ref[:, at]
        sin = sin_ref[:, at]
        half = HD // 2
        for part in range(2):
            for h in range(heads):
                base = part * width + h * HD
                first = total[base : base + half]
                second = total[base + half : base + HD]
                turned = jnp.concatenate(
                    [first * cos - second * sin, second * cos + first * sin], axis=0
                ).astype(BF16)
                packed_ref[base : base + HD, at] = turned
                if part == 1:
                    k_rows[h, at, :] = turned.T
        packed_ref[2 * width :, at] = total[2 * width :].astype(BF16)
        return carry

    lax.fori_loop(0, blocks, pack, 0)
    scale = HD**-0.5 * LOG2E

    def attend(i, carry):
        at = pl.ds(pl.multiple_of(i * BLOCK, BLOCK), BLOCK)
        start = start_ref[:, at]
        end = end_ref[:, at]
        queries = [packed_ref[h * HD : (h + 1) * HD, at] for h in range(heads)]

        def step(j, state):
            there = pl.ds(pl.multiple_of(j * BLOCK, BLOCK), BLOCK)
            where = lax.broadcasted_iota(jnp.int32, (BLOCK, BLOCK), 0) + j * BLOCK
            same = jnp.logical_and(where >= start, where < end)
            following = []
            for h in range(heads):
                top, total, acc = state[h]
                scores = nn_dot(k_rows[h, there, :], queries[h]) * scale
                scores = jnp.where(same, scores, -1e30)
                new_top = jnp.maximum(top, jnp.max(scores, axis=0, keepdims=True))
                shrink = jnp.exp2(top - new_top)
                probs = jnp.exp2(scores - new_top)
                total = total * shrink + jnp.sum(probs, axis=0, keepdims=True)
                base = 2 * width + h * HD
                acc = acc * shrink + nn_dot(packed_ref[base : base + HD, there], probs.astype(BF16))
                following.append((new_top, total, acc))
            return tuple(following)

        first = tuple(
            (
                jnp.full((1, BLOCK), -1e30, F32),
                jnp.zeros((1, BLOCK), F32),
                jnp.zeros((HD, BLOCK), F32),
            )
            for _ in range(heads)
        )
        last = lax.fori_loop(low_ref[i], high_ref[i], step, first)
        outs = []
        for h in range(heads):
            top, total, acc = last[h]
            out = acc / total
            out_ref[h * HD : (h + 1) * HD, at] = out
            lse_ref[h : h + 1, at] = top + jnp.log2(total)
            outs.append(out)
        o_rows[at, :] = jnp.concatenate(outs, axis=0).astype(BF16).T
        return carry

    lax.fori_loop(0, blocks, attend, 0)

    def arrive(i, carry):
        here = lax.broadcasted_iota(jnp.int32, (rows, group), 0) + i * rows
        hot = jnp.where(here == order_ref[...], 1.0, 0.0).astype(BF16)
        att_ref[i] = nn_dot(hot, o_rows[...]).astype(BF16)
        return carry

    lax.fori_loop(0, seq_count, arrive, 0)


def run_attention_forward(x_all, gain, w_heads, layout, heads):
    seq_count, rows, dim = x_all.shape
    group = seq_count * rows
    width = heads * HD
    low, high, order, start, end, cos, sin = layout
    return pl.pallas_call(
        functools.partial(attention_forward, seq_count, heads, group),
        name="attention_forward",
        out_shape=(
            jax.ShapeDtypeStruct((seq_count, rows, dim), BF16),
            jax.ShapeDtypeStruct((3 * width, group), BF16),
            jax.ShapeDtypeStruct((seq_count, rows, width), BF16),
            jax.ShapeDtypeStruct((width, group), F32),
            jax.ShapeDtypeStruct((heads, group), F32),
        ),
        in_specs=[smem_spec()] * 2 + [vmem_spec()] * 8,
        out_specs=[vmem_spec()] * 5,
        scratch_shapes=[
            pltpu.VMEM((seq_count, 3 * width, rows), BF16),
            pltpu.VMEM((heads, group, HD), BF16),
            pltpu.VMEM((group, width), BF16),
        ],
        compiler_params=params(),
        cost_estimate=cost(24e9, 20e6),
    )(low, high, x_all, gain, w_heads, order, start, end, cos, sin)


def attention_backward(
    seq_count, heads, group, low_ref, high_ref, dout_ref, packed_ref, out_ref, lse_ref, order_ref,
    start_ref, end_ref, cos_ref, sin_ref, grad_ref, dout_t, dpack_t, drows, qrows, krows, vrows,
    delta_ref, dq_t, grows,
):
    width = heads * HD
    rows = group // seq_count
    blocks = group // BLOCK
    scale = HD**-0.5

    def turn(i, carry):
        dout_t[i] = dout_ref[i].T
        return carry

    lax.fori_loop(0, seq_count, turn, 0)

    def pack(i, carry):
        at = pl.ds(pl.multiple_of(i * BLOCK, BLOCK), BLOCK)
        order = order_ref[:, at]
        total = jnp.zeros((width, BLOCK), F32)
        for s in range(seq_count):
            here = lax.broadcasted_iota(jnp.int32, (rows, BLOCK), 0) + s * rows
            hot = jnp.where(here == order, 1.0, 0.0).astype(BF16)
            total = total + nn_dot(dout_t[s], hot)
        dpack_t[:, at] = total.astype(BF16)
        for h in range(heads):
            mine = total[h * HD : (h + 1) * HD]
            delta_ref[h : h + 1, at] = jnp.sum(
                mine * out_ref[h * HD : (h + 1) * HD, at], axis=0, keepdims=True
            )
            drows[h, at, :] = mine.T.astype(BF16)
            for part, ref in enumerate((qrows, krows, vrows)):
                base = part * width + h * HD
                ref[h, at, :] = packed_ref[base : base + HD, at].T
        dq_t[:, at] = jnp.zeros((width, BLOCK), F32)
        return carry

    lax.fori_loop(0, blocks, pack, 0)

    def keys(j, carry):
        there = pl.ds(pl.multiple_of(j * BLOCK, BLOCK), BLOCK)
        where = lax.broadcasted_iota(jnp.int32, (BLOCK, BLOCK), 0) + j * BLOCK

        def queries(i, state):
            at = pl.ds(pl.multiple_of(i * BLOCK, BLOCK), BLOCK)
            same = jnp.logical_and(where >= start_ref[:, at], where < end_ref[:, at])
            following = []
            for h in range(heads):
                dk, dv = state[h]
                base = h * HD
                key_rows = krows[h, there, :]
                query_t = packed_ref[base : base + HD, at]
                scores = nn_dot(key_rows, query_t) * (scale * LOG2E)
                scores = jnp.where(same, scores, -1e30)
                probs = jnp.exp2(scores - lse_ref[h : h + 1, at])
                dprobs = nn_dot(vrows[h, there, :], dpack_t[base : base + HD, at])
                raw = (probs * (dprobs - delta_ref[h : h + 1, at]) * scale).astype(BF16)
                dv = dv + nn_dot(probs.astype(BF16), drows[h, at, :])
                dk = dk + nn_dot(raw, qrows[h, at, :])
                key_t = packed_ref[width + base : width + base + HD, there]
                dq_t[base : base + HD, at] += nn_dot(key_t, raw)
                following.append((dk, dv))
            return tuple(following)

        zero = jnp.zeros((BLOCK, HD), F32)
        last = lax.fori_loop(low_ref[j], high_ref[j], queries, tuple((zero, zero) for _ in range(heads)))
        cos = cos_ref[:, there]
        sin = sin_ref[:, there]
        half = HD // 2
        turned = []
        for h in range(heads):
            dk_t = last[h][0].T
            first, second = dk_t[:half], dk_t[half:]
            turned.append(first * cos + second * sin)
            turned.append(second * cos - first * sin)
        grows[there, width : 2 * width] = jnp.concatenate(turned, axis=0).T.astype(BF16)
        grows[there, 2 * width :] = jnp.concatenate([last[h][1] for h in range(heads)], axis=1).astype(BF16)
        return carry

    lax.fori_loop(0, blocks, keys, 0)

    def finish(i, carry):
        at = pl.ds(pl.multiple_of(i * BLOCK, BLOCK), BLOCK)
        cos = cos_ref[:, at]
        sin = sin_ref[:, at]
        half = HD // 2
        turned = []
        for h in range(heads):
            first = dq_t[h * HD : h * HD + half, at]
            second = dq_t[h * HD + half : (h + 1) * HD, at]
            turned.append(first * cos + second * sin)
            turned.append(second * cos - first * sin)
        grows[at, :width] = jnp.concatenate(turned, axis=0).T.astype(BF16)
        return carry

    lax.fori_loop(0, blocks, finish, 0)

    def arrive(i, carry):
        here = lax.broadcasted_iota(jnp.int32, (rows, group), 0) + i * rows
        hot = jnp.where(here == order_ref[...], 1.0, 0.0).astype(BF16)
        grad_ref[i] = nn_dot(hot, grows[...]).astype(BF16)
        return carry

    lax.fori_loop(0, seq_count, arrive, 0)


def run_attention_backward(dout, packed, out_t, lse, layout, heads):
    seq_count, rows, width = dout.shape
    group = seq_count * rows
    low, high, order, start, end, cos, sin = layout
    return pl.pallas_call(
        functools.partial(attention_backward, seq_count, heads, group),
        name="attention_backward",
        out_shape=jax.ShapeDtypeStruct((seq_count, rows, 3 * width), BF16),
        in_specs=[smem_spec()] * 2 + [vmem_spec()] * 9,
        out_specs=vmem_spec(),
        scratch_shapes=[
            pltpu.VMEM((seq_count, width, rows), BF16),
            pltpu.VMEM((width, group), BF16),
            pltpu.VMEM((heads, group, HD), BF16),
            pltpu.VMEM((heads, group, HD), BF16),
            pltpu.VMEM((heads, group, HD), BF16),
            pltpu.VMEM((heads, group, HD), BF16),
            pltpu.VMEM((heads, group), F32),
            pltpu.VMEM((width, group), F32),
            pltpu.VMEM((group, 3 * width), BF16),
        ],
        compiler_params=params(),
        cost_estimate=cost(30e9, 10e6),
    )(low, high, dout, packed, out_t, lse, order, start, end, cos, sin)


def qkv_weight_grad(seq_count, normed_ref, grad_ref, gw_ref, total):
    total[...] = jnp.zeros_like(total)

    def step(i, carry):
        total[...] += nn_dot(grad_ref[i].T, normed_ref[i])
        return carry

    lax.fori_loop(0, seq_count, step, 0)
    gw_ref[...] = total[...].T.astype(BF16)


def run_qkv_weight_grad(normed, grad):
    seq_count, rows, dim = normed.shape
    width = grad.shape[-1]
    return pl.pallas_call(
        functools.partial(qkv_weight_grad, seq_count),
        name="qkv_weight_grad",
        out_shape=jax.ShapeDtypeStruct((dim, width), BF16),
        in_specs=[vmem_spec()] * 2,
        out_specs=vmem_spec(),
        scratch_shapes=[pltpu.VMEM((width, dim), F32)],
        compiler_params=params(),
        cost_estimate=cost(3e9, 6e6),
    )(normed, grad)


def padded(hidden):
    return -(-hidden // 128) * 128


def hidden_grad(count, hidden, place_ref, cot_ref, *refs):
    downs, (out_ref, full, sems) = refs[:-3], refs[-3:]
    copies = down_copies(place_ref, downs, full, sems, count, hidden)
    for copy in copies:
        copy.start()
    tail = padded(hidden) - hidden
    if tail:
        full[pl.ds(hidden, tail), :] = jnp.zeros((tail, full.shape[1]), BF16)
    for copy in copies:
        copy.wait()
    cot = cot_ref[...]
    tiles = padded(hidden) // 128

    def step(i, carry):
        at = pl.multiple_of(i * 128, 128)
        out_ref[:, pl.ds(at, 128)] = nt_dot(cot, full[pl.ds(at, 128), :])
        return carry

    lax.fori_loop(0, tiles, step, 0)


def run_hidden_grad(place, cot, downs, count, hidden):
    rows, dim = cot.shape
    return pl.pallas_call(
        functools.partial(hidden_grad, count, hidden),
        name="hidden_grad",
        out_shape=jax.ShapeDtypeStruct((rows, padded(hidden)), F32),
        in_specs=[smem_spec(), vmem_spec()] + [any_spec()] * len(downs),
        out_specs=vmem_spec(),
        scratch_shapes=[
            pltpu.VMEM((padded(hidden), dim), BF16),
            pltpu.SemaphoreType.DMA((2 * count + 1,)),
        ],
        compiler_params=params(),
        cost_estimate=cost(4e9, 9e6),
    )(place, cot, *downs)


def layer_result(count, hidden, place_ref, mid_ref, hid_ref, *refs):
    downs, (out_ref, full, sems) = refs[:-3], refs[-3:]
    copies = down_copies(place_ref, downs, full, sems, count, hidden)
    for copy in copies:
        copy.start()
    tail = padded(hidden) - hidden
    if tail:
        full[pl.ds(hidden, tail), :] = jnp.zeros((tail, full.shape[1]), BF16)
    for copy in copies:
        copy.wait()

    def step(i, carry):
        at = pl.ds(pl.multiple_of(i * 256, 256), 256)
        out_ref[:, at] = (mid_ref[:, at] + nn_dot(hid_ref[...], full[:, at])).astype(BF16)
        return carry

    lax.fori_loop(0, out_ref.shape[1] // 256, step, 0)


def run_layer_result(place, middle, hidden_rows, downs, count, hidden):
    rows, dim = middle.shape
    return pl.pallas_call(
        functools.partial(layer_result, count, hidden),
        name="layer_result",
        out_shape=jax.ShapeDtypeStruct((rows, dim), BF16),
        in_specs=[smem_spec()] + [vmem_spec()] * 2 + [any_spec()] * len(downs),
        out_specs=vmem_spec(),
        scratch_shapes=[
            pltpu.VMEM((padded(hidden), dim), BF16),
            pltpu.SemaphoreType.DMA((2 * count + 1,)),
        ],
        compiler_params=params(),
        cost_estimate=cost(4e9, 9e6),
    )(place, middle, hidden_rows, *downs)


def feed_forward(
    count, hidden, heads_width, place_ref, x_ref, att_ref, cot_ref, gain_ref, gh_ref, *refs
):
    outs_w, refs = refs[: 2 * count + 1], refs[2 * count + 1 :]
    ins_w, refs = refs[: 2 * count + 1], refs[2 * count + 1 :]
    (mid_ref, gmid_ref, nt_ref, gboth_ref, hid_ref, gbr_ref, ga_ref, att_all_ref) = refs[:8]
    wo, wi, both, early, late, sem_o, sem_i = refs[8:]
    dim = x_ref.shape[1]
    rows = dim // (count + 1)
    copies_o = row_copies(place_ref, outs_w[0], outs_w[1 : 1 + count], outs_w[1 + count :], wo, sem_o, rows)
    copies_i = row_copies(place_ref, ins_w[0], ins_w[1 : 1 + count], ins_w[1 + count :], wi, sem_i, rows)
    for copy in copies_o:
        copy.start()
    for copy in copies_i:
        copy.start()
    att = jnp.concatenate([att_ref[s] for s in range(att_ref.shape[0])], axis=1)
    att_all_ref[...] = att
    for copy in copies_o:
        copy.wait()

    def branch(i, carry):
        at = pl.ds(pl.multiple_of(i * 256, 256), 256)
        mid_ref[:, at] = x_ref[:, at].astype(F32) + nn_dot(att_all_ref[...], wo[:, at])
        return carry

    lax.fori_loop(0, dim // 256, branch, 0)
    middle = mid_ref[...]
    center = middle - jnp.mean(middle, axis=-1, keepdims=True)
    spread = jnp.mean(center * center, axis=-1, keepdims=True)
    scale = lax.rsqrt(spread + NORM_EPS)
    nt_ref[...] = (center * scale * gain_ref[...]).astype(BF16)
    for copy in copies_i:
        copy.wait()
    wide = 2 * hidden // 128

    def expand(i, carry):
        at = pl.ds(pl.multiple_of(i * 256, 256), 256)
        both[:, at] = nn_dot(nt_ref[...], wi[:, at])
        return carry

    lax.fori_loop(0, wide // 2, expand, 0)
    if wide % 2:
        both[:, pl.ds(128 * (wide - 1), 128)] = nn_dot(nt_ref[...], wi[:, pl.ds(128 * (wide - 1), 128)])
    both[:, pl.ds(128 * wide, 128)] = jnp.zeros((both.shape[0], 128), F32)
    tiles = padded(hidden) // 128
    whole = hidden // 128
    lanes = lax.broadcasted_iota(jnp.int32, (both.shape[0], 128), 1)
    shift = hidden % 128

    def tile(i):
        return pl.ds(pl.multiple_of(i * 128, 128), 128)

    def gates(i):
        a = both[:, tile(i)]
        if shift:
            left = pltpu.roll(both[:, tile(whole + i)], 128 - shift, 1)
            right = pltpu.roll(both[:, tile(whole + i + 1)], 128 - shift, 1)
            b = jnp.where(lanes < 128 - shift, left, right)
        else:
            b = both[:, tile(whole + i)]
        gh = gh_ref[:, tile(i)]
        phi = 0.5 * (1.0 + lax.erf(a * (0.5**0.5)))
        gelu = a * phi
        slope = phi + a * ((0.5 / math.pi) ** 0.5 * jnp.exp(-0.5 * a * a))
        hid_ref[:, tile(i)] = (gelu * b).astype(BF16)
        return gh * b * slope, gh * gelu

    if shift:
        first_a, first_b = gates(0)
        gboth_ref[:, tile(0)] = first_a.astype(BF16)
        early[...] = pltpu.roll(first_b, shift, 1)
        late[...] = early[...]

        def inner(i, carry):
            ga, gb = gates(i)
            turned = pltpu.roll(gb, shift, 1)
            gboth_ref[:, tile(i)] = ga.astype(BF16)
            gboth_ref[:, tile(whole + i)] = jnp.where(lanes < shift, late[...], turned).astype(BF16)
            late[...] = turned
            return carry

        lax.fori_loop(1, tiles - 1, inner, 0)
        ga, gb = gates(tiles - 1)
        turned = pltpu.roll(gb, shift, 1)
        gboth_ref[:, tile(whole)] = jnp.where(lanes < shift, ga, early[...]).astype(BF16)
        gboth_ref[:, tile(2 * whole)] = jnp.where(lanes < shift, late[...], turned).astype(BF16)
    else:

        def inner(i, carry):
            ga, gb = gates(i)
            gboth_ref[:, tile(i)] = ga.astype(BF16)
            gboth_ref[:, tile(whole + i)] = gb.astype(BF16)
            return carry

        lax.fori_loop(0, tiles, inner, 0)

    def back(i, carry):
        at = pl.multiple_of(i * 128, 128)
        both[:, pl.ds(at, 128)] = nt_dot(gboth_ref[...], wi[pl.ds(at, 128), :])
        return carry

    lax.fori_loop(0, dim // 128, back, 0)
    middle = mid_ref[...]
    center = middle - jnp.mean(middle, axis=-1, keepdims=True)
    spread = jnp.mean(center * center, axis=-1, keepdims=True)
    scale = lax.rsqrt(spread + NORM_EPS)
    normal = center * scale
    e = both[:, pl.ds(0, dim)] * gain_ref[...]
    pull = e - jnp.mean(e, axis=-1, keepdims=True) - normal * jnp.mean(e * normal, axis=-1, keepdims=True)
    gmid = cot_ref[...].astype(F32) + scale * pull
    gmid_ref[...] = gmid
    gbr_ref[...] = gmid.astype(BF16)

    def spread_out(i, carry):
        at = pl.multiple_of(i * 128, 128)
        both[:, pl.ds(at, 128)] = nt_dot(gbr_ref[...], wo[pl.ds(at, 128), :])
        return carry

    lax.fori_loop(0, dim // 128, spread_out, 0)
    for s in range(att_ref.shape[0]):
        ga_ref[s] = both[:, s * heads_width : (s + 1) * heads_width].astype(BF16)


def run_feed_forward(place, x, att, cot, gain, grad_hidden, w_out, w_in, count, hidden):
    rows, dim = x.shape
    seq_count, _, heads_width = att.shape
    return pl.pallas_call(
        functools.partial(feed_forward, count, hidden, heads_width),
        name="feed_forward",
        out_shape=(
            jax.ShapeDtypeStruct((rows, dim), F32),
            jax.ShapeDtypeStruct((rows, dim), F32),
            jax.ShapeDtypeStruct((rows, dim), BF16),
            jax.ShapeDtypeStruct((rows, 2 * hidden), BF16),
            jax.ShapeDtypeStruct((rows, padded(hidden)), BF16),
            jax.ShapeDtypeStruct((rows, dim), BF16),
            jax.ShapeDtypeStruct((seq_count, rows, heads_width), BF16),
            jax.ShapeDtypeStruct((rows, dim), BF16),
        ),
        in_specs=[smem_spec()] + [vmem_spec()] * 5 + [any_spec()] * (len(w_out) + len(w_in)),
        out_specs=[vmem_spec()] * 8,
        scratch_shapes=[
            pltpu.VMEM((dim, dim), BF16),
            pltpu.VMEM((dim, 2 * hidden), BF16),
            pltpu.VMEM((rows, 2 * hidden + 128), F32),
            pltpu.VMEM((rows, 128), F32),
            pltpu.VMEM((rows, 128), F32),
            pltpu.SemaphoreType.DMA((2 * count + 1,)),
            pltpu.SemaphoreType.DMA((2 * count + 1,)),
        ],
        compiler_params=params(),
        cost_estimate=cost(16e9, 24e6),
    )(place, x, att, cot, gain, grad_hidden, *w_out, *w_in)


def row_grad(count, rows, place_ref, left_ref, left_other_ref, right_ref, right_other_ref, out_ref, turned, picked):
    half = rows // 2
    tokens = left_ref.shape[0]

    @pl.when(pl.program_id(0) == 0)
    def _():
        turned[:, :tokens] = left_ref[...].T
        turned[:, tokens:] = left_other_ref[...].T
        core = place_ref[2 * count + 1]
        for key in range(count + 1):
            base = pl.multiple_of(place_ref[key] * rows + core * half, 16)
            picked[key * half : (key + 1) * half, :] = turned[pl.ds(base, half), :]

    right = jnp.concatenate([right_ref[...], right_other_ref[...]], axis=0)
    result = nn_dot(picked[...], right).astype(BF16)
    for key in range(count + 1):
        out_ref[key] = result[key * half : (key + 1) * half]


def run_row_grad(name, place, left, left_other, right, right_other, count):
    tokens, features = left.shape
    columns = right.shape[1]
    rows = features // (count + 1)
    wide = 1024 if columns % 1024 == 0 else 896
    steps = pl.cdiv(columns, wide)
    return pl.pallas_call(
        functools.partial(row_grad, count, rows),
        name=name,
        out_shape=jax.ShapeDtypeStruct((count + 1, rows // 2, columns), BF16),
        grid=(steps,),
        in_specs=[
            smem_spec(),
            pl.BlockSpec((tokens, features), lambda i: (0, 0)),
            pl.BlockSpec((tokens, features), lambda i: (0, 0)),
            pl.BlockSpec((tokens, wide), lambda i: (0, i)),
            pl.BlockSpec((tokens, wide), lambda i: (0, i)),
        ],
        out_specs=pl.BlockSpec((count + 1, rows // 2, wide), lambda i: (0, 0, i)),
        scratch_shapes=[
            pltpu.VMEM((features, 2 * tokens), BF16),
            pltpu.VMEM((features // 2, 2 * tokens), BF16),
        ],
        compiler_params=params(),
        cost_estimate=cost(2.0 * 2 * tokens * features * columns, 4 * tokens * columns + features * columns),
    )(place, left, left_other, right, right_other)


def down_grad(count, hidden, place_ref, hid_ref, hid_other_ref, cot_ref, cot_other_ref, out_ref, turned, picked):
    tokens = hid_ref.shape[0]
    half = cot_ref.shape[1] // 2
    rows = hidden // (count + 1)

    @pl.when(pl.program_id(0) == 0)
    def _():
        turned[:, :tokens] = hid_ref[...].T
        turned[:, tokens:] = hid_other_ref[...].T
        left = pl.ds(pl.multiple_of(place_ref[2 * count + 1] * half, 128), half)
        picked[:tokens] = cot_ref[:, left]
        picked[tokens:] = cot_other_ref[:, left]

    if rows % 16 == 0:
        base = pl.multiple_of(place_ref[pl.program_id(0)] * rows, 16)
        out_ref[0] = nn_dot(turned[pl.ds(base, rows), :], picked[...]).astype(BF16)
    else:
        out_ref[0] = nn_dot(turned[:hidden, :], picked[...]).astype(BF16)


def run_down_grad(place, hid, hid_other, cot, cot_other, count, hidden):
    tokens, dim = cot.shape
    rows = hidden // (count + 1)
    steps, rows = (count + 1, rows) if rows % 16 == 0 else (1, hidden)
    whole = lambda i: (0, 0)
    return pl.pallas_call(
        functools.partial(down_grad, count, hidden),
        name="down_grad",
        out_shape=jax.ShapeDtypeStruct((steps, rows, dim // 2), BF16),
        grid=(steps,),
        in_specs=[
            smem_spec(),
            pl.BlockSpec(hid.shape, whole),
            pl.BlockSpec(hid.shape, whole),
            pl.BlockSpec(cot.shape, whole),
            pl.BlockSpec(cot.shape, whole),
        ],
        out_specs=pl.BlockSpec((1, rows, dim // 2), lambda i: (i, 0, 0)),
        scratch_shapes=[
            pltpu.VMEM((hid.shape[1], 2 * tokens), BF16),
            pltpu.VMEM((2 * tokens, dim // 2), BF16),
        ],
        compiler_params=params(),
        cost_estimate=cost(3e9, 6e6),
    )(place, hid, hid_other, cot, cot_other)


def input_grad(count, place_ref, x_ref, gmid_ref, gain_ref, g_ref, *refs):
    weights, (out_ref, full, grad, total, sems) = refs[:-5], refs[-5:]
    seq_count, _, width = g_ref.shape
    width //= 3
    dim = x_ref.shape[1]
    rows = dim // (count + 1)
    copies = row_copies(place_ref, weights[0], weights[1 : 1 + count], weights[1 + count :], full, sems, rows)
    for copy in copies:
        copy.start()
    grad[...] = jnp.concatenate(
        [g_ref[s][:, part * width : (part + 1) * width] for part in range(3) for s in range(seq_count)],
        axis=1,
    )
    for copy in copies:
        copy.wait()

    def step(i, carry):
        at = pl.multiple_of(i * 128, 128)
        total[:, pl.ds(at, 128)] = nt_dot(grad[...], full[pl.ds(at, 128), :])
        return carry

    lax.fori_loop(0, dim // 128, step, 0)
    x = x_ref[...].astype(F32)
    center = x - jnp.mean(x, axis=-1, keepdims=True)
    spread = jnp.mean(center * center, axis=-1, keepdims=True)
    scale = lax.rsqrt(spread + NORM_EPS)
    normal = center * scale
    e = total[...] * gain_ref[...]
    pull = e - jnp.mean(e, axis=-1, keepdims=True) - normal * jnp.mean(e * normal, axis=-1, keepdims=True)
    out_ref[...] = (gmid_ref[...] + scale * pull).astype(BF16)


def run_input_grad(place, x, gmid, gain, grads, weights, count):
    rows, dim = x.shape
    columns = weights[0].shape[1]
    return pl.pallas_call(
        functools.partial(input_grad, count),
        name="input_grad",
        out_shape=jax.ShapeDtypeStruct((rows, dim), BF16),
        in_specs=[smem_spec()] + [vmem_spec()] * 4 + [any_spec()] * len(weights),
        out_specs=vmem_spec(),
        scratch_shapes=[
            pltpu.VMEM((dim, columns), BF16),
            pltpu.VMEM((rows, columns), BF16),
            pltpu.VMEM((rows, dim), F32),
            pltpu.SemaphoreType.DMA((2 * count + 1,)),
        ],
        compiler_params=params(),
        cost_estimate=cost(4e9, 10e6),
    )(place, x, gmid, gain, grads, *weights)


def sequence_layout(lengths, order, group):
    ends = jnp.cumsum(lengths)
    starts = ends - lengths
    index = jnp.arange(group, dtype=jnp.int32)
    passed = index[:, None] >= ends[None, :]
    start = jnp.sum(jnp.where(passed, lengths[None, :], 0), axis=1).astype(jnp.int32)
    inside = jnp.logical_and(index[:, None] >= starts[None, :], jnp.logical_not(passed))
    end = jnp.sum(jnp.where(inside, ends[None, :], 0), axis=1).astype(jnp.int32)
    places = index - start
    half = HD // 2
    speeds = jnp.power(F32(ROPE_BASE), -2.0 * jnp.arange(half, dtype=F32) / HD)
    angles = speeds[:, None] * places.astype(F32)[None, :]
    low = start[::BLOCK] // BLOCK
    high = (end[BLOCK - 1 :: BLOCK] + BLOCK - 1) // BLOCK
    return (low, high, order[None, :], start[None, :], end[None, :], jnp.cos(angles), jnp.sin(angles))


def local(tokens, seq_lengths, seq_order, norm_one, w_qkv, w_out, norm_two, w_in, w_down, cotangent):
    seq_count = lax.axis_size("seq")
    fsdp_count = lax.axis_size("fsdp")
    levels = fsdp_count.bit_length() - 1
    count = fsdp_count - 1
    seq_at = lax.axis_index("seq")
    fsdp_at = lax.axis_index("fsdp")
    core = seq_at % 2
    place_z = seq_at // 2
    x = tokens[0]
    cot = cotangent[0]
    rows, dim = x.shape
    group = rows * seq_count
    heads = dim // HD // seq_count
    width = heads * HD
    hidden = w_in.shape[1] // 2
    gather = functools.partial(plane_gather, seq_count=seq_count, fsdp_count=fsdp_count)
    swap = functools.partial(core_swap, seq_count=seq_count)

    keys = [jnp.array([plane_mask(c, key, levels) for key in range(1, fsdp_count)], jnp.int32) for c in (0, 1)]
    mine = fsdp_at ^ jnp.where(core == 0, keys[0], keys[1])
    other = fsdp_at ^ jnp.where(core == 0, keys[1], keys[0])
    place = jnp.concatenate([fsdp_at[None], mine, other, core[None]]).astype(jnp.int32)

    def half_rows(weight):
        half = weight.shape[0] // 2
        return lax.dynamic_slice_in_dim(weight, core * half, half, 0)

    def half_columns(weight):
        half = weight.shape[1] // 2
        return lax.dynamic_slice_in_dim(weight, core * half, half, 1)

    def spread_weight(weight, piece):
        pieces = gather(piece)[1:]
        return [weight] + pieces + [swap(p) for p in pieces]

    x_all = lax.all_gather(x, "seq", axis=0, tiled=False)
    own_heads = lax.dynamic_slice_in_dim(w_qkv.reshape(w_qkv.shape[0], 3, dim), seq_at * width, width, 2)
    w_heads = lax.all_gather(own_heads.reshape(w_qkv.shape[0], 3 * width), "fsdp", axis=0, tiled=True)
    gains = lax.all_gather(jnp.stack([norm_one, norm_two]), "fsdp", axis=1, tiled=True).astype(F32)
    gain_one, gain_two = gains[0:1], gains[1:2]
    outs = spread_weight(w_out, half_rows(w_out))
    if w_down.shape[0] % 16 == 0:
        downs = spread_weight(w_down, half_columns(w_down))
    else:
        downs = [lax.all_gather(w_down, "fsdp", axis=0, tiled=True)]
    ins = spread_weight(w_in, half_rows(w_in))
    qkvs = spread_weight(w_qkv, half_rows(w_qkv))
    cot_other = swap(cot)

    layout = sequence_layout(seq_lengths[0], seq_order[0], group)
    normed, packed, att, out_t, lse = run_attention_forward(x_all, gain_one, w_heads, layout, heads)
    att = lax.all_to_all(att, "seq", split_axis=0, concat_axis=0, tiled=True)
    grad_hidden = run_hidden_grad(place, cot, downs, count, hidden)
    middle, gmid, normed_two, gboth, hid, gbranch, gatt, att_all = run_feed_forward(
        place, x, att, cot, gain_two, grad_hidden, outs, ins, count, hidden
    )
    dout = lax.all_to_all(gatt, "seq", split_axis=0, concat_axis=0, tiled=True)
    layer_out = run_layer_result(place, middle, hid, downs, count, hidden)

    def finish(block):
        block = line_gather(line_reduce(block, place_z, seq_count), place_z, seq_count)
        return block

    reduce = functools.partial(plane_reduce, seq_count=seq_count, fsdp_count=fsdp_count)
    gw_in = run_row_grad("in_grad", place, normed_two, swap(normed_two), gboth, swap(gboth), count)
    gw_in = finish(reduce([gw_in[k] for k in range(fsdp_count)]))
    gw_in = ordered(core, gw_in, swap(gw_in)).astype(F32)
    gw_down = run_down_grad(place, hid, swap(hid), cot, cot_other, count, hidden)
    if w_down.shape[0] % 16 == 0:
        gw_down = [gw_down[k] for k in range(fsdp_count)]
    else:
        each = w_down.shape[0]
        gw_down = [lax.dynamic_slice_in_dim(gw_down[0], place[k] * each, each, 0) for k in range(fsdp_count)]
    gw_down = reduce(gw_down).T
    gw_down = finish(gw_down)
    gw_down = ordered(core, gw_down, swap(gw_down)).T.astype(F32)
    gw_out = run_row_grad("out_grad", place, att_all, swap(att_all), gbranch, swap(gbranch), count)
    gw_out = finish(reduce([gw_out[k] for k in range(fsdp_count)]))
    gw_out = ordered(core, gw_out, swap(gw_out)).astype(F32)

    grads = run_attention_backward(dout, packed, out_t, lse, layout, heads)
    grad_rows = lax.all_to_all(grads, "seq", split_axis=0, concat_axis=0, tiled=True)
    gw_heads = run_qkv_weight_grad(normed, grads)
    each = w_qkv.shape[0]
    gw_heads = reduce([lax.dynamic_slice_in_dim(gw_heads, place[k] * each, each, 0) for k in range(fsdp_count)])
    block = gw_heads[None]
    block = ordered(core, block, swap(block))[None]
    block = line_gather(block, place_z, seq_count)
    index = []
    for z in range(seq_count // 2):
        at = 0
        for level in range(line_levels(seq_count)):
            at = at * 2 + (z >> level & 1)
        index.append(at)
    block = jnp.stack([block[at] for at in index]).reshape(seq_count, each, 3, width)
    gw_qkv = block.transpose(1, 2, 0, 3).reshape(each, 3 * dim).astype(F32)
    grad_tokens = run_input_grad(place, x, gmid, gain_one, grad_rows, qkvs, count)

    grad_one = jnp.sum(gw_qkv * w_qkv.astype(F32), axis=1) / norm_one.astype(F32)
    grad_two = jnp.sum(gw_in * w_in.astype(F32), axis=1) / norm_two.astype(F32)
    return (layer_out[None], grad_tokens[None], grad_one, gw_qkv, gw_out, grad_two, gw_in, gw_down)


def solution(mesh):
    tokens = P("fsdp", "seq", None)
    rows = P("fsdp", None)
    return jax.shard_map(
        local,
        mesh=mesh,
        in_specs=(tokens, rows, rows, P("fsdp"), rows, rows, P("fsdp"), rows, rows, tokens),
        out_specs=(tokens, tokens, P("fsdp"), rows, rows, P("fsdp"), rows, rows),
        check_vma=False,
    )
```

```python
import functools
import math

import jax
import jax.numpy as jnp
from jax import lax
from jax.experimental import pallas as pl
from jax.experimental.pallas import tpu as pltpu
from jax.sharding import PartitionSpec as P

HD = 64
NORM_EPS = 1e-05
ROPE_BASE = 160000.0
BLOCK = 256
WIDE = 512
LOG2E = math.log2(math.e)
AXES = ("seq", "fsdp")
F32 = jnp.float32
BF16 = jnp.bfloat16
VMEM_LIMIT = 60 * 1024 * 1024


def core_swap(value, seq_count):
    return lax.ppermute(value, "seq", [(i, i ^ 1) for i in range(seq_count)])


def plane_bit(core, phase, levels):
    return (phase + core * (levels // 2)) % levels


def plane_mask(core, key, levels):
    mask = 0
    for phase in range(levels):
        if key >> phase & 1:
            mask |= 1 << plane_bit(core, phase, levels)
    return mask


def plane_swap(value, phase, seq_count, fsdp_count):
    levels = fsdp_count.bit_length() - 1
    pairs = []
    for s in range(seq_count):
        step = 1 << plane_bit(s & 1, phase, levels)
        for f in range(fsdp_count):
            pairs.append((s * fsdp_count + f, s * fsdp_count + (f ^ step)))
    return lax.ppermute(value, AXES, pairs)


def after(value, *others):
    return lax.optimization_barrier((value, *others))[0]


def plane_gather(piece, seq_count, fsdp_count, *others):
    pieces = [piece]
    for phase in range(fsdp_count.bit_length() - 1):
        if phase == 1:
            pieces[0] = after(piece, pieces[1], *others)
        pieces = pieces + [plane_swap(p, phase, seq_count, fsdp_count) for p in pieces]
    return pieces[1:]


def added(*values):
    return sum(v.astype(F32) for v in values).astype(BF16)


def plane_reduce(first, b, c, seq_count, fsdp_count):
    second = plane_swap(added(b[0], first[1]), 0, seq_count, fsdp_count)
    return c[0], first[0], second


def line_swap(value, level, seq_count):
    return lax.ppermute(value, "seq", [(i, i ^ (2 << level)) for i in range(seq_count)])


def line_reduce(parts, seq_count):
    got = line_swap(added(*(p[2:] for p in parts)), 0, seq_count)
    last = line_swap(added(*(p[1] for p in parts), got[1]), 1, seq_count)
    return added(*(p[0] for p in parts), got[0], last)


def line_gather(block, seq_count):
    pair = jnp.stack([block, line_swap(block, 1, seq_count)])
    rest = line_swap(pair, 0, seq_count)
    return [pair, rest, core_swap(pair, seq_count), core_swap(rest, seq_count)]


def any_spec():
    return pl.BlockSpec(memory_space=pl.ANY)


def vmem_spec():
    return pl.BlockSpec(memory_space=pltpu.VMEM)


def smem_spec():
    return pl.BlockSpec(memory_space=pltpu.SMEM)


def params():
    return pltpu.CompilerParams(vmem_limit_bytes=VMEM_LIMIT)


def cost(flops, moved):
    return pl.CostEstimate(flops=int(flops), bytes_accessed=int(moved), transcendentals=0)


def nt_dot(a, b):
    return lax.dot_general(a, b, (((1,), (1,)), ((), ())), preferred_element_type=F32)


def nn_dot(a, b):
    return jnp.dot(a, b, preferred_element_type=F32)


def own_copy(place_ref, own, full, sems, rows):
    base = pl.multiple_of(place_ref[0] * rows, 16)
    return pltpu.make_async_copy(own, full.at[pl.ds(base, rows), :], sems.at[0])


def row_copies(place_ref, own, mine, others, left, full, sems):
    count = len(mine)
    rows = own.shape[0]
    half = rows // 2
    core = place_ref[2 * count + 1]
    copies = [own_copy(place_ref, own, full, sems, rows)]
    for which, (refs, side) in enumerate(((mine, core), (others, 1 - core))):
        for i, ref in enumerate(refs):
            at = 1 + which * count + i
            base = pl.multiple_of(place_ref[at] * rows + side * half, 16)
            copies.append(
                pltpu.make_async_copy(
                    ref.at[:, pl.ds(left, full.shape[1])], full.at[pl.ds(base, half), :], sems.at[at]
                )
            )
    return copies


def down_blocks(rows, tall):
    return [(start, min(tall, rows - start)) for start in range(0, rows, tall)]


def down_copies(place_ref, own, mine, others, left, full, sems, hidden):
    if not mine:
        return [pltpu.make_async_copy(own, full.at[pl.ds(0, hidden), :], sems.at[0])]
    count = len(mine)
    rows = own.shape[0]
    half = own.shape[1] // 2
    core = place_ref[2 * count + 1]
    blocks = down_blocks(rows, mine[0].shape[0])
    copies = [own_copy(place_ref, own, full, sems, rows)]
    for which, (refs, side) in enumerate(((mine, core), (others, 1 - core))):
        for i, ref in enumerate(refs):
            at = 1 + which * count + i
            side_at = pl.multiple_of(side * half, 128)
            for k, (start, tall) in enumerate(blocks):
                base = pl.multiple_of(place_ref[at] * rows + start, 16)
                copies.append(
                    pltpu.make_async_copy(
                        ref.at[pl.ds(0, tall), pl.ds(left + k * half, half)],
                        full.at[pl.ds(base, tall), pl.ds(side_at, half)],
                        sems.at[1 + (at - 1) * len(blocks) + k],
                    )
                )
    return copies


def pack_pieces(place_ref, in_ref, out_ref, down_ref, packed_ref, sems):
    half = in_ref.shape[0] // 2
    core = place_ref[place_ref.shape[0] - 2]
    base = pl.multiple_of(core * half, 16)
    wide, also = in_ref.shape[1], out_ref.shape[1]
    copies = [
        pltpu.make_async_copy(
            in_ref.at[pl.ds(base, half), :], packed_ref.at[:, pl.ds(0, wide)], sems.at[0]
        ),
        pltpu.make_async_copy(
            out_ref.at[pl.ds(base, half), :], packed_ref.at[:, pl.ds(wide, also)], sems.at[1]
        ),
    ]
    if packed_ref.shape[1] > wide + also:
        columns = down_ref.shape[1] // 2
        side = pl.multiple_of(core * columns, 128)
        for k, (start, tall) in enumerate(down_blocks(down_ref.shape[0], half)):
            copies.append(
                pltpu.make_async_copy(
                    down_ref.at[pl.ds(start, tall), pl.ds(side, columns)],
                    packed_ref.at[pl.ds(0, tall), pl.ds(wide + also + k * columns, columns)],
                    sems.at[2 + k],
                )
            )
    for copy in copies:
        copy.start()
    for copy in copies:
        copy.wait()


def run_pack_pieces(place, w_in, w_out, w_down, regular):
    half = w_in.shape[0] // 2
    blocks = len(down_blocks(w_down.shape[0], half)) if regular else 0
    wide = w_in.shape[1] + w_out.shape[1] + blocks * (w_down.shape[1] // 2)
    return pl.pallas_call(
        pack_pieces,
        name="pack_pieces",
        out_shape=jax.ShapeDtypeStruct((half, wide), BF16),
        in_specs=[smem_spec()] + [any_spec()] * 3,
        out_specs=vmem_spec(),
        scratch_shapes=[pltpu.SemaphoreType.DMA((2 + blocks,))],
        compiler_params=params(),
        cost_estimate=cost(1e6, 5e6),
    )(place, w_in, w_out, w_down)


def attention_forward(
    seq_count, heads, group, low_ref, high_ref, place_ref, x_hbm, order_ref, start_ref, end_ref,
    cos_ref, sin_ref, *refs,
):
    pieces, refs = refs[:-15], refs[-15:]
    gains_ref, normed_hbm, packed_ref, att_ref, out_ref, lse_ref = refs[:6]
    w_ref, x_ref, normed_ref, qkv_t, k_rows, o_rows, scores_ref, x_sems, normed_sems = refs[6:15]
    width = heads * HD
    rows = group // seq_count
    blocks = group // BLOCK
    fetches = [pltpu.make_async_copy(x_hbm.at[i], x_ref.at[i], x_sems.at[i]) for i in range(seq_count)]
    stores = [
        pltpu.make_async_copy(normed_ref.at[i], normed_hbm.at[i], normed_sems.at[i]) for i in range(seq_count)
    ]
    for fetch in fetches:
        fetch.start()
    if len(pieces) == 2:
        w_ref[...] = pieces[0][...]
        gains_ref[...] = pieces[1][...]
    else:
        tall = w_ref.shape[0] // len(pieces)
        for mask, piece in enumerate(pieces):
            base = pl.multiple_of((place_ref[0] ^ mask) * tall, 128)
            w_ref[pl.ds(base, tall), :] = piece[:tall]
            gains_ref[:, pl.ds(base, tall)] = piece[tall : tall + 2, :tall].astype(F32)
    gain_ref = gains_ref.at[pl.ds(0, 1), :]

    def project(i):
        x = x_ref[i].astype(F32)
        center = x - jnp.mean(x, axis=-1, keepdims=True)
        spread = jnp.mean(center * center, axis=-1, keepdims=True)
        normed = (center * lax.rsqrt(spread + NORM_EPS) * gain_ref[...]).astype(BF16)
        normed_ref[i] = normed
        qkv = nn_dot(normed, w_ref[...]).astype(BF16)
        qkv_t[i] = qkv.T

    for i in range(seq_count):
        fetches[i].wait()
        project(i)
        stores[i].start()

    def pack(i, carry):
        at = pl.ds(pl.multiple_of(i * BLOCK, BLOCK), BLOCK)
        order = order_ref[:, at]
        total = jnp.zeros((3 * width, BLOCK), F32)
        for s in range(seq_count):
            here = lax.broadcasted_iota(jnp.int32, (rows, BLOCK), 0) + s * rows
            hot = jnp.where(here == order, 1.0, 0.0).astype(BF16)
            total = total + nn_dot(qkv_t[s], hot)
        cos = cos_ref[:, at]
        sin = sin_ref[:, at]
        half = HD // 2
        for part in range(2):
            for h in range(heads):
                base = part * width + h * HD
                first = total[base : base + half]
                second = total[base + half : base + HD]
                turned = jnp.concatenate(
                    [first * cos - second * sin, second * cos + first * sin], axis=0
                ).astype(BF16)
                packed_ref[base : base + HD, at] = turned
                if part == 1:
                    k_rows[h, at, :] = turned.T
        packed_ref[2 * width :, at] = total[2 * width :].astype(BF16)
        return carry

    lax.fori_loop(0, blocks, pack, 0)
    scale = HD**-0.5 * LOG2E

    def attend(i, carry):
        at = pl.ds(pl.multiple_of(i * WIDE, WIDE), WIDE)
        start = start_ref[:, at]
        end = end_ref[:, at]
        queries = [packed_ref[h * HD : (h + 1) * HD, at] for h in range(heads)]

        low, high = low_ref[i], high_ref[i]

        def score(j, tops):
            there = pl.ds(pl.multiple_of(j * BLOCK, BLOCK), BLOCK)
            where = lax.broadcasted_iota(jnp.int32, (BLOCK, WIDE), 0) + j * BLOCK
            same = jnp.logical_and(where >= start, where < end)
            following = []
            for h in range(heads):
                scores = jnp.where(same, nn_dot(k_rows[h, there, :], queries[h]) * scale, -1e30)
                scores_ref[j, h] = scores
                following.append(jnp.maximum(tops[h], jnp.max(scores.reshape(-1, 8, WIDE), axis=0)))
            return tuple(following)

        tops = lax.fori_loop(low, high, score, tuple(jnp.full((8, WIDE), -1e30, F32) for _ in range(heads)))
        tops = [jnp.max(top, axis=0, keepdims=True) for top in tops]

        def weigh(j, state):
            there = pl.ds(pl.multiple_of(j * BLOCK, BLOCK), BLOCK)
            following = []
            for h in range(heads):
                total, acc = state[h]
                probs = jnp.exp2(scores_ref[j, h] - tops[h])
                total = total + jnp.sum(probs.reshape(-1, 8, WIDE), axis=0)
                base = 2 * width + h * HD
                acc = acc + nn_dot(packed_ref[base : base + HD, there], probs.astype(BF16))
                following.append((total, acc))
            return tuple(following)

        first = tuple((jnp.zeros((8, WIDE), F32), jnp.zeros((HD, WIDE), F32)) for _ in range(heads))
        last = lax.fori_loop(low, high, weigh, first)
        outs = []
        for h in range(heads):
            total, acc = last[h]
            total = jnp.sum(total, axis=0, keepdims=True)
            out = acc / total
            out_ref[h * HD : (h + 1) * HD, at] = out
            lse_ref[h : h + 1, at] = tops[h] + jnp.log2(total)
            outs.append(out)
        o_rows[at, :] = jnp.concatenate(outs, axis=0).astype(BF16).T
        return carry

    lax.fori_loop(0, group // WIDE, attend, 0)

    def arrive(i, carry):
        here = lax.broadcasted_iota(jnp.int32, (rows, group), 0) + i * rows
        hot = jnp.where(here == order_ref[...], 1.0, 0.0).astype(BF16)
        att_ref[i] = nn_dot(hot, o_rows[...]).astype(BF16)
        return carry

    lax.fori_loop(0, seq_count, arrive, 0)
    for store in stores:
        store.wait()


def run_attention_forward(place, x_all, pieces, layout, heads):
    seq_count, rows, dim = x_all.shape
    group = seq_count * rows
    width = heads * HD
    (low, high), _, order, start, end, cos, sin = layout
    return pl.pallas_call(
        functools.partial(attention_forward, seq_count, heads, group),
        name="attention_forward",
        out_shape=(
            jax.ShapeDtypeStruct((2, dim), F32),
            jax.ShapeDtypeStruct((seq_count, rows, dim), BF16),
            jax.ShapeDtypeStruct((3 * width, group), BF16),
            jax.ShapeDtypeStruct((seq_count, rows, width), BF16),
            jax.ShapeDtypeStruct((width, group), F32),
            jax.ShapeDtypeStruct((heads, group), F32),
        ),
        in_specs=[smem_spec()] * 3 + [any_spec()] + [vmem_spec()] * (5 + len(pieces)),
        out_specs=[vmem_spec(), any_spec()] + [vmem_spec()] * 4,
        scratch_shapes=[
            pltpu.VMEM((dim, 3 * width), BF16),
            pltpu.VMEM((seq_count, rows, dim), BF16),
            pltpu.VMEM((seq_count, rows, dim), BF16),
            pltpu.VMEM((seq_count, 3 * width, rows), BF16),
            pltpu.VMEM((heads, group, HD), BF16),
            pltpu.VMEM((group, width), BF16),
            pltpu.VMEM((group // BLOCK, heads, BLOCK, WIDE), F32),
            pltpu.SemaphoreType.DMA((seq_count,)),
            pltpu.SemaphoreType.DMA((seq_count,)),
        ],
        compiler_params=params(),
        cost_estimate=cost(24e9, 20e6),
    )(low, high, place, x_all, order, start, end, cos, sin, *pieces)


def attention_backward(
    seq_count, heads, group, low_ref, high_ref, dout_ref, packed_ref, out_ref, lse_ref, order_ref,
    start_ref, end_ref, cos_ref, sin_ref, grad_ref, dout_t, dpack_t, drows, qrows, krows, vrows,
    delta_ref, dq_t, grows,
):
    width = heads * HD
    rows = group // seq_count
    blocks = group // BLOCK
    scale = HD**-0.5

    def turn(i, carry):
        dout_t[i] = dout_ref[i].T
        return carry

    lax.fori_loop(0, seq_count, turn, 0)

    def pack(i, carry):
        at = pl.ds(pl.multiple_of(i * BLOCK, BLOCK), BLOCK)
        order = order_ref[:, at]
        total = jnp.zeros((width, BLOCK), F32)
        for s in range(seq_count):
            here = lax.broadcasted_iota(jnp.int32, (rows, BLOCK), 0) + s * rows
            hot = jnp.where(here == order, 1.0, 0.0).astype(BF16)
            total = total + nn_dot(dout_t[s], hot)
        dpack_t[:, at] = total.astype(BF16)
        for h in range(heads):
            mine = total[h * HD : (h + 1) * HD]
            delta_ref[h : h + 1, at] = jnp.sum(
                mine * out_ref[h * HD : (h + 1) * HD, at], axis=0, keepdims=True
            )
            drows[h, at, :] = mine.T.astype(BF16)
            for part, ref in enumerate((qrows, krows, vrows)):
                base = part * width + h * HD
                ref[h, at, :] = packed_ref[base : base + HD, at].T
        dq_t[:, at] = jnp.zeros((width, BLOCK), F32)
        return carry

    lax.fori_loop(0, blocks, pack, 0)

    def keys(j, carry):
        there = pl.ds(pl.multiple_of(j * BLOCK, BLOCK), BLOCK)
        where = lax.broadcasted_iota(jnp.int32, (BLOCK, WIDE), 0) + j * BLOCK

        def queries(i, state):
            at = pl.ds(pl.multiple_of(i * WIDE, WIDE), WIDE)
            same = jnp.logical_and(where >= start_ref[:, at], where < end_ref[:, at])
            following = []
            for h in range(heads):
                dk, dv = state[h]
                base = h * HD
                key_rows = krows[h, there, :]
                query_t = packed_ref[base : base + HD, at]
                scores = nn_dot(key_rows, query_t) * (scale * LOG2E)
                scores = jnp.where(same, scores, -1e30)
                probs = jnp.exp2(scores - lse_ref[h : h + 1, at])
                dprobs = nn_dot(vrows[h, there, :], dpack_t[base : base + HD, at])
                raw = (probs * (dprobs - delta_ref[h : h + 1, at]) * scale).astype(BF16)
                dv = dv + nn_dot(probs.astype(BF16), drows[h, at, :])
                dk = dk + nn_dot(raw, qrows[h, at, :])
                key_t = packed_ref[width + base : width + base + HD, there]
                dq_t[base : base + HD, at] += nn_dot(key_t, raw)
                following.append((dk, dv))
            return tuple(following)

        zero = jnp.zeros((BLOCK, HD), F32)
        last = lax.fori_loop(low_ref[j], high_ref[j], queries, tuple((zero, zero) for _ in range(heads)))
        cos = cos_ref[:, there]
        sin = sin_ref[:, there]
        half = HD // 2
        turned = []
        for h in range(heads):
            dk_t = last[h][0].T
            first, second = dk_t[:half], dk_t[half:]
            turned.append(first * cos + second * sin)
            turned.append(second * cos - first * sin)
        grows[there, width : 2 * width] = jnp.concatenate(turned, axis=0).T.astype(BF16)
        grows[there, 2 * width :] = jnp.concatenate([last[h][1] for h in range(heads)], axis=1).astype(BF16)
        return carry

    lax.fori_loop(0, blocks, keys, 0)

    def finish(i, carry):
        at = pl.ds(pl.multiple_of(i * BLOCK, BLOCK), BLOCK)
        cos = cos_ref[:, at]
        sin = sin_ref[:, at]
        half = HD // 2
        turned = []
        for h in range(heads):
            first = dq_t[h * HD : h * HD + half, at]
            second = dq_t[h * HD + half : (h + 1) * HD, at]
            turned.append(first * cos + second * sin)
            turned.append(second * cos - first * sin)
        grows[at, :width] = jnp.concatenate(turned, axis=0).T.astype(BF16)
        return carry

    lax.fori_loop(0, blocks, finish, 0)

    def arrive(i, carry):
        here = lax.broadcasted_iota(jnp.int32, (rows, group), 0) + i * rows
        hot = jnp.where(here == order_ref[...], 1.0, 0.0).astype(BF16)
        grad_ref[i] = nn_dot(hot, grows[...]).astype(BF16)
        return carry

    lax.fori_loop(0, seq_count, arrive, 0)


def run_attention_backward(dout, packed, out_t, lse, layout, heads):
    seq_count, rows, width = dout.shape
    group = seq_count * rows
    _, (low, high), order, start, end, cos, sin = layout
    return pl.pallas_call(
        functools.partial(attention_backward, seq_count, heads, group),
        name="attention_backward",
        out_shape=jax.ShapeDtypeStruct((seq_count, rows, 3 * width), BF16),
        in_specs=[smem_spec()] * 2 + [vmem_spec()] * 9,
        out_specs=vmem_spec(),
        scratch_shapes=[
            pltpu.VMEM((seq_count, width, rows), BF16),
            pltpu.VMEM((width, group), BF16),
            pltpu.VMEM((heads, group, HD), BF16),
            pltpu.VMEM((heads, group, HD), BF16),
            pltpu.VMEM((heads, group, HD), BF16),
            pltpu.VMEM((heads, group, HD), BF16),
            pltpu.VMEM((heads, group), F32),
            pltpu.VMEM((width, group), F32),
            pltpu.VMEM((group, 3 * width), BF16),
        ],
        compiler_params=params(),
        cost_estimate=cost(30e9, 10e6),
    )(low, high, dout, packed, out_t, lse, order, start, end, cos, sin)


def qkv_weight_grad(seq_count, place_ref, normed_ref, grad_ref, *refs):
    outs, (total, turned) = refs[:-2], refs[-2:]
    total[...] = jnp.zeros_like(total)

    def step(i, carry):
        total[...] += nn_dot(grad_ref[i].T, normed_ref[i])
        return carry

    lax.fori_loop(0, seq_count, step, 0)
    if len(outs) == 1:
        outs[0][...] = total[...].T.astype(BF16)
        return
    turned[...] = total[...].T
    rows = outs[0].shape[1]
    for ref, keys in zip(outs, ((2, 3), (1,), (0,))):
        for at, key in enumerate(keys):
            base = pl.multiple_of(place_ref[key] * rows, 16)
            ref[at] = turned[pl.ds(base, rows), :].astype(BF16)


def run_qkv_weight_grad(place, normed, grad, regular):
    seq_count, rows, dim = normed.shape
    width = grad.shape[-1]
    if regular:
        outs = tuple(jax.ShapeDtypeStruct((n, dim // 4, width), BF16) for n in (2, 1, 1))
    else:
        outs = (jax.ShapeDtypeStruct((dim, width), BF16),)
    return pl.pallas_call(
        functools.partial(qkv_weight_grad, seq_count),
        name="qkv_weight_grad",
        out_shape=outs,
        in_specs=[smem_spec()] + [vmem_spec()] * 2,
        out_specs=[vmem_spec()] * len(outs),
        scratch_shapes=[pltpu.VMEM((width, dim), F32), pltpu.VMEM((dim, width), F32)],
        compiler_params=params(),
        cost_estimate=cost(3e9, 6e6),
    )(place, normed, grad)


def padded(hidden):
    return -(-hidden // 128) * 128


def load_down(place_ref, refs, count, hidden, left, full, sems):
    copies = down_copies(place_ref, refs[0], refs[1 : 1 + count], refs[1 + count :], left, full, sems, hidden)
    for copy in copies:
        copy.start()
    tail = padded(hidden) - hidden
    if tail:
        full[pl.ds(hidden, tail), :] = jnp.zeros((tail, full.shape[1]), BF16)
    for copy in copies:
        copy.wait()


def down_semaphores(downs):
    if len(downs) == 1:
        return pltpu.SemaphoreType.DMA((1,))
    blocks = len(down_blocks(downs[0].shape[0], downs[1].shape[0]))
    return pltpu.SemaphoreType.DMA((1 + (len(downs) - 1) * blocks,))


def hidden_grad(hidden, left, place_ref, cot_ref, *refs):
    downs, (out_ref, full, sems) = refs[:-3], refs[-3:]
    load_down(place_ref, downs, (len(downs) - 1) // 2, hidden, left, full, sems)
    cot = cot_ref[...]
    tiles = padded(hidden) // 128

    def step(i, carry):
        at = pl.multiple_of(i * 128, 128)
        out_ref[:, pl.ds(at, 128)] = nt_dot(cot, full[pl.ds(at, 128), :])
        return carry

    lax.fori_loop(0, tiles, step, 0)


def run_hidden_grad(place, cot, downs, left, hidden):
    rows, dim = cot.shape
    return pl.pallas_call(
        functools.partial(hidden_grad, hidden, left),
        name="hidden_grad",
        out_shape=jax.ShapeDtypeStruct((rows, padded(hidden)), F32),
        in_specs=[smem_spec(), vmem_spec()] + [any_spec()] * len(downs),
        out_specs=vmem_spec(),
        scratch_shapes=[pltpu.VMEM((padded(hidden), dim), BF16), down_semaphores(downs)],
        compiler_params=params(),
        cost_estimate=cost(4e9, 9e6),
    )(place, cot, *downs)


def layer_result(hidden, left, place_ref, mid_ref, keep_ref, *refs):
    downs, (out_ref, full, sems) = refs[:-3], refs[-3:]
    load_down(place_ref, downs, (len(downs) - 1) // 2, hidden, left, full, sems)
    wide = padded(hidden)

    def step(i, carry):
        at = pl.ds(pl.multiple_of(i * 256, 256), 256)
        out_ref[:, at] = (mid_ref[:, at] + nn_dot(keep_ref[:, :wide], full[:, at])).astype(BF16)
        return carry

    lax.fori_loop(0, out_ref.shape[1] // 256, step, 0)


def run_layer_result(place, middle, keep, downs, left, hidden):
    rows, dim = middle.shape
    return pl.pallas_call(
        functools.partial(layer_result, hidden, left),
        name="layer_result",
        out_shape=jax.ShapeDtypeStruct((rows, dim), BF16),
        in_specs=[smem_spec()] + [vmem_spec()] * 2 + [any_spec()] * len(downs),
        out_specs=vmem_spec(),
        scratch_shapes=[pltpu.VMEM((padded(hidden), dim), BF16), down_semaphores(downs)],
        compiler_params=params(),
        cost_estimate=cost(4e9, 9e6),
    )(place, middle, keep, *downs)


def feed_forward(
    count, hidden, heads_width, place_ref, x_ref, att_ref, cot_ref, gain_ref, gh_hbm, *refs
):
    out_own, in_own, mine, others = refs[0], refs[1], refs[2 : 2 + count], refs[2 + count : 2 + 2 * count]
    mid_ref, gmid_ref, send_hbm, keep_hbm, ga_ref = refs[2 + 2 * count : 7 + 2 * count]
    wo, wi, both, early, late, send_ref, keep_ref, gh_ref, sem_o, sem_i, sems = refs[7 + 2 * count :]
    fetch = pltpu.make_async_copy(gh_hbm, gh_ref, sems.at[0])
    send_out = pltpu.make_async_copy(send_ref, send_hbm, sems.at[1])
    keep_out = pltpu.make_async_copy(keep_ref, keep_hbm, sems.at[2])
    dim = x_ref.shape[1]
    wide_hidden = padded(hidden)
    nt_ref = send_ref.at[:, pl.ds(2 * hidden, dim)]
    gboth_ref = send_ref
    hid_ref = keep_ref
    gbr_ref = keep_ref.at[:, pl.ds(wide_hidden, dim)]
    att_all_ref = keep_ref.at[:, pl.ds(wide_hidden + dim, dim)]
    keep_ref[:, pl.ds(wide_hidden + 2 * dim, dim)] = cot_ref[...]
    copies_o = row_copies(place_ref, out_own, mine, others, 2 * hidden, wo, sem_o)
    copies_i = row_copies(place_ref, in_own, mine, others, 0, wi, sem_i)
    for copy in copies_o:
        copy.start()
    for copy in copies_i:
        copy.start()
    fetch.start()
    att = jnp.concatenate([att_ref[s] for s in range(att_ref.shape[0])], axis=1)
    att_all_ref[...] = att
    for copy in copies_o:
        copy.wait()

    def branch(i, carry):
        at = pl.ds(pl.multiple_of(i * 256, 256), 256)
        mid_ref[:, at] = x_ref[:, at].astype(F32) + nn_dot(att_all_ref[...], wo[:, at])
        return carry

    lax.fori_loop(0, dim // 256, branch, 0)
    middle = mid_ref[...]
    center = middle - jnp.mean(middle, axis=-1, keepdims=True)
    spread = jnp.mean(center * center, axis=-1, keepdims=True)
    scale = lax.rsqrt(spread + NORM_EPS)
    nt_ref[...] = (center * scale * gain_ref[...]).astype(BF16)
    for copy in copies_i:
        copy.wait()
    fetch.wait()
    wide = 2 * hidden // 128

    def expand(i, carry):
        at = pl.ds(pl.multiple_of(i * 256, 256), 256)
        both[:, at] = nn_dot(nt_ref[...], wi[:, at])
        return carry

    lax.fori_loop(0, wide // 2, expand, 0)
    if wide % 2:
        both[:, pl.ds(128 * (wide - 1), 128)] = nn_dot(nt_ref[...], wi[:, pl.ds(128 * (wide - 1), 128)])
    both[:, pl.ds(128 * wide, 128)] = jnp.zeros((both.shape[0], 128), F32)
    tiles = padded(hidden) // 128
    whole = hidden // 128
    lanes = lax.broadcasted_iota(jnp.int32, (both.shape[0], 128), 1)
    shift = hidden % 128

    def tile(i):
        return pl.ds(pl.multiple_of(i * 128, 128), 128)

    def gates(i):
        a = both[:, tile(i)]
        if shift:
            left = pltpu.roll(both[:, tile(whole + i)], 128 - shift, 1)
            right = pltpu.roll(both[:, tile(whole + i + 1)], 128 - shift, 1)
            b = jnp.where(lanes < 128 - shift, left, right)
        else:
            b = both[:, tile(whole + i)]
        gh = gh_ref[:, tile(i)]
        phi = 0.5 * (1.0 + lax.erf(a * (0.5**0.5)))
        gelu = a * phi
        slope = phi + a * ((0.5 / math.pi) ** 0.5 * jnp.exp(-0.5 * a * a))
        hid_ref[:, tile(i)] = (gelu * b).astype(BF16)
        return gh * b * slope, gh * gelu

    if shift:
        first_a, first_b = gates(0)
        gboth_ref[:, tile(0)] = first_a.astype(BF16)
        early[...] = pltpu.roll(first_b, shift, 1)
        late[...] = early[...]

        def inner(i, carry):
            ga, gb = gates(i)
            turned = pltpu.roll(gb, shift, 1)
            gboth_ref[:, tile(i)] = ga.astype(BF16)
            gboth_ref[:, tile(whole + i)] = jnp.where(lanes < shift, late[...], turned).astype(BF16)
            late[...] = turned
            return carry

        lax.fori_loop(1, tiles - 1, inner, 0)
        ga, gb = gates(tiles - 1)
        turned = pltpu.roll(gb, shift, 1)
        gboth_ref[:, tile(whole)] = jnp.where(lanes < shift, ga, early[...]).astype(BF16)
        gboth_ref[:, tile(2 * whole)] = jnp.where(lanes < shift, late[...], turned).astype(BF16)
    else:

        def inner(i, carry):
            ga, gb = gates(i)
            gboth_ref[:, tile(i)] = ga.astype(BF16)
            gboth_ref[:, tile(whole + i)] = gb.astype(BF16)
            return carry

        lax.fori_loop(0, tiles, inner, 0)

    send_out.start()

    def back(i, carry):
        at = pl.multiple_of(i * 128, 128)
        both[:, pl.ds(at, 128)] = nt_dot(gboth_ref[:, : 2 * hidden], wi[pl.ds(at, 128), :])
        return carry

    lax.fori_loop(0, dim // 128, back, 0)
    middle = mid_ref[...]
    center = middle - jnp.mean(middle, axis=-1, keepdims=True)
    spread = jnp.mean(center * center, axis=-1, keepdims=True)
    scale = lax.rsqrt(spread + NORM_EPS)
    normal = center * scale
    e = both[:, pl.ds(0, dim)] * gain_ref[...]
    pull = e - jnp.mean(e, axis=-1, keepdims=True) - normal * jnp.mean(e * normal, axis=-1, keepdims=True)
    gmid = cot_ref[...].astype(F32) + scale * pull
    gmid_ref[...] = gmid
    gbr_ref[...] = gmid.astype(BF16)
    keep_out.start()

    def spread_out(i, carry):
        at = pl.multiple_of(i * 128, 128)
        both[:, pl.ds(at, 128)] = nt_dot(gbr_ref[...], wo[pl.ds(at, 128), :])
        return carry

    lax.fori_loop(0, dim // 128, spread_out, 0)
    for s in range(att_ref.shape[0]):
        ga_ref[s] = both[:, s * heads_width : (s + 1) * heads_width].astype(BF16)
    send_out.wait()
    keep_out.wait()


def run_feed_forward(place, x, att, cot, gain, grad_hidden, w_out, w_in, mine, others, hidden):
    rows, dim = x.shape
    seq_count, _, heads_width = att.shape
    count = len(mine)
    return pl.pallas_call(
        functools.partial(feed_forward, count, hidden, heads_width),
        name="feed_forward",
        out_shape=(
            jax.ShapeDtypeStruct((rows, dim), F32),
            jax.ShapeDtypeStruct((rows, dim), F32),
            jax.ShapeDtypeStruct((rows, 2 * hidden + dim), BF16),
            jax.ShapeDtypeStruct((rows, padded(hidden) + 3 * dim), BF16),
            jax.ShapeDtypeStruct((seq_count, rows, heads_width), BF16),
        ),
        in_specs=[smem_spec()] + [vmem_spec()] * 4 + [any_spec()] * (3 + 2 * count),
        out_specs=[vmem_spec()] * 2 + [any_spec()] * 2 + [vmem_spec()],
        scratch_shapes=[
            pltpu.VMEM((dim, dim), BF16),
            pltpu.VMEM((dim, 2 * hidden), BF16),
            pltpu.VMEM((rows, 2 * hidden + 128), F32),
            pltpu.VMEM((rows, 128), F32),
            pltpu.VMEM((rows, 128), F32),
            pltpu.VMEM((rows, 2 * hidden + dim), BF16),
            pltpu.VMEM((rows, padded(hidden) + 3 * dim), BF16),
            pltpu.VMEM((rows, padded(hidden)), F32),
            pltpu.SemaphoreType.DMA((2 * count + 1,)),
            pltpu.SemaphoreType.DMA((2 * count + 1,)),
            pltpu.SemaphoreType.DMA((3,)),
        ],
        compiler_params=params(),
        cost_estimate=cost(16e9, 24e6),
    )(place, x, att, cot, gain, grad_hidden, w_out, w_in, *mine, *others)


ORDER = (0, 2, 1, 3)


def in_grad(hidden, wide, place_ref, send_ref, other_ref, a_ref, b_ref, c_ref, turned, picked):
    tokens = send_ref.shape[0]
    rows = turned.shape[0] // 4
    half, short = rows // 2, rows // 8

    @pl.when(pl.program_id(0) == 0)
    def _():
        turned[:, :tokens] = send_ref[:, 2 * hidden :].T
        turned[:, tokens:] = other_ref[:, 2 * hidden :].T
        core, z = place_ref[7], place_ref[8]
        for at, key in enumerate((2, 3, 1, 0)):
            for j, k in enumerate(ORDER):
                base = pl.multiple_of(place_ref[key] * rows + core * half + (z ^ k) * short, 16)
                to = at * half + j * short
                picked[to : to + short, :] = turned[pl.ds(base, short), :]

    at = pl.ds(pl.multiple_of(pl.program_id(0) * wide, 128), wide)
    right = jnp.concatenate([send_ref[:, at], other_ref[:, at]], axis=0)
    result = nn_dot(picked[...], right).astype(BF16)
    a_ref[0] = result[:half]
    a_ref[1] = result[half : 2 * half]
    b_ref[0] = result[2 * half : 3 * half]
    c_ref[0] = result[3 * half :]


def run_in_grad(place, send, other, hidden):
    tokens = send.shape[0]
    features = send.shape[1] - 2 * hidden
    columns = 2 * hidden
    half = features // 8
    wide = 896
    whole = pl.BlockSpec(send.shape, lambda i: (0, 0))
    return pl.pallas_call(
        functools.partial(in_grad, hidden, wide),
        name="in_grad",
        out_shape=tuple(jax.ShapeDtypeStruct((n, half, columns), BF16) for n in (2, 1, 1)),
        grid=(pl.cdiv(columns, wide),),
        in_specs=[smem_spec(), whole, whole],
        out_specs=[pl.BlockSpec((n, half, wide), lambda i: (0, 0, i)) for n in (2, 1, 1)],
        scratch_shapes=[
            pltpu.VMEM((features, 2 * tokens), BF16),
            pltpu.VMEM((features // 2, 2 * tokens), BF16),
        ],
        compiler_params=params(),
        cost_estimate=cost(2.0 * 2 * tokens * features * columns, 4 * tokens * columns + features * columns),
    )(place, send, other)


def rest_grad(hidden, place_ref, keep_ref, other_ref, a_ref, b_ref, c_ref, turned, picked):
    tokens = keep_ref.shape[0]
    wide = padded(hidden)
    dim = (keep_ref.shape[1] - wide) // 3
    half = dim // 2
    down_rows = hidden // 4
    short = dim // 32
    core, z = place_ref[7], place_ref[8]
    at = pl.program_id(0)

    @pl.when(at == 0)
    def _():
        turned[:wide, :tokens] = keep_ref[:, :wide].T
        turned[:wide, tokens:] = other_ref[:, :wide].T
        turned[wide:, :tokens] = keep_ref[:, wide + dim : wide + 2 * dim].T
        turned[wide:, tokens:] = other_ref[:, wide + dim : wide + 2 * dim].T
        for j, k in enumerate(ORDER):
            left = pl.ds(pl.multiple_of(wide + 2 * dim + core * half + (z ^ k) * 128, 128), 128)
            picked[:tokens, j * 128 : (j + 1) * 128] = keep_ref[:, left]
            picked[tokens:, j * 128 : (j + 1) * 128] = other_ref[:, left]
        picked[:tokens, half:] = keep_ref[:, wide : wide + dim]
        picked[tokens:, half:] = other_ref[:, wide : wide + dim]

    owner = place_ref[jnp.where(at < 2, at + 2, 3 - at)]
    base = pl.multiple_of(owner * down_rows, 16)
    down = nn_dot(turned[pl.ds(base, down_rows), :], picked[:, :half]).astype(BF16)
    left = []
    for k in ORDER:
        base = pl.multiple_of(wide + owner * 8 * short + core * 4 * short + (z ^ k) * short, 16)
        left.append(turned[pl.ds(base, short), :])
    out = nn_dot(jnp.concatenate(left, axis=0), picked[:, half:]).astype(BF16)
    first = dim // 128 * short

    def store(ref):
        for j in range(4):
            for t in range(dim // 128):
                ref[0, j, t * short : (t + 1) * short, :] = out[
                    j * short : (j + 1) * short, t * 128 : (t + 1) * 128
                ]
            ref[0, j, first:, :] = down[:, j * 128 : (j + 1) * 128]

    pl.when(at < 2)(lambda: store(a_ref))
    pl.when(at == 2)(lambda: store(b_ref))
    pl.when(at == 3)(lambda: store(c_ref))


def run_rest_grad(place, keep, other, hidden):
    tokens = keep.shape[0]
    wide = padded(hidden)
    dim = (keep.shape[1] - wide) // 3
    tall = dim // 128 * (dim // 32) + hidden // 4
    whole = pl.BlockSpec(keep.shape, lambda i: (0, 0))
    return pl.pallas_call(
        functools.partial(rest_grad, hidden),
        name="rest_grad",
        out_shape=tuple(jax.ShapeDtypeStruct((n, 4, tall, 128), BF16) for n in (2, 1, 1)),
        grid=(4,),
        in_specs=[smem_spec(), whole, whole],
        out_specs=[
            pl.BlockSpec((1, 4, tall, 128), lambda i: (jnp.minimum(i, 1), 0, 0, 0)),
            pl.BlockSpec((1, 4, tall, 128), lambda i: (0, 0, 0, 0)),
            pl.BlockSpec((1, 4, tall, 128), lambda i: (0, 0, 0, 0)),
        ],
        scratch_shapes=[
            pltpu.VMEM((wide + dim, 2 * tokens), BF16),
            pltpu.VMEM((2 * tokens, dim + dim // 2), BF16),
        ],
        compiler_params=params(),
        cost_estimate=cost(4e9, 10e6),
    )(place, keep, other)


def unpack_in(place_ref, *refs):
    pieces, w_ref, out_ref, sum_ref = refs[:4], refs[4], refs[5], refs[6]
    at = pl.program_id(0)
    for q, ref in enumerate(pieces):

        @pl.when(at // 2 == q)
        def _(ref=ref):
            value = ref[0].astype(F32)
            out_ref[...] = value
            sum_ref[...] = jnp.sum(value * w_ref[...].astype(F32), axis=1, keepdims=True)


def row_block(i, place_ref):
    order = jnp.where(i % 4 == 1, 2, jnp.where(i % 4 == 2, 1, i % 4))
    side = jnp.where(i < 4, place_ref[7], 1 - place_ref[7])
    return (side * 4 + (place_ref[8] ^ order), 0)


def run_unpack_in(place, pieces, weight):
    rows, columns = weight.shape
    short = rows // 8
    specs = [
        pl.BlockSpec((1, short, columns), lambda i, p, q=q: (jnp.clip(i - 2 * q, 0, 1), 0, 0))
        for q in range(4)
    ]
    block = pl.BlockSpec((short, columns), row_block)
    return pl.pallas_call(
        unpack_in,
        name="unpack_in",
        out_shape=(jax.ShapeDtypeStruct((rows, columns), F32), jax.ShapeDtypeStruct((rows, 1), F32)),
        grid_spec=pltpu.PrefetchScalarGridSpec(
            num_scalar_prefetch=1,
            grid=(8,),
            in_specs=specs + [block],
            out_specs=[block, pl.BlockSpec((short, 1), row_block)],
        ),
        compiler_params=params(),
        cost_estimate=cost(1e7, 11e6),
    )(place, *pieces, weight)


def sources(place_ref, pieces):
    core, z = place_ref[7], place_ref[8]
    for q, ref in enumerate(pieces):
        for at in range(2):
            yield ref.at[at], (core if q < 2 else 1 - core), z ^ ORDER[2 * (q % 2) + at]


def unpack_rest(place_ref, *refs):
    pieces, out_ref, down_ref = refs[:4], refs[4], refs[5]
    dim = out_ref.shape[1]
    short = dim // 32
    first = dim // 128 * short
    for ref, side, z in sources(place_ref, pieces):
        base = pl.multiple_of(side * 4 * short + z * short, 16)
        for t in range(dim // 128):
            out_ref[pl.ds(base, short), t * 128 : (t + 1) * 128] = ref[
                t * short : (t + 1) * short, :
            ].astype(F32)
        left = pl.multiple_of(side * (dim // 2) + z * 128, 128)
        down_ref[:, pl.ds(left, 128)] = ref[first:, :].astype(F32)


def run_unpack_rest(place, pieces, out_shape, down_shape):
    return pl.pallas_call(
        unpack_rest,
        name="unpack_rest",
        out_shape=(jax.ShapeDtypeStruct(out_shape, F32), jax.ShapeDtypeStruct(down_shape, F32)),
        in_specs=[smem_spec()] + [vmem_spec()] * 4,
        out_specs=[vmem_spec()] * 2,
        compiler_params=params(),
        cost_estimate=cost(1e7, 6e6),
    )(place, *pieces)


def unpack_qkv(place_ref, *refs):
    pieces, w_ref, out_ref, sum_ref = refs[:4], refs[4], refs[5], refs[6]
    width = pieces[0].shape[2] // 3
    dim = out_ref.shape[1] // 3
    total = jnp.zeros_like(sum_ref)
    for ref, side, z in sources(place_ref, pieces):
        for part in range(3):
            left = pl.multiple_of(part * dim + (z * 2 + side) * width, 128)
            value = ref[:, part * width : (part + 1) * width].astype(F32)
            out_ref[:, pl.ds(left, width)] = value
            weight = w_ref[:, pl.ds(left, width)].astype(F32)
            total = total + jnp.sum(value * weight, axis=1, keepdims=True)
    sum_ref[...] = total


def run_unpack_qkv(place, pieces, weight):
    return pl.pallas_call(
        unpack_qkv,
        name="unpack_qkv",
        out_shape=(
            jax.ShapeDtypeStruct(weight.shape, F32),
            jax.ShapeDtypeStruct((weight.shape[0], 1), F32),
        ),
        in_specs=[smem_spec()] + [vmem_spec()] * 5,
        out_specs=[vmem_spec()] * 2,
        compiler_params=params(),
        cost_estimate=cost(1e7, 7e6),
    )(place, *pieces, weight)


def input_grad(count, place_ref, x_ref, gmid_ref, gain_ref, g_ref, *refs):
    weights, (out_ref, full, grad, total, sems) = refs[:-5], refs[-5:]
    seq_count, _, width = g_ref.shape
    width //= 3
    dim = x_ref.shape[1]
    copies = row_copies(place_ref, weights[0], weights[1 : 1 + count], weights[1 + count :], 0, full, sems)
    for copy in copies:
        copy.start()
    grad[...] = jnp.concatenate(
        [g_ref[s][:, part * width : (part + 1) * width] for part in range(3) for s in range(seq_count)],
        axis=1,
    )
    for copy in copies:
        copy.wait()

    def step(i, carry):
        at = pl.multiple_of(i * 128, 128)
        total[:, pl.ds(at, 128)] = nt_dot(grad[...], full[pl.ds(at, 128), :])
        return carry

    lax.fori_loop(0, dim // 128, step, 0)
    x = x_ref[...].astype(F32)
    center = x - jnp.mean(x, axis=-1, keepdims=True)
    spread = jnp.mean(center * center, axis=-1, keepdims=True)
    scale = lax.rsqrt(spread + NORM_EPS)
    normal = center * scale
    e = total[...] * gain_ref[...]
    pull = e - jnp.mean(e, axis=-1, keepdims=True) - normal * jnp.mean(e * normal, axis=-1, keepdims=True)
    out_ref[...] = (gmid_ref[...] + scale * pull).astype(BF16)


def run_input_grad(place, x, gmid, gain, grads, weights, count):
    rows, dim = x.shape
    columns = weights[0].shape[1]
    return pl.pallas_call(
        functools.partial(input_grad, count),
        name="input_grad",
        out_shape=jax.ShapeDtypeStruct((rows, dim), BF16),
        in_specs=[smem_spec()] + [vmem_spec()] * 4 + [any_spec()] * len(weights),
        out_specs=vmem_spec(),
        scratch_shapes=[
            pltpu.VMEM((dim, columns), BF16),
            pltpu.VMEM((rows, columns), BF16),
            pltpu.VMEM((rows, dim), F32),
            pltpu.SemaphoreType.DMA((2 * count + 1,)),
        ],
        compiler_params=params(),
        cost_estimate=cost(4e9, 10e6),
    )(place, x, gmid, gain, grads, *weights)


def sequence_layout(lengths, order, group):
    ends = jnp.cumsum(lengths)
    starts = ends - lengths
    index = jnp.arange(group, dtype=jnp.int32)
    passed = index[:, None] >= ends[None, :]
    start = jnp.sum(jnp.where(passed, lengths[None, :], 0), axis=1).astype(jnp.int32)
    inside = jnp.logical_and(index[:, None] >= starts[None, :], jnp.logical_not(passed))
    end = jnp.sum(jnp.where(inside, ends[None, :], 0), axis=1).astype(jnp.int32)
    places = index - start
    half = HD // 2
    speeds = jnp.power(F32(ROPE_BASE), -2.0 * jnp.arange(half, dtype=F32) / HD)
    angles = speeds[:, None] * places.astype(F32)[None, :]
    keys = (start[::WIDE] // BLOCK, (end[WIDE - 1 :: WIDE] + BLOCK - 1) // BLOCK)
    queries = (start[::BLOCK] // WIDE, (end[BLOCK - 1 :: BLOCK] + WIDE - 1) // WIDE)
    return (keys, queries, order[None, :], start[None, :], end[None, :], jnp.cos(angles), jnp.sin(angles))


def local(tokens, seq_lengths, seq_order, norm_one, w_qkv, w_out, norm_two, w_in, w_down, cotangent):
    seq_count = lax.axis_size("seq")
    fsdp_count = lax.axis_size("fsdp")
    levels = fsdp_count.bit_length() - 1
    count = fsdp_count - 1
    seq_at = lax.axis_index("seq")
    fsdp_at = lax.axis_index("fsdp")
    core = seq_at % 2
    x = tokens[0]
    cot = cotangent[0]
    rows, dim = x.shape
    group = rows * seq_count
    heads = dim // HD // seq_count
    width = heads * HD
    hidden = w_in.shape[1] // 2
    def gather(piece, *others):
        return plane_gather(piece, seq_count, fsdp_count, *others)

    swap = functools.partial(core_swap, seq_count=seq_count)

    keys = [jnp.array([plane_mask(c, key, levels) for key in range(1, fsdp_count)], jnp.int32) for c in (0, 1)]
    mine = fsdp_at ^ jnp.where(core == 0, keys[0], keys[1])
    other = fsdp_at ^ jnp.where(core == 0, keys[1], keys[0])
    place = jnp.stack([fsdp_at, *mine, *other, core, seq_at // 2]).astype(jnp.int32)

    regular = fsdp_count == 4 and seq_count == 8 and w_down.shape[0] % 16 == 0 and dim == 1024

    x_all = lax.all_gather(x, "seq", axis=0, tiled=False)
    own_heads = lax.dynamic_slice_in_dim(w_qkv.reshape(w_qkv.shape[0], 3, dim), seq_at * width, width, 2)
    own_heads = own_heads.reshape(w_qkv.shape[0], 3 * width)
    gains = jnp.stack([norm_one, norm_two])
    if regular:
        extra = jnp.pad(gains, ((0, 14), (0, 3 * width - gains.shape[1])))
        own_heads = jnp.concatenate([own_heads, extra], axis=0)
        head_pieces = [own_heads] + [
            lax.ppermute(own_heads, "fsdp", [(f, f ^ mask) for f in range(4)]) for mask in (1, 2, 3)
        ]
    else:
        head_pieces = [
            lax.all_gather(own_heads, "fsdp", axis=0, tiled=True),
            lax.all_gather(gains, "fsdp", axis=1, tiled=True).astype(F32),
        ]
    piece = run_pack_pieces(place, w_in, w_out, w_down, regular)
    mine = gather(piece)
    left = 2 * hidden + dim

    layout = sequence_layout(seq_lengths[0], seq_order[0], group)
    gains, normed, packed, att, out_t, lse = run_attention_forward(place, x_all, head_pieces, layout, heads)
    gain_one, gain_two = gains[:1], gains[1:]
    qkv_piece = lax.dynamic_slice_in_dim(w_qkv, core * (w_qkv.shape[0] // 2), w_qkv.shape[0] // 2, 0)
    att_done = lax.all_to_all(att, "seq", split_axis=0, concat_axis=0, tiled=True)
    others = [swap(mine[0])] + [swap(after(p, att, *([att_done] if i else []))) for i, p in enumerate(mine[1:])]
    if regular:
        downs = [w_down] + mine + others
    else:
        downs = [lax.all_gather(w_down, "fsdp", axis=0, tiled=True)]
    att = att_done
    qkv_mine = gather(after(qkv_piece, att))
    grad_hidden = run_hidden_grad(place, cot, downs, left, hidden)
    middle, gmid, send, keep, gatt = run_feed_forward(
        place, x, after(att, qkv_mine[0]), cot, gain_two, grad_hidden, w_out, w_in, mine, others, hidden
    )
    send = after(send, *qkv_mine)
    qkvs = [w_qkv] + qkv_mine + [swap(p) for p in qkv_mine]
    dout = lax.all_to_all(gatt, "seq", split_axis=0, concat_axis=0, tiled=True)
    reduce = functools.partial(plane_reduce, seq_count=seq_count, fsdp_count=fsdp_count)
    send_other, keep_other = swap(send), swap(keep)
    wide = padded(hidden)
    if regular:
        short = w_in.shape[0] // 8
        in_a, in_b, in_c = run_in_grad(place, send, send_other, hidden)
        rest_a, rest_b, rest_c = run_rest_grad(place, keep, after(keep_other, in_b), hidden)
        dout = after(dout, in_b, rest_b)
        in_a = plane_swap(in_a, 1, seq_count, fsdp_count)
        rest_a = plane_swap(rest_a, 1, seq_count, fsdp_count)
    else:
        rest_a = keep_other

    grads = run_attention_backward(dout, packed, out_t, lse, layout, heads)
    layer_out = run_layer_result(place, middle, after(keep, grads), downs, left, hidden)
    grad_rows = lax.all_to_all(grads, "seq", split_axis=0, concat_axis=0, tiled=True)
    gw_heads = run_qkv_weight_grad(place, normed, after(grads, rest_a), regular)
    grad_tokens = run_input_grad(place, x, gmid, gain_one, grad_rows, qkvs, count)
    each = w_qkv.shape[0]
    if regular:
        in_parts = [p.reshape(4, short, 2 * hidden) for p in reduce(in_a, in_b, in_c)]
        in_parts[2] = after(in_parts[2], grad_rows, layer_out)
        rest_parts = reduce(rest_a, rest_b, rest_c)
        in_block = line_reduce(in_parts, seq_count)
        rest_block = line_reduce(rest_parts, seq_count)
        in_pieces = line_gather(after(in_block, grad_tokens), seq_count)
        rest_pieces = line_gather(rest_block, seq_count)
        qkv_a, qkv_b, qkv_c = gw_heads
        qkv_a = plane_swap(qkv_a, 1, seq_count, fsdp_count)
        qkv_pieces = line_gather(added(*reduce(qkv_a, qkv_b, qkv_c)), seq_count)
        gw_qkv, sum_qkv = run_unpack_qkv(place, qkv_pieces, w_qkv)
        gw_in, sum_in = run_unpack_in(place, in_pieces, w_in)
        gw_out, gw_down = run_unpack_rest(place, rest_pieces, w_out.shape, w_down.shape)
        sum_qkv = sum_qkv[:, 0]
        sum_in = sum_in[:, 0]
    else:

        def total(left_rows, right_rows):
            full = lax.dot_general(
                left_rows, right_rows, (((0,), (0,)), ((), ())), preferred_element_type=F32
            )
            return lax.psum(lax.psum_scatter(full, "fsdp", scatter_dimension=0, tiled=True), "seq")

        gw_in = total(send[:, 2 * hidden :], send[:, : 2 * hidden])
        gw_down = total(keep[:, :hidden], cot)
        gw_out = total(keep[:, wide + dim : wide + 2 * dim], keep[:, wide : wide + dim])
        sum_in = jnp.sum(gw_in * w_in.astype(F32), axis=1)
        gw_heads = lax.all_to_all(gw_heads[0].reshape(fsdp_count, each, -1), "fsdp", 0, 0, tiled=True)
        gw_heads = jnp.sum(gw_heads.astype(F32), axis=0).astype(BF16)
        gw_qkv = lax.all_gather(gw_heads, "seq", axis=0, tiled=False).reshape(seq_count, each, 3, width)
        gw_qkv = gw_qkv.transpose(1, 2, 0, 3).reshape(each, 3 * dim).astype(F32)
        sum_qkv = jnp.sum(gw_qkv * w_qkv.astype(F32), axis=1)

    grad_one = sum_qkv / norm_one.astype(F32)
    grad_two = sum_in / norm_two.astype(F32)
    return (layer_out[None], grad_tokens[None], grad_one, gw_qkv, gw_out, grad_two, gw_in, gw_down)


def solution(mesh):
    tokens = P("fsdp", "seq", None)
    rows = P("fsdp", None)
    return jax.shard_map(
        local,
        mesh=mesh,
        in_specs=(tokens, rows, rows, P("fsdp"), rows, rows, P("fsdp"), rows, rows, tokens),
        out_specs=(tokens, tokens, P("fsdp"), rows, rows, P("fsdp"), rows, rows),
        check_vma=False,
    )
```

```python
import functools
import math

import jax
import jax.numpy as jnp
from jax import lax
from jax.experimental import pallas as pl
from jax.experimental.pallas import tpu as pltpu
from jax.sharding import PartitionSpec as P

HD = 64
NORM_EPS = 1e-05
ROPE_BASE = 160000.0
BLOCK = 256
WIDE = 512
LOG2E = math.log2(math.e)
AXES = ("seq", "fsdp")
F32 = jnp.float32
BF16 = jnp.bfloat16
VMEM_LIMIT = 60 * 1024 * 1024


def core_swap(value, seq_count):
    return lax.ppermute(value, "seq", [(i, i ^ 1) for i in range(seq_count)])


def plane_bit(core, phase, levels):
    return (phase + core * (levels // 2)) % levels


def plane_mask(core, key, levels):
    mask = 0
    for phase in range(levels):
        if key >> phase & 1:
            mask |= 1 << plane_bit(core, phase, levels)
    return mask


def plane_swap(value, phase, seq_count, fsdp_count):
    levels = fsdp_count.bit_length() - 1
    pairs = []
    for s in range(seq_count):
        step = 1 << plane_bit(s & 1, phase, levels)
        for f in range(fsdp_count):
            pairs.append((s * fsdp_count + f, s * fsdp_count + (f ^ step)))
    return lax.ppermute(value, AXES, pairs)


def after(value, *others):
    return lax.optimization_barrier((value, *others))[0]


def plane_gather_rest(piece, first, seq_count, fsdp_count, *others):
    pieces = [after(piece, first, *others), after(first, *others)]
    for phase in range(1, fsdp_count.bit_length() - 1):
        pieces = pieces + [plane_swap(p, phase, seq_count, fsdp_count) for p in pieces]
    return [first] + pieces[2:]


def added(*values):
    return sum(v.astype(F32) for v in values).astype(BF16)


def plane_reduce(first, b, c, seq_count, fsdp_count):
    second = plane_swap(added(b[0], first[1]), 0, seq_count, fsdp_count)
    return c[0], first[0], second


def line_swap(value, level, seq_count):
    return lax.ppermute(value, "seq", [(i, i ^ (2 << (level ^ (i & 1)))) for i in range(seq_count)])


def line_reduce(parts, seq_count):
    got = line_swap(added(*(p[2:] for p in parts)), 0, seq_count)
    last = line_swap(added(*(p[1] for p in parts), got[1]), 1, seq_count)
    return added(*(p[0] for p in parts), got[0], last)


def line_gather(block, seq_count, *others):
    pair = jnp.stack([block, line_swap(block, 1, seq_count)])
    rest = line_swap(pair, 0, seq_count)
    return [pair, rest, core_swap(pair, seq_count), core_swap(after(rest, *others), seq_count)]


def any_spec():
    return pl.BlockSpec(memory_space=pl.ANY)


def vmem_spec():
    return pl.BlockSpec(memory_space=pltpu.VMEM)


def smem_spec():
    return pl.BlockSpec(memory_space=pltpu.SMEM)


def params():
    return pltpu.CompilerParams(vmem_limit_bytes=VMEM_LIMIT)


def cost(flops, moved):
    return pl.CostEstimate(flops=int(flops), bytes_accessed=int(moved), transcendentals=0)


def nt_dot(a, b):
    return lax.dot_general(a, b, (((1,), (1,)), ((), ())), preferred_element_type=F32)


def nn_dot(a, b):
    return jnp.dot(a, b, preferred_element_type=F32)


def own_copy(place_ref, own, full, sems, rows):
    base = pl.multiple_of(place_ref[0] * rows, 16)
    return pltpu.make_async_copy(own, full.at[pl.ds(base, rows), :], sems.at[0])


def row_copies(place_ref, own, mine, others, left, full, sems):
    count = len(mine)
    rows = own.shape[0]
    half = rows // 2
    core = place_ref[2 * count + 1]
    copies = [own_copy(place_ref, own, full, sems, rows)]
    for which, (refs, side) in enumerate(((mine, core), (others, 1 - core))):
        for i, ref in enumerate(refs):
            at = 1 + which * count + i
            base = pl.multiple_of(place_ref[at] * rows + side * half, 16)
            copies.append(
                pltpu.make_async_copy(
                    ref.at[:, pl.ds(left, full.shape[1])], full.at[pl.ds(base, half), :], sems.at[at]
                )
            )
    return copies


def down_blocks(rows, columns, tall):
    whole = rows // tall
    blocks = [(k * tall, 0, tall, columns, 0, k * columns) for k in range(whole)]
    left = rows - whole * tall
    if left:
        blocks += [
            (whole * tall, 128 * q, left, 128, q * left, whole * columns) for q in range(columns // 128)
        ]
    return blocks


def down_width(rows, columns, tall):
    return rows // tall * columns + (128 if rows % tall else 0)


def down_copies(place_ref, own, mine, others, left, full, sems, hidden):
    if not mine:
        return [pltpu.make_async_copy(own, full.at[pl.ds(0, hidden), :], sems.at[0])]
    count = len(mine)
    rows = own.shape[0]
    half = own.shape[1] // 2
    core = place_ref[2 * count + 1]
    blocks = down_blocks(rows, half, mine[0].shape[0])
    copies = [own_copy(place_ref, own, full, sems, rows)]
    for which, (refs, side) in enumerate(((mine, core), (others, 1 - core))):
        for i, ref in enumerate(refs):
            at = 1 + which * count + i
            side_at = pl.multiple_of(side * half, 128)
            for k, (row, column, tall, wide, packed_row, packed_column) in enumerate(blocks):
                base = pl.multiple_of(place_ref[at] * rows + row, 16)
                copies.append(
                    pltpu.make_async_copy(
                        ref.at[pl.ds(packed_row, tall), pl.ds(left + packed_column, wide)],
                        full.at[pl.ds(base, tall), pl.ds(pl.multiple_of(side_at + column, 128), wide)],
                        sems.at[1 + (at - 1) * len(blocks) + k],
                    )
                )
    return copies


def pack_pieces(place_ref, in_ref, out_ref, down_ref, first_ref, second_ref, sems):
    half = in_ref.shape[0] // 2
    core = place_ref[place_ref.shape[0] - 2]
    base = pl.multiple_of(core * half, 16)
    also = out_ref.shape[1]
    copies = [
        pltpu.make_async_copy(
            out_ref.at[pl.ds(base, half), :], first_ref.at[:, pl.ds(0, also)], sems.at[0]
        ),
        pltpu.make_async_copy(in_ref.at[pl.ds(base, half), :], second_ref, sems.at[1]),
    ]
    if first_ref.shape[1] > also:
        columns = down_ref.shape[1] // 2
        side = pl.multiple_of(core * columns, 128)
        blocks = down_blocks(down_ref.shape[0], columns, half)
        for k, (row, column, tall, part, packed_row, packed_column) in enumerate(blocks):
            copies.append(
                pltpu.make_async_copy(
                    down_ref.at[pl.ds(row, tall), pl.ds(pl.multiple_of(side + column, 128), part)],
                    first_ref.at[pl.ds(packed_row, tall), pl.ds(also + packed_column, part)],
                    sems.at[2 + k],
                )
            )
    for copy in copies:
        copy.start()
    for copy in copies:
        copy.wait()


def run_pack_pieces(place, w_in, w_out, w_down, regular):
    half = w_in.shape[0] // 2
    down = (w_down.shape[0], w_down.shape[1] // 2, half)
    blocks = len(down_blocks(*down)) if regular else 0
    wide = w_out.shape[1] + (down_width(*down) if regular else 0)
    return pl.pallas_call(
        pack_pieces,
        name="pack_pieces",
        out_shape=(
            jax.ShapeDtypeStruct((half, wide), BF16),
            jax.ShapeDtypeStruct((half, w_in.shape[1]), BF16),
        ),
        in_specs=[smem_spec()] + [any_spec()] * 3,
        out_specs=[vmem_spec()] * 2,
        scratch_shapes=[pltpu.SemaphoreType.DMA((2 + blocks,))],
        compiler_params=params(),
        cost_estimate=cost(1e6, 5e6),
    )(place, w_in, w_out, w_down)


def attention_forward(
    seq_count, heads, group, low_ref, high_ref, place_ref, x_hbm, order_ref, start_ref, end_ref,
    cos_ref, sin_ref, *refs,
):
    pieces, refs = refs[:-15], refs[-15:]
    gains_ref, normed_hbm, packed_ref, att_ref, out_ref, lse_ref = refs[:6]
    w_ref, x_ref, normed_ref, qkv_t, k_rows, o_rows, scores_ref, x_sems, normed_sems = refs[6:15]
    width = heads * HD
    rows = group // seq_count
    blocks = group // BLOCK
    fetches = [pltpu.make_async_copy(x_hbm.at[i], x_ref.at[i], x_sems.at[i]) for i in range(seq_count)]
    stores = [
        pltpu.make_async_copy(normed_ref.at[i], normed_hbm.at[i], normed_sems.at[i]) for i in range(seq_count)
    ]
    for fetch in fetches:
        fetch.start()
    if len(pieces) == 2:
        w_ref[...] = pieces[0][...]
        gains_ref[...] = pieces[1][...]
    else:
        tall = w_ref.shape[0] // len(pieces)
        for mask, piece in enumerate(pieces):
            base = pl.multiple_of((place_ref[0] ^ mask) * tall, 128)
            w_ref[pl.ds(base, tall), :] = piece[:tall]
            gains_ref[:, pl.ds(base, tall)] = piece[tall : tall + 2, :tall].astype(F32)
    gain_ref = gains_ref.at[pl.ds(0, 1), :]

    def project(i):
        x = x_ref[i].astype(F32)
        center = x - jnp.mean(x, axis=-1, keepdims=True)
        spread = jnp.mean(center * center, axis=-1, keepdims=True)
        normed = (center * lax.rsqrt(spread + NORM_EPS) * gain_ref[...]).astype(BF16)
        normed_ref[i] = normed
        qkv = nn_dot(normed, w_ref[...]).astype(BF16)
        qkv_t[i] = qkv.T

    for i in range(seq_count):
        fetches[i].wait()
        project(i)
        stores[i].start()

    def pack(i, carry):
        at = pl.ds(pl.multiple_of(i * BLOCK, BLOCK), BLOCK)
        order = order_ref[:, at]
        total = jnp.zeros((3 * width, BLOCK), F32)
        for s in range(seq_count):
            here = lax.broadcasted_iota(jnp.int32, (rows, BLOCK), 0) + s * rows
            hot = jnp.where(here == order, 1.0, 0.0).astype(BF16)
            total = total + nn_dot(qkv_t[s], hot)
        cos = cos_ref[:, at]
        sin = sin_ref[:, at]
        half = HD // 2
        for part in range(2):
            for h in range(heads):
                base = part * width + h * HD
                first = total[base : base + half]
                second = total[base + half : base + HD]
                turned = jnp.concatenate(
                    [first * cos - second * sin, second * cos + first * sin], axis=0
                ).astype(BF16)
                packed_ref[base : base + HD, at] = turned
                if part == 1:
                    k_rows[h, at, :] = turned.T
        packed_ref[2 * width :, at] = total[2 * width :].astype(BF16)
        return carry

    lax.fori_loop(0, blocks, pack, 0)
    scale = HD**-0.5 * LOG2E

    def attend(i, carry):
        at = pl.ds(pl.multiple_of(i * WIDE, WIDE), WIDE)
        start = start_ref[:, at]
        end = end_ref[:, at]
        queries = [packed_ref[h * HD : (h + 1) * HD, at] for h in range(heads)]

        low, high = low_ref[i], high_ref[i]

        def score(j, tops):
            there = pl.ds(pl.multiple_of(j * BLOCK, BLOCK), BLOCK)
            where = lax.broadcasted_iota(jnp.int32, (BLOCK, WIDE), 0) + j * BLOCK
            same = jnp.logical_and(where >= start, where < end)
            following = []
            for h in range(heads):
                scores = jnp.where(same, nn_dot(k_rows[h, there, :], queries[h]) * scale, -1e30)
                scores_ref[j, h] = scores
                following.append(jnp.maximum(tops[h], jnp.max(scores.reshape(-1, 8, WIDE), axis=0)))
            return tuple(following)

        tops = lax.fori_loop(low, high, score, tuple(jnp.full((8, WIDE), -1e30, F32) for _ in range(heads)))
        tops = [jnp.max(top, axis=0, keepdims=True) for top in tops]

        def weigh(j, state):
            there = pl.ds(pl.multiple_of(j * BLOCK, BLOCK), BLOCK)
            following = []
            for h in range(heads):
                total, acc = state[h]
                probs = jnp.exp2(scores_ref[j, h] - tops[h])
                total = total + jnp.sum(probs.reshape(-1, 8, WIDE), axis=0)
                base = 2 * width + h * HD
                acc = acc + nn_dot(packed_ref[base : base + HD, there], probs.astype(BF16))
                following.append((total, acc))
            return tuple(following)

        first = tuple((jnp.zeros((8, WIDE), F32), jnp.zeros((HD, WIDE), F32)) for _ in range(heads))
        last = lax.fori_loop(low, high, weigh, first)
        outs = []
        for h in range(heads):
            total, acc = last[h]
            total = jnp.sum(total, axis=0, keepdims=True)
            out = acc / total
            out_ref[h * HD : (h + 1) * HD, at] = out
            lse_ref[h : h + 1, at] = tops[h] + jnp.log2(total)
            outs.append(out)
        o_rows[at, :] = jnp.concatenate(outs, axis=0).astype(BF16).T
        return carry

    lax.fori_loop(0, group // WIDE, attend, 0)

    def arrive(i, carry):
        here = lax.broadcasted_iota(jnp.int32, (rows, group), 0) + i * rows
        hot = jnp.where(here == order_ref[...], 1.0, 0.0).astype(BF16)
        att_ref[i] = nn_dot(hot, o_rows[...]).astype(BF16)
        return carry

    lax.fori_loop(0, seq_count, arrive, 0)
    for store in stores:
        store.wait()


def run_attention_forward(place, x_all, pieces, layout, heads):
    seq_count, rows, dim = x_all.shape
    group = seq_count * rows
    width = heads * HD
    (low, high), _, order, start, end, cos, sin = layout
    return pl.pallas_call(
        functools.partial(attention_forward, seq_count, heads, group),
        name="attention_forward",
        out_shape=(
            jax.ShapeDtypeStruct((2, dim), F32),
            jax.ShapeDtypeStruct((seq_count, rows, dim), BF16),
            jax.ShapeDtypeStruct((3 * width, group), BF16),
            jax.ShapeDtypeStruct((seq_count, rows, width), BF16),
            jax.ShapeDtypeStruct((width, group), F32),
            jax.ShapeDtypeStruct((heads, group), F32),
        ),
        in_specs=[smem_spec()] * 3 + [any_spec()] + [vmem_spec()] * (5 + len(pieces)),
        out_specs=[vmem_spec(), any_spec()] + [vmem_spec()] * 4,
        scratch_shapes=[
            pltpu.VMEM((dim, 3 * width), BF16),
            pltpu.VMEM((seq_count, rows, dim), BF16),
            pltpu.VMEM((seq_count, rows, dim), BF16),
            pltpu.VMEM((seq_count, 3 * width, rows), BF16),
            pltpu.VMEM((heads, group, HD), BF16),
            pltpu.VMEM((group, width), BF16),
            pltpu.VMEM((group // BLOCK, heads, BLOCK, WIDE), F32),
            pltpu.SemaphoreType.DMA((seq_count,)),
            pltpu.SemaphoreType.DMA((seq_count,)),
        ],
        compiler_params=params(),
        cost_estimate=cost(24e9, 20e6),
    )(low, high, place, x_all, order, start, end, cos, sin, *pieces)


def attention_backward(
    seq_count, heads, group, low_ref, high_ref, dout_ref, packed_ref, out_ref, lse_ref, order_ref,
    start_ref, end_ref, cos_ref, sin_ref, grad_ref, dout_t, dpack_t, drows, qrows, krows, vrows,
    delta_ref, dq_t, grows,
):
    width = heads * HD
    rows = group // seq_count
    blocks = group // BLOCK
    scale = HD**-0.5

    def turn(i, carry):
        dout_t[i] = dout_ref[i].T
        return carry

    lax.fori_loop(0, seq_count, turn, 0)

    def pack(i, carry):
        at = pl.ds(pl.multiple_of(i * BLOCK, BLOCK), BLOCK)
        order = order_ref[:, at]
        total = jnp.zeros((width, BLOCK), F32)
        for s in range(seq_count):
            here = lax.broadcasted_iota(jnp.int32, (rows, BLOCK), 0) + s * rows
            hot = jnp.where(here == order, 1.0, 0.0).astype(BF16)
            total = total + nn_dot(dout_t[s], hot)
        dpack_t[:, at] = total.astype(BF16)
        for h in range(heads):
            mine = total[h * HD : (h + 1) * HD]
            delta_ref[h : h + 1, at] = jnp.sum(
                mine * out_ref[h * HD : (h + 1) * HD, at], axis=0, keepdims=True
            )
            drows[h, at, :] = mine.T.astype(BF16)
            for part, ref in enumerate((qrows, krows, vrows)):
                base = part * width + h * HD
                ref[h, at, :] = packed_ref[base : base + HD, at].T
        dq_t[:, at] = jnp.zeros((width, BLOCK), F32)
        return carry

    lax.fori_loop(0, blocks, pack, 0)

    def keys(j, carry):
        there = pl.ds(pl.multiple_of(j * BLOCK, BLOCK), BLOCK)
        where = lax.broadcasted_iota(jnp.int32, (BLOCK, WIDE), 0) + j * BLOCK

        def queries(i, state):
            at = pl.ds(pl.multiple_of(i * WIDE, WIDE), WIDE)
            same = jnp.logical_and(where >= start_ref[:, at], where < end_ref[:, at])
            following = []
            for h in range(heads):
                dk, dv = state[h]
                base = h * HD
                key_rows = krows[h, there, :]
                query_t = packed_ref[base : base + HD, at]
                scores = nn_dot(key_rows, query_t) * (scale * LOG2E)
                scores = jnp.where(same, scores, -1e30)
                probs = jnp.exp2(scores - lse_ref[h : h + 1, at])
                dprobs = nn_dot(vrows[h, there, :], dpack_t[base : base + HD, at])
                raw = (probs * (dprobs - delta_ref[h : h + 1, at]) * scale).astype(BF16)
                dv = dv + nn_dot(probs.astype(BF16), drows[h, at, :])
                dk = dk + nn_dot(raw, qrows[h, at, :])
                key_t = packed_ref[width + base : width + base + HD, there]
                dq_t[base : base + HD, at] += nn_dot(key_t, raw)
                following.append((dk, dv))
            return tuple(following)

        zero = jnp.zeros((BLOCK, HD), F32)
        last = lax.fori_loop(low_ref[j], high_ref[j], queries, tuple((zero, zero) for _ in range(heads)))
        cos = cos_ref[:, there]
        sin = sin_ref[:, there]
        half = HD // 2
        turned = []
        for h in range(heads):
            dk_t = last[h][0].T
            first, second = dk_t[:half], dk_t[half:]
            turned.append(first * cos + second * sin)
            turned.append(second * cos - first * sin)
        grows[there, width : 2 * width] = jnp.concatenate(turned, axis=0).T.astype(BF16)
        grows[there, 2 * width :] = jnp.concatenate([last[h][1] for h in range(heads)], axis=1).astype(BF16)
        return carry

    lax.fori_loop(0, blocks, keys, 0)

    def finish(i, carry):
        at = pl.ds(pl.multiple_of(i * BLOCK, BLOCK), BLOCK)
        cos = cos_ref[:, at]
        sin = sin_ref[:, at]
        half = HD // 2
        turned = []
        for h in range(heads):
            first = dq_t[h * HD : h * HD + half, at]
            second = dq_t[h * HD + half : (h + 1) * HD, at]
            turned.append(first * cos + second * sin)
            turned.append(second * cos - first * sin)
        grows[at, :width] = jnp.concatenate(turned, axis=0).T.astype(BF16)
        return carry

    lax.fori_loop(0, blocks, finish, 0)

    def arrive(i, carry):
        here = lax.broadcasted_iota(jnp.int32, (rows, group), 0) + i * rows
        hot = jnp.where(here == order_ref[...], 1.0, 0.0).astype(BF16)
        grad_ref[i] = nn_dot(hot, grows[...]).astype(BF16)
        return carry

    lax.fori_loop(0, seq_count, arrive, 0)


def run_attention_backward(dout, packed, out_t, lse, layout, heads):
    seq_count, rows, width = dout.shape
    group = seq_count * rows
    _, (low, high), order, start, end, cos, sin = layout
    return pl.pallas_call(
        functools.partial(attention_backward, seq_count, heads, group),
        name="attention_backward",
        out_shape=jax.ShapeDtypeStruct((seq_count, rows, 3 * width), BF16),
        in_specs=[smem_spec()] * 2 + [vmem_spec()] * 9,
        out_specs=vmem_spec(),
        scratch_shapes=[
            pltpu.VMEM((seq_count, width, rows), BF16),
            pltpu.VMEM((width, group), BF16),
            pltpu.VMEM((heads, group, HD), BF16),
            pltpu.VMEM((heads, group, HD), BF16),
            pltpu.VMEM((heads, group, HD), BF16),
            pltpu.VMEM((heads, group, HD), BF16),
            pltpu.VMEM((heads, group), F32),
            pltpu.VMEM((width, group), F32),
            pltpu.VMEM((group, 3 * width), BF16),
        ],
        compiler_params=params(),
        cost_estimate=cost(30e9, 10e6),
    )(low, high, dout, packed, out_t, lse, order, start, end, cos, sin)


def qkv_weight_grad(seq_count, place_ref, normed_ref, grad_ref, *refs):
    outs, (total, turned) = refs[:-2], refs[-2:]
    total[...] = jnp.zeros_like(total)

    def step(i, carry):
        total[...] += nn_dot(grad_ref[i].T, normed_ref[i])
        return carry

    lax.fori_loop(0, seq_count, step, 0)
    if len(outs) == 1:
        outs[0][...] = total[...].T.astype(BF16)
        return
    turned[...] = total[...].T
    rows = outs[0].shape[1]
    for ref, keys in zip(outs, ((2, 3), (1,), (0,))):
        for at, key in enumerate(keys):
            base = pl.multiple_of(place_ref[key] * rows, 16)
            ref[at] = turned[pl.ds(base, rows), :].astype(BF16)


def run_qkv_weight_grad(place, normed, grad, regular):
    seq_count, rows, dim = normed.shape
    width = grad.shape[-1]
    if regular:
        outs = tuple(jax.ShapeDtypeStruct((n, dim // 4, width), BF16) for n in (2, 1, 1))
    else:
        outs = (jax.ShapeDtypeStruct((dim, width), BF16),)
    return pl.pallas_call(
        functools.partial(qkv_weight_grad, seq_count),
        name="qkv_weight_grad",
        out_shape=outs,
        in_specs=[smem_spec()] + [vmem_spec()] * 2,
        out_specs=[vmem_spec()] * len(outs),
        scratch_shapes=[pltpu.VMEM((width, dim), F32), pltpu.VMEM((dim, width), F32)],
        compiler_params=params(),
        cost_estimate=cost(3e9, 6e6),
    )(place, normed, grad)


def padded(hidden):
    return -(-hidden // 128) * 128


def load_down(place_ref, refs, count, hidden, left, full, sems):
    copies = down_copies(place_ref, refs[0], refs[1 : 1 + count], refs[1 + count :], left, full, sems, hidden)
    for copy in copies:
        copy.start()
    tail = padded(hidden) - hidden
    if tail:
        full[pl.ds(hidden, tail), :] = jnp.zeros((tail, full.shape[1]), BF16)
    for copy in copies:
        copy.wait()


def down_semaphores(downs):
    if len(downs) == 1:
        return pltpu.SemaphoreType.DMA((1,))
    blocks = len(down_blocks(downs[0].shape[0], downs[0].shape[1] // 2, downs[1].shape[0]))
    return pltpu.SemaphoreType.DMA((1 + (len(downs) - 1) * blocks,))


def hidden_grad(hidden, left, place_ref, cot_ref, *refs):
    downs, (out_ref, full, sems) = refs[:-3], refs[-3:]
    load_down(place_ref, downs, (len(downs) - 1) // 2, hidden, left, full, sems)
    cot = cot_ref[...]
    tiles = padded(hidden) // 128
    wide = 128 * max(n for n in (1, 2, 3) if tiles % n == 0)

    def step(i, carry):
        at = pl.multiple_of(i * wide, 128)
        out_ref[:, pl.ds(at, wide)] = nt_dot(cot, full[pl.ds(at, wide), :])
        return carry

    lax.fori_loop(0, padded(hidden) // wide, step, 0)


def run_hidden_grad(place, cot, downs, left, hidden):
    rows, dim = cot.shape
    return pl.pallas_call(
        functools.partial(hidden_grad, hidden, left),
        name="hidden_grad",
        out_shape=jax.ShapeDtypeStruct((rows, padded(hidden)), F32),
        in_specs=[smem_spec(), vmem_spec()] + [any_spec()] * len(downs),
        out_specs=vmem_spec(),
        scratch_shapes=[pltpu.VMEM((padded(hidden), dim), BF16), down_semaphores(downs)],
        compiler_params=params(),
        cost_estimate=cost(4e9, 9e6),
    )(place, cot, *downs)


def layer_result(hidden, left, place_ref, mid_ref, keep_ref, *refs):
    downs, (out_ref, full, sems) = refs[:-3], refs[-3:]
    load_down(place_ref, downs, (len(downs) - 1) // 2, hidden, left, full, sems)
    wide = padded(hidden)

    def step(i, carry):
        at = pl.ds(pl.multiple_of(i * 256, 256), 256)
        out_ref[:, at] = (mid_ref[:, at] + nn_dot(keep_ref[:, :wide], full[:, at])).astype(BF16)
        return carry

    lax.fori_loop(0, out_ref.shape[1] // 256, step, 0)


def run_layer_result(place, middle, keep, downs, left, hidden):
    rows, dim = middle.shape
    return pl.pallas_call(
        functools.partial(layer_result, hidden, left),
        name="layer_result",
        out_shape=jax.ShapeDtypeStruct((rows, dim), BF16),
        in_specs=[smem_spec()] + [vmem_spec()] * 2 + [any_spec()] * len(downs),
        out_specs=vmem_spec(),
        scratch_shapes=[pltpu.VMEM((padded(hidden), dim), BF16), down_semaphores(downs)],
        compiler_params=params(),
        cost_estimate=cost(4e9, 9e6),
    )(place, middle, keep, *downs)


def feed_forward(
    count, hidden, heads_width, place_ref, x_ref, att_ref, cot_ref, gain_ref, gh_hbm, *refs
):
    out_own, in_own, refs = refs[0], refs[1], refs[2:]
    first, others, refs = refs[:count], refs[count : 2 * count], refs[2 * count :]
    second, second_others, refs = refs[:count], refs[count : 2 * count], refs[2 * count :]
    mid_ref, gmid_ref, send_hbm, keep_hbm, ga_ref = refs[:5]
    wo, wi, both, early, late, send_ref, keep_ref, gh_ref, sem_o, sem_i, sems = refs[5:]
    fetch = pltpu.make_async_copy(gh_hbm, gh_ref, sems.at[0])
    send_out = pltpu.make_async_copy(send_ref, send_hbm, sems.at[1])
    keep_out = pltpu.make_async_copy(keep_ref, keep_hbm, sems.at[2])
    dim = x_ref.shape[1]
    wide_hidden = padded(hidden)
    nt_ref = send_ref.at[:, pl.ds(2 * hidden, dim)]
    gboth_ref = send_ref
    hid_ref = keep_ref
    gbr_ref = keep_ref.at[:, pl.ds(wide_hidden, dim)]
    att_all_ref = keep_ref.at[:, pl.ds(wide_hidden + dim, dim)]
    keep_ref[:, pl.ds(wide_hidden + 2 * dim, dim)] = cot_ref[...]
    copies_o = row_copies(place_ref, out_own, first, others, 0, wo, sem_o)
    copies_i = row_copies(place_ref, in_own, second, second_others, 0, wi, sem_i)
    for copy in copies_o:
        copy.start()
    for copy in copies_i:
        copy.start()
    fetch.start()
    att = jnp.concatenate([att_ref[s] for s in range(att_ref.shape[0])], axis=1)
    att_all_ref[...] = att
    for copy in copies_o:
        copy.wait()

    def branch(i, carry):
        at = pl.ds(pl.multiple_of(i * 256, 256), 256)
        mid_ref[:, at] = x_ref[:, at].astype(F32) + nn_dot(att_all_ref[...], wo[:, at])
        return carry

    lax.fori_loop(0, dim // 256, branch, 0)
    middle = mid_ref[...]
    center = middle - jnp.mean(middle, axis=-1, keepdims=True)
    spread = jnp.mean(center * center, axis=-1, keepdims=True)
    scale = lax.rsqrt(spread + NORM_EPS)
    nt_ref[...] = (center * scale * gain_ref[...]).astype(BF16)
    for copy in copies_i:
        copy.wait()
    fetch.wait()
    wide = 2 * hidden // 128

    def expand(i, carry):
        at = pl.ds(pl.multiple_of(i * 256, 256), 256)
        both[:, at] = nn_dot(nt_ref[...], wi[:, at])
        return carry

    lax.fori_loop(0, wide // 2, expand, 0)
    if wide % 2:
        both[:, pl.ds(128 * (wide - 1), 128)] = nn_dot(nt_ref[...], wi[:, pl.ds(128 * (wide - 1), 128)])
    both[:, pl.ds(128 * wide, 128)] = jnp.zeros((both.shape[0], 128), F32)
    tiles = padded(hidden) // 128
    whole = hidden // 128
    lanes = lax.broadcasted_iota(jnp.int32, (both.shape[0], 128), 1)
    shift = hidden % 128

    def tile(i):
        return pl.ds(pl.multiple_of(i * 128, 128), 128)

    def gates(i):
        a = both[:, tile(i)]
        if shift:
            left = pltpu.roll(both[:, tile(whole + i)], 128 - shift, 1)
            right = pltpu.roll(both[:, tile(whole + i + 1)], 128 - shift, 1)
            b = jnp.where(lanes < 128 - shift, left, right)
        else:
            b = both[:, tile(whole + i)]
        gh = gh_ref[:, tile(i)]
        phi = 0.5 * (1.0 + lax.erf(a * (0.5**0.5)))
        gelu = a * phi
        slope = phi + a * ((0.5 / math.pi) ** 0.5 * jnp.exp(-0.5 * a * a))
        hid_ref[:, tile(i)] = (gelu * b).astype(BF16)
        return gh * b * slope, gh * gelu

    if shift:
        first_a, first_b = gates(0)
        gboth_ref[:, tile(0)] = first_a.astype(BF16)
        early[...] = pltpu.roll(first_b, shift, 1)
        late[...] = early[...]

        def inner(i, carry):
            ga, gb = gates(i)
            turned = pltpu.roll(gb, shift, 1)
            gboth_ref[:, tile(i)] = ga.astype(BF16)
            gboth_ref[:, tile(whole + i)] = jnp.where(lanes < shift, late[...], turned).astype(BF16)
            late[...] = turned
            return carry

        lax.fori_loop(1, tiles - 1, inner, 0)
        ga, gb = gates(tiles - 1)
        turned = pltpu.roll(gb, shift, 1)
        gboth_ref[:, tile(whole)] = jnp.where(lanes < shift, ga, early[...]).astype(BF16)
        gboth_ref[:, tile(2 * whole)] = jnp.where(lanes < shift, late[...], turned).astype(BF16)
    else:

        def inner(i, carry):
            ga, gb = gates(i)
            gboth_ref[:, tile(i)] = ga.astype(BF16)
            gboth_ref[:, tile(whole + i)] = gb.astype(BF16)
            return carry

        lax.fori_loop(0, tiles, inner, 0)

    send_out.start()

    def back(i, carry):
        at = pl.multiple_of(i * 256, 256)
        both[:, pl.ds(at, 256)] = nt_dot(gboth_ref[:, : 2 * hidden], wi[pl.ds(at, 256), :])
        return carry

    lax.fori_loop(0, dim // 256, back, 0)
    middle = mid_ref[...]
    center = middle - jnp.mean(middle, axis=-1, keepdims=True)
    spread = jnp.mean(center * center, axis=-1, keepdims=True)
    scale = lax.rsqrt(spread + NORM_EPS)
    normal = center * scale
    e = both[:, pl.ds(0, dim)] * gain_ref[...]
    pull = e - jnp.mean(e, axis=-1, keepdims=True) - normal * jnp.mean(e * normal, axis=-1, keepdims=True)
    gmid = cot_ref[...].astype(F32) + scale * pull
    gmid_ref[...] = gmid
    gbr_ref[...] = gmid.astype(BF16)
    keep_out.start()

    def spread_out(i, carry):
        at = pl.multiple_of(i * 256, 256)
        both[:, pl.ds(at, 256)] = nt_dot(gbr_ref[...], wo[pl.ds(at, 256), :])
        return carry

    lax.fori_loop(0, dim // 256, spread_out, 0)
    for s in range(att_ref.shape[0]):
        ga_ref[s] = both[:, s * heads_width : (s + 1) * heads_width].astype(BF16)
    send_out.wait()
    keep_out.wait()


def run_feed_forward(place, x, att, cot, gain, grad_hidden, w_out, w_in, first, second, hidden):
    rows, dim = x.shape
    seq_count, _, heads_width = att.shape
    count = len(first) // 2
    return pl.pallas_call(
        functools.partial(feed_forward, count, hidden, heads_width),
        name="feed_forward",
        out_shape=(
            jax.ShapeDtypeStruct((rows, dim), F32),
            jax.ShapeDtypeStruct((rows, dim), F32),
            jax.ShapeDtypeStruct((rows, 2 * hidden + dim), BF16),
            jax.ShapeDtypeStruct((rows, padded(hidden) + 3 * dim), BF16),
            jax.ShapeDtypeStruct((seq_count, rows, heads_width), BF16),
        ),
        in_specs=[smem_spec()] + [vmem_spec()] * 4 + [any_spec()] * (3 + 4 * count),
        out_specs=[vmem_spec()] * 2 + [any_spec()] * 2 + [vmem_spec()],
        scratch_shapes=[
            pltpu.VMEM((dim, dim), BF16),
            pltpu.VMEM((dim, 2 * hidden), BF16),
            pltpu.VMEM((rows, 2 * hidden + 128), F32),
            pltpu.VMEM((rows, 128), F32),
            pltpu.VMEM((rows, 128), F32),
            pltpu.VMEM((rows, 2 * hidden + dim), BF16),
            pltpu.VMEM((rows, padded(hidden) + 3 * dim), BF16),
            pltpu.VMEM((rows, padded(hidden)), F32),
            pltpu.SemaphoreType.DMA((2 * count + 1,)),
            pltpu.SemaphoreType.DMA((2 * count + 1,)),
            pltpu.SemaphoreType.DMA((3,)),
        ],
        compiler_params=params(),
        cost_estimate=cost(16e9, 24e6),
    )(place, x, att, cot, gain, grad_hidden, w_out, w_in, *first, *second)


def block_order(core):
    return (0, 2 - core, 1 + core, 3)


def in_grad(hidden, wide, place_ref, send_ref, other_ref, a_ref, b_ref, c_ref, turned, picked):
    tokens = send_ref.shape[0]
    rows = turned.shape[0] // 4
    half, short = rows // 2, rows // 8

    @pl.when(pl.program_id(0) == 0)
    def _():
        turned[:, :tokens] = send_ref[:, 2 * hidden :].T
        turned[:, tokens:] = other_ref[:, 2 * hidden :].T
        core, z = place_ref[7], place_ref[8]
        for at, key in enumerate((2, 3, 1, 0)):
            for j, k in enumerate(block_order(core)):
                base = pl.multiple_of(place_ref[key] * rows + core * half + (z ^ k) * short, 16)
                to = at * half + j * short
                picked[to : to + short, :] = turned[pl.ds(base, short), :]

    at = pl.ds(pl.multiple_of(pl.program_id(0) * wide, 128), wide)
    right = jnp.concatenate([send_ref[:, at], other_ref[:, at]], axis=0)
    result = nn_dot(picked[...], right).astype(BF16)
    a_ref[0] = result[:half]
    a_ref[1] = result[half : 2 * half]
    b_ref[0] = result[2 * half : 3 * half]
    c_ref[0] = result[3 * half :]


def run_in_grad(place, send, other, hidden):
    tokens = send.shape[0]
    features = send.shape[1] - 2 * hidden
    columns = 2 * hidden
    half = features // 8
    wide = 896
    whole = pl.BlockSpec(send.shape, lambda i: (0, 0))
    return pl.pallas_call(
        functools.partial(in_grad, hidden, wide),
        name="in_grad",
        out_shape=tuple(jax.ShapeDtypeStruct((n, half, columns), BF16) for n in (2, 1, 1)),
        grid=(pl.cdiv(columns, wide),),
        in_specs=[smem_spec(), whole, whole],
        out_specs=[pl.BlockSpec((n, half, wide), lambda i: (0, 0, i)) for n in (2, 1, 1)],
        scratch_shapes=[
            pltpu.VMEM((features, 2 * tokens), BF16),
            pltpu.VMEM((features // 2, 2 * tokens), BF16),
        ],
        compiler_params=params(),
        cost_estimate=cost(2.0 * 2 * tokens * features * columns, 4 * tokens * columns + features * columns),
    )(place, send, other)


def rest_grad(hidden, place_ref, keep_ref, other_ref, a_ref, b_ref, c_ref, turned, picked):
    tokens = keep_ref.shape[0]
    wide = padded(hidden)
    dim = (keep_ref.shape[1] - wide) // 3
    half = dim // 2
    down_rows = hidden // 4
    short = dim // 32
    core, z = place_ref[7], place_ref[8]
    at = pl.program_id(0)

    @pl.when(at == 0)
    def _():
        turned[:wide, :tokens] = keep_ref[:, :wide].T
        turned[:wide, tokens:] = other_ref[:, :wide].T
        turned[wide:, :tokens] = keep_ref[:, wide + dim : wide + 2 * dim].T
        turned[wide:, tokens:] = other_ref[:, wide + dim : wide + 2 * dim].T
        for j, k in enumerate(block_order(core)):
            left = pl.ds(pl.multiple_of(wide + 2 * dim + core * half + (z ^ k) * 128, 128), 128)
            picked[:tokens, j * 128 : (j + 1) * 128] = keep_ref[:, left]
            picked[tokens:, j * 128 : (j + 1) * 128] = other_ref[:, left]
        picked[:tokens, half:] = keep_ref[:, wide : wide + dim]
        picked[tokens:, half:] = other_ref[:, wide : wide + dim]

    owner = place_ref[jnp.where(at < 2, at + 2, 3 - at)]
    base = pl.multiple_of(owner * down_rows, 16)
    down = nn_dot(turned[pl.ds(base, down_rows), :], picked[:, :half]).astype(BF16)
    left = []
    for k in block_order(core):
        base = pl.multiple_of(wide + owner * 8 * short + core * 4 * short + (z ^ k) * short, 16)
        left.append(turned[pl.ds(base, short), :])
    out = nn_dot(jnp.concatenate(left, axis=0), picked[:, half:]).astype(BF16)
    first = dim // 128 * short

    def store(ref):
        for j in range(4):
            for t in range(dim // 128):
                ref[0, j, t * short : (t + 1) * short, :] = out[
                    j * short : (j + 1) * short, t * 128 : (t + 1) * 128
                ]
            ref[0, j, first:, :] = down[:, j * 128 : (j + 1) * 128]

    pl.when(at < 2)(lambda: store(a_ref))
    pl.when(at == 2)(lambda: store(b_ref))
    pl.when(at == 3)(lambda: store(c_ref))


def run_rest_grad(place, keep, other, hidden):
    tokens = keep.shape[0]
    wide = padded(hidden)
    dim = (keep.shape[1] - wide) // 3
    tall = dim // 128 * (dim // 32) + hidden // 4
    whole = pl.BlockSpec(keep.shape, lambda i: (0, 0))
    return pl.pallas_call(
        functools.partial(rest_grad, hidden),
        name="rest_grad",
        out_shape=tuple(jax.ShapeDtypeStruct((n, 4, tall, 128), BF16) for n in (2, 1, 1)),
        grid=(4,),
        in_specs=[smem_spec(), whole, whole],
        out_specs=[
            pl.BlockSpec((1, 4, tall, 128), lambda i: (jnp.minimum(i, 1), 0, 0, 0)),
            pl.BlockSpec((1, 4, tall, 128), lambda i: (0, 0, 0, 0)),
            pl.BlockSpec((1, 4, tall, 128), lambda i: (0, 0, 0, 0)),
        ],
        scratch_shapes=[
            pltpu.VMEM((wide + dim, 2 * tokens), BF16),
            pltpu.VMEM((2 * tokens, dim + dim // 2), BF16),
        ],
        compiler_params=params(),
        cost_estimate=cost(4e9, 10e6),
    )(place, keep, other)


def unpack_in(place_ref, *refs):
    pieces, w_ref, out_ref, sum_ref = refs[:4], refs[4], refs[5], refs[6]
    at = pl.program_id(0)
    for q, ref in enumerate(pieces):

        @pl.when(at // 2 == q)
        def _(ref=ref):
            value = ref[0].astype(F32)
            out_ref[...] = value
            sum_ref[...] = jnp.sum(value * w_ref[...].astype(F32), axis=1, keepdims=True)


def row_block(i, place_ref):
    side = jnp.where(i < 4, place_ref[7], 1 - place_ref[7])
    order = jnp.where(i % 4 == 1, 2 - side, jnp.where(i % 4 == 2, 1 + side, i % 4))
    return (side * 4 + (place_ref[8] ^ order), 0)


def run_unpack_in(place, pieces, weight):
    rows, columns = weight.shape
    short = rows // 8
    specs = [
        pl.BlockSpec((1, short, columns), lambda i, p, q=q: (jnp.clip(i - 2 * q, 0, 1), 0, 0))
        for q in range(4)
    ]
    block = pl.BlockSpec((short, columns), row_block)
    return pl.pallas_call(
        unpack_in,
        name="unpack_in",
        out_shape=(jax.ShapeDtypeStruct((rows, columns), F32), jax.ShapeDtypeStruct((rows, 1), F32)),
        grid_spec=pltpu.PrefetchScalarGridSpec(
            num_scalar_prefetch=1,
            grid=(8,),
            in_specs=specs + [block],
            out_specs=[block, pl.BlockSpec((short, 1), row_block)],
        ),
        compiler_params=params(),
        cost_estimate=cost(1e7, 11e6),
    )(place, *pieces, weight)


def sources(place_ref, pieces):
    core, z = place_ref[7], place_ref[8]
    for q, ref in enumerate(pieces):
        for at in range(2):
            side = core if q < 2 else 1 - core
            yield ref.at[at], side, z ^ block_order(side)[2 * (q % 2) + at]


def unpack_rest(place_ref, *refs):
    pieces, out_ref, down_ref = refs[:4], refs[4], refs[5]
    dim = out_ref.shape[1]
    short = dim // 32
    first = dim // 128 * short
    for ref, side, z in sources(place_ref, pieces):
        base = pl.multiple_of(side * 4 * short + z * short, 16)
        for t in range(dim // 128):
            out_ref[pl.ds(base, short), t * 128 : (t + 1) * 128] = ref[
                t * short : (t + 1) * short, :
            ].astype(F32)
        left = pl.multiple_of(side * (dim // 2) + z * 128, 128)
        down_ref[:, pl.ds(left, 128)] = ref[first:, :].astype(F32)


def run_unpack_rest(place, pieces, out_shape, down_shape):
    return pl.pallas_call(
        unpack_rest,
        name="unpack_rest",
        out_shape=(jax.ShapeDtypeStruct(out_shape, F32), jax.ShapeDtypeStruct(down_shape, F32)),
        in_specs=[smem_spec()] + [vmem_spec()] * 4,
        out_specs=[vmem_spec()] * 2,
        compiler_params=params(),
        cost_estimate=cost(1e7, 6e6),
    )(place, *pieces)


def unpack_qkv(place_ref, *refs):
    pieces, w_ref, out_ref, sum_ref = refs[:4], refs[4], refs[5], refs[6]
    width = pieces[0].shape[2] // 3
    dim = out_ref.shape[1] // 3
    total = jnp.zeros_like(sum_ref)
    for ref, side, z in sources(place_ref, pieces):
        for part in range(3):
            left = pl.multiple_of(part * dim + (z * 2 + side) * width, 128)
            value = ref[:, part * width : (part + 1) * width].astype(F32)
            out_ref[:, pl.ds(left, width)] = value
            weight = w_ref[:, pl.ds(left, width)].astype(F32)
            total = total + jnp.sum(value * weight, axis=1, keepdims=True)
    sum_ref[...] = total


def run_unpack_qkv(place, pieces, weight):
    return pl.pallas_call(
        unpack_qkv,
        name="unpack_qkv",
        out_shape=(
            jax.ShapeDtypeStruct(weight.shape, F32),
            jax.ShapeDtypeStruct((weight.shape[0], 1), F32),
        ),
        in_specs=[smem_spec()] + [vmem_spec()] * 5,
        out_specs=[vmem_spec()] * 2,
        compiler_params=params(),
        cost_estimate=cost(1e7, 7e6),
    )(place, *pieces, weight)


def input_grad(count, place_ref, x_ref, gmid_ref, gain_ref, g_ref, *refs):
    weights, (out_ref, full, grad, total, sems) = refs[:-5], refs[-5:]
    seq_count, _, width = g_ref.shape
    width //= 3
    dim = x_ref.shape[1]
    copies = row_copies(place_ref, weights[0], weights[1 : 1 + count], weights[1 + count :], 0, full, sems)
    for copy in copies:
        copy.start()
    grad[...] = jnp.concatenate(
        [g_ref[s][:, part * width : (part + 1) * width] for part in range(3) for s in range(seq_count)],
        axis=1,
    )
    for copy in copies:
        copy.wait()

    def step(i, carry):
        at = pl.multiple_of(i * 256, 256)
        total[:, pl.ds(at, 256)] = nt_dot(grad[...], full[pl.ds(at, 256), :])
        return carry

    lax.fori_loop(0, dim // 256, step, 0)
    x = x_ref[...].astype(F32)
    center = x - jnp.mean(x, axis=-1, keepdims=True)
    spread = jnp.mean(center * center, axis=-1, keepdims=True)
    scale = lax.rsqrt(spread + NORM_EPS)
    normal = center * scale
    e = total[...] * gain_ref[...]
    pull = e - jnp.mean(e, axis=-1, keepdims=True) - normal * jnp.mean(e * normal, axis=-1, keepdims=True)
    out_ref[...] = (gmid_ref[...] + scale * pull).astype(BF16)


def run_input_grad(place, x, gmid, gain, grads, weights, count):
    rows, dim = x.shape
    columns = weights[0].shape[1]
    return pl.pallas_call(
        functools.partial(input_grad, count),
        name="input_grad",
        out_shape=jax.ShapeDtypeStruct((rows, dim), BF16),
        in_specs=[smem_spec()] + [vmem_spec()] * 4 + [any_spec()] * len(weights),
        out_specs=vmem_spec(),
        scratch_shapes=[
            pltpu.VMEM((dim, columns), BF16),
            pltpu.VMEM((rows, columns), BF16),
            pltpu.VMEM((rows, dim), F32),
            pltpu.SemaphoreType.DMA((2 * count + 1,)),
        ],
        compiler_params=params(),
        cost_estimate=cost(4e9, 10e6),
    )(place, x, gmid, gain, grads, *weights)


def sequence_layout(lengths, order, group):
    ends = jnp.cumsum(lengths)
    starts = ends - lengths
    index = jnp.arange(group, dtype=jnp.int32)
    passed = index[:, None] >= ends[None, :]
    start = jnp.sum(jnp.where(passed, lengths[None, :], 0), axis=1).astype(jnp.int32)
    inside = jnp.logical_and(index[:, None] >= starts[None, :], jnp.logical_not(passed))
    end = jnp.sum(jnp.where(inside, ends[None, :], 0), axis=1).astype(jnp.int32)
    places = index - start
    half = HD // 2
    speeds = jnp.power(F32(ROPE_BASE), -2.0 * jnp.arange(half, dtype=F32) / HD)
    angles = speeds[:, None] * places.astype(F32)[None, :]
    keys = (start[::WIDE] // BLOCK, (end[WIDE - 1 :: WIDE] + BLOCK - 1) // BLOCK)
    queries = (start[::BLOCK] // WIDE, (end[BLOCK - 1 :: BLOCK] + WIDE - 1) // WIDE)
    return (keys, queries, order[None, :], start[None, :], end[None, :], jnp.cos(angles), jnp.sin(angles))


def local(tokens, seq_lengths, seq_order, norm_one, w_qkv, w_out, norm_two, w_in, w_down, cotangent):
    seq_count = lax.axis_size("seq")
    fsdp_count = lax.axis_size("fsdp")
    levels = fsdp_count.bit_length() - 1
    count = fsdp_count - 1
    seq_at = lax.axis_index("seq")
    fsdp_at = lax.axis_index("fsdp")
    core = seq_at % 2
    x = tokens[0]
    cot = cotangent[0]
    rows, dim = x.shape
    group = rows * seq_count
    heads = dim // HD // seq_count
    width = heads * HD
    hidden = w_in.shape[1] // 2
    counts = (seq_count, fsdp_count)
    swap = functools.partial(core_swap, seq_count=seq_count)

    keys = [jnp.array([plane_mask(c, key, levels) for key in range(1, fsdp_count)], jnp.int32) for c in (0, 1)]
    mine = fsdp_at ^ jnp.where(core == 0, keys[0], keys[1])
    other = fsdp_at ^ jnp.where(core == 0, keys[1], keys[0])
    place = jnp.stack([fsdp_at, *mine, *other, core, seq_at // 2]).astype(jnp.int32)
    regular = fsdp_count == 4 and seq_count == 8 and w_down.shape[0] % 16 == 0 and dim == 1024

    x_all = lax.all_gather(x, "seq", axis=0, tiled=False)
    own_heads = lax.dynamic_slice_in_dim(w_qkv.reshape(w_qkv.shape[0], 3, dim), seq_at * width, width, 2)
    own_heads = own_heads.reshape(w_qkv.shape[0], 3 * width)
    gains = jnp.stack([norm_one, norm_two])
    if regular:
        extra = jnp.pad(gains, ((0, 14), (0, 3 * width - gains.shape[1])))
        own_heads = jnp.concatenate([own_heads, extra], axis=0)
        head_pieces = [own_heads] + [
            lax.ppermute(own_heads, "fsdp", [(f, f ^ mask) for f in range(4)]) for mask in (1, 2, 3)
        ]
    else:
        head_pieces = [
            lax.all_gather(own_heads, "fsdp", axis=0, tiled=True),
            lax.all_gather(gains, "fsdp", axis=1, tiled=True).astype(F32),
        ]
    first_piece, second_piece = run_pack_pieces(place, w_in, w_out, w_down, regular)
    first_a, second_a = plane_swap(first_piece, 0, *counts), plane_swap(second_piece, 0, *counts)
    first = plane_gather_rest(first_piece, first_a, *counts)
    second = plane_gather_rest(second_piece, second_a, *counts, first_a)
    left = dim

    layout = sequence_layout(seq_lengths[0], seq_order[0], group)
    gains, normed, packed, att, out_t, lse = run_attention_forward(place, x_all, head_pieces, layout, heads)
    gain_one, gain_two = gains[:1], gains[1:]
    qkv_piece = lax.dynamic_slice_in_dim(w_qkv, core * (w_qkv.shape[0] // 2), w_qkv.shape[0] // 2, 0)
    att_done = lax.all_to_all(att, "seq", split_axis=0, concat_axis=0, tiled=True)
    first = first + [swap(first[0])] + [swap(after(piece, att)) for piece in first[1:]]
    if regular:
        downs = [w_down] + first
    else:
        downs = [lax.all_gather(w_down, "fsdp", axis=0, tiled=True)]
    grad_hidden = run_hidden_grad(place, cot, downs, left, hidden)
    second = second + [swap(second[0])] + [swap(after(piece, att_done, grad_hidden)) for piece in second[1:]]
    att = att_done
    middle, gmid, send, keep, gatt = run_feed_forward(
        place, x, att, cot, gain_two, grad_hidden, w_out, w_in, first, second, hidden
    )
    dout = lax.all_to_all(gatt, "seq", split_axis=0, concat_axis=0, tiled=True)
    reduce = functools.partial(plane_reduce, seq_count=seq_count, fsdp_count=fsdp_count)
    send_other, keep_other = swap(send), swap(keep)
    wide = padded(hidden)
    if regular:
        short = w_in.shape[0] // 8
        in_a, in_b, in_c = run_in_grad(place, send, send_other, hidden)
        dout = after(dout, in_b)
        in_a = plane_swap(in_a, 1, *counts)
        in_sum = added(in_b[0], in_a[1])
    else:
        in_b = in_sum = gatt
    qkv_piece = after(qkv_piece, in_b)
    qkv_mine = {1 << phase: plane_swap(qkv_piece, phase, *counts) for phase in range(levels)}
    keep_other = after(keep_other, *qkv_mine.values())

    grads = run_attention_backward(dout, packed, out_t, lse, layout, heads)
    grad_rows = lax.all_to_all(grads, "seq", split_axis=0, concat_axis=0, tiled=True)
    gw_heads = run_qkv_weight_grad(place, normed, after(grads, in_sum), regular)
    each = w_qkv.shape[0]
    qkv_rest = in_sum
    if regular:
        in_second = plane_swap(in_sum, 0, *counts)
        in_parts = [p.reshape(4, short, 2 * hidden) for p in (in_c[0], in_a[0], in_second)]
        rest_a, rest_b, rest_c = run_rest_grad(place, keep, after(keep_other, in_sum), hidden)
        in_z1 = line_swap(after(added(*(p[2:] for p in in_parts)), rest_b), 0, seq_count)
        layer_out = run_layer_result(place, middle, after(keep, rest_b), downs, left, hidden)
        rest_parts = reduce(plane_swap(after(rest_a, in_second), 1, *counts), rest_b, rest_c)
        qkv_rest = rest_parts[2]
    else:
        layer_out = run_layer_result(place, middle, keep, downs, left, hidden)
    for phase in range(1, levels):
        for key in range(1, 1 << phase):
            qkv_mine[key + (1 << phase)] = plane_swap(after(qkv_mine[key], qkv_rest), phase, *counts)
    qkv_mine = [qkv_mine[key] for key in range(1, fsdp_count)]
    qkvs = [w_qkv] + qkv_mine + [swap(p) for p in qkv_mine]
    grad_tokens = run_input_grad(place, x, gmid, gain_one, grad_rows, qkvs, count)
    if regular:
        qkv_a, qkv_b, qkv_c = gw_heads
        qkv_a = plane_swap(after(qkv_a, rest_parts[1]), 1, *counts)
        qkv_block = added(*reduce(qkv_a, qkv_b, qkv_c))
        in_sum = after(added(*(p[1] for p in in_parts), in_z1[1]), grad_rows, layer_out)
        in_z2 = line_swap(in_sum, 1, seq_count)
        in_block = added(*(p[0] for p in in_parts), in_z1[0], in_z2)
        rest_z1 = line_swap(after(added(*(p[2:] for p in rest_parts)), in_z1), 0, seq_count)
        rest_z2 = line_swap(after(added(*(p[1] for p in rest_parts), rest_z1[1]), in_z2), 1, seq_count)
        rest_block = added(*(p[0] for p in rest_parts), rest_z1[0], rest_z2)
        in_pieces = line_gather(in_block, seq_count)
        gw_in, sum_in = run_unpack_in(place, in_pieces, w_in)
        rest_pieces = line_gather(rest_block, seq_count, sum_in)
        qkv_pieces = line_gather(after(qkv_block, rest_z2, grad_tokens), seq_count, sum_in)
        gw_qkv, sum_qkv = run_unpack_qkv(place, qkv_pieces, w_qkv)
        gw_out, gw_down = run_unpack_rest(place, rest_pieces, w_out.shape, w_down.shape)
        sum_qkv = sum_qkv[:, 0]
        sum_in = sum_in[:, 0]
    else:

        def total(left_rows, right_rows):
            full = lax.dot_general(
                left_rows, right_rows, (((0,), (0,)), ((), ())), preferred_element_type=F32
            )
            return lax.psum(lax.psum_scatter(full, "fsdp", scatter_dimension=0, tiled=True), "seq")

        gw_in = total(send[:, 2 * hidden :], send[:, : 2 * hidden])
        gw_down = total(keep[:, :hidden], cot)
        gw_out = total(keep[:, wide + dim : wide + 2 * dim], keep[:, wide : wide + dim])
        sum_in = jnp.sum(gw_in * w_in.astype(F32), axis=1)
        gw_heads = lax.all_to_all(gw_heads[0].reshape(fsdp_count, each, -1), "fsdp", 0, 0, tiled=True)
        gw_heads = jnp.sum(gw_heads.astype(F32), axis=0).astype(BF16)
        gw_qkv = lax.all_gather(gw_heads, "seq", axis=0, tiled=False).reshape(seq_count, each, 3, width)
        gw_qkv = gw_qkv.transpose(1, 2, 0, 3).reshape(each, 3 * dim).astype(F32)
        sum_qkv = jnp.sum(gw_qkv * w_qkv.astype(F32), axis=1)

    grad_one = sum_qkv / norm_one.astype(F32)
    grad_two = sum_in / norm_two.astype(F32)
    return (layer_out[None], grad_tokens[None], grad_one, gw_qkv, gw_out, grad_two, gw_in, gw_down)


def solution(mesh):
    tokens = P("fsdp", "seq", None)
    rows = P("fsdp", None)
    return jax.shard_map(
        local,
        mesh=mesh,
        in_specs=(tokens, rows, rows, P("fsdp"), rows, rows, P("fsdp"), rows, rows, tokens),
        out_specs=(tokens, tokens, P("fsdp"), rows, rows, P("fsdp"), rows, rows),
        check_vma=False,
    )
```

```python
import functools
import math

import jax
import jax.numpy as jnp
from jax import lax
from jax.experimental import pallas as pl
from jax.experimental.pallas import tpu as pltpu
from jax.sharding import PartitionSpec as P

HD = 64
NORM_EPS = 1e-05
ROPE_BASE = 160000.0
BLOCK = 256
WIDE = 512
LOG2E = math.log2(math.e)
AXES = ("seq", "fsdp")
F32 = jnp.float32
BF16 = jnp.bfloat16
VMEM_LIMIT = 60 * 1024 * 1024


def core_swap(value, seq_count):
    return lax.ppermute(value, "seq", [(i, i ^ 1) for i in range(seq_count)])


def plane_bit(core, phase, levels):
    return (phase + core * (levels // 2)) % levels


def plane_mask(core, key, levels):
    mask = 0
    for phase in range(levels):
        if key >> phase & 1:
            mask |= 1 << plane_bit(core, phase, levels)
    return mask


def plane_swap(value, phase, seq_count, fsdp_count):
    levels = fsdp_count.bit_length() - 1
    pairs = []
    for s in range(seq_count):
        step = 1 << plane_bit(s & 1, phase, levels)
        for f in range(fsdp_count):
            pairs.append((s * fsdp_count + f, s * fsdp_count + (f ^ step)))
    return lax.ppermute(value, AXES, pairs)


def after(value, *others):
    return lax.optimization_barrier((value, *others))[0]


def plane_gather_rest(piece, first, seq_count, fsdp_count, *others):
    pieces = [after(piece, first, *others), after(first, *others)]
    for phase in range(1, fsdp_count.bit_length() - 1):
        pieces = pieces + [plane_swap(p, phase, seq_count, fsdp_count) for p in pieces]
    return [first] + pieces[2:]


def added(*values):
    return sum(v.astype(F32) for v in values).astype(BF16)


def plane_reduce(first, b, c, seq_count, fsdp_count):
    second = plane_swap(added(b[0], first[1]), 0, seq_count, fsdp_count)
    return c[0], first[0], second


def line_swap(value, level, seq_count):
    return lax.ppermute(value, "seq", [(i, i ^ (2 << (level ^ (i & 1)))) for i in range(seq_count)])


def line_reduce(parts, seq_count):
    got = line_swap(added(*(p[2:] for p in parts)), 0, seq_count)
    last = line_swap(added(*(p[1] for p in parts), got[1]), 1, seq_count)
    return added(*(p[0] for p in parts), got[0], last)


def line_gather(block, seq_count, *others):
    pair = jnp.stack([block, line_swap(block, 1, seq_count)])
    rest = line_swap(pair, 0, seq_count)
    return [pair, rest, core_swap(pair, seq_count), core_swap(after(rest, *others), seq_count)]


def any_spec():
    return pl.BlockSpec(memory_space=pl.ANY)


def vmem_spec():
    return pl.BlockSpec(memory_space=pltpu.VMEM)


def smem_spec():
    return pl.BlockSpec(memory_space=pltpu.SMEM)


def params():
    return pltpu.CompilerParams(vmem_limit_bytes=VMEM_LIMIT)


def cost(flops, moved):
    return pl.CostEstimate(flops=int(flops), bytes_accessed=int(moved), transcendentals=0)


def nt_dot(a, b):
    return lax.dot_general(a, b, (((1,), (1,)), ((), ())), preferred_element_type=F32)


def nn_dot(a, b):
    return jnp.dot(a, b, preferred_element_type=F32)


def own_copy(place_ref, own, full, sems, rows):
    base = pl.multiple_of(place_ref[0] * rows, 16)
    return pltpu.make_async_copy(own, full.at[pl.ds(base, rows), :], sems.at[0])


def row_copies(place_ref, own, mine, others, left, full, sems):
    count = len(mine)
    rows = own.shape[0]
    half = rows // 2
    core = place_ref[2 * count + 1]
    copies = [own_copy(place_ref, own, full, sems, rows)]
    for which, (refs, side) in enumerate(((mine, core), (others, 1 - core))):
        for i, ref in enumerate(refs):
            at = 1 + which * count + i
            base = pl.multiple_of(place_ref[at] * rows + side * half, 16)
            copies.append(
                pltpu.make_async_copy(
                    ref.at[:, pl.ds(left, full.shape[1])], full.at[pl.ds(base, half), :], sems.at[at]
                )
            )
    return copies


def down_blocks(rows, columns, tall):
    whole = rows // tall
    blocks = [(k * tall, 0, tall, columns, 0, k * columns) for k in range(whole)]
    left = rows - whole * tall
    if left:
        blocks += [
            (whole * tall, 128 * q, left, 128, q * left, whole * columns) for q in range(columns // 128)
        ]
    return blocks


def down_width(rows, columns, tall):
    return rows // tall * columns + (128 if rows % tall else 0)


def down_copies(place_ref, own, mine, others, left, full, sems, hidden):
    if not mine:
        return [pltpu.make_async_copy(own, full.at[pl.ds(0, hidden), :], sems.at[0])]
    count = len(mine)
    rows = own.shape[0]
    half = own.shape[1] // 2
    core = place_ref[2 * count + 1]
    blocks = down_blocks(rows, half, mine[0].shape[0])
    copies = [own_copy(place_ref, own, full, sems, rows)]
    for which, (refs, side) in enumerate(((mine, core), (others, 1 - core))):
        for i, ref in enumerate(refs):
            at = 1 + which * count + i
            side_at = pl.multiple_of(side * half, 128)
            for k, (row, column, tall, wide, packed_row, packed_column) in enumerate(blocks):
                base = pl.multiple_of(place_ref[at] * rows + row, 16)
                copies.append(
                    pltpu.make_async_copy(
                        ref.at[pl.ds(packed_row, tall), pl.ds(left + packed_column, wide)],
                        full.at[pl.ds(base, tall), pl.ds(pl.multiple_of(side_at + column, 128), wide)],
                        sems.at[1 + (at - 1) * len(blocks) + k],
                    )
                )
    return copies


def pack_pieces(place_ref, in_ref, out_ref, down_ref, first_ref, second_ref, sems):
    half = in_ref.shape[0] // 2
    core = place_ref[place_ref.shape[0] - 2]
    base = pl.multiple_of(core * half, 16)
    also = out_ref.shape[1]
    copies = [
        pltpu.make_async_copy(
            out_ref.at[pl.ds(base, half), :], first_ref.at[:, pl.ds(0, also)], sems.at[0]
        ),
        pltpu.make_async_copy(in_ref.at[pl.ds(base, half), :], second_ref, sems.at[1]),
    ]
    if first_ref.shape[1] > also:
        columns = down_ref.shape[1] // 2
        side = pl.multiple_of(core * columns, 128)
        blocks = down_blocks(down_ref.shape[0], columns, half)
        for k, (row, column, tall, part, packed_row, packed_column) in enumerate(blocks):
            copies.append(
                pltpu.make_async_copy(
                    down_ref.at[pl.ds(row, tall), pl.ds(pl.multiple_of(side + column, 128), part)],
                    first_ref.at[pl.ds(packed_row, tall), pl.ds(also + packed_column, part)],
                    sems.at[2 + k],
                )
            )
    for copy in copies:
        copy.start()
    for copy in copies:
        copy.wait()


def run_pack_pieces(place, w_in, w_out, w_down, regular):
    half = w_in.shape[0] // 2
    down = (w_down.shape[0], w_down.shape[1] // 2, half)
    blocks = len(down_blocks(*down)) if regular else 0
    wide = w_out.shape[1] + (down_width(*down) if regular else 0)
    return pl.pallas_call(
        pack_pieces,
        name="pack_pieces",
        out_shape=(
            jax.ShapeDtypeStruct((half, wide), BF16),
            jax.ShapeDtypeStruct((half, w_in.shape[1]), BF16),
        ),
        in_specs=[smem_spec()] + [any_spec()] * 3,
        out_specs=[vmem_spec()] * 2,
        scratch_shapes=[pltpu.SemaphoreType.DMA((2 + blocks,))],
        compiler_params=params(),
        cost_estimate=cost(1e6, 5e6),
    )(place, w_in, w_out, w_down)


def attention_forward(
    seq_count, heads, group, low_ref, high_ref, place_ref, order_ref, start_ref, end_ref,
    cos_ref, sin_ref, *refs,
):
    x_hbm, refs = (refs[:1], refs[1:]) if len(refs[0].shape) == 3 else (refs[:seq_count], refs[seq_count:])
    pieces, refs = refs[:-15], refs[-15:]
    gains_ref, w_ref, normed_hbm, packed_ref, att_ref, out_ref, lse_ref = refs[:7]
    x_ref, normed_ref, qkv_t, k_rows, o_rows, scores_ref, x_sems, normed_sems = refs[7:]
    width = heads * HD
    rows = group // seq_count
    blocks = group // BLOCK
    if len(x_hbm) == 1:
        chunks = list(range(seq_count))
        x_hbm = [x_hbm[0].at[i] for i in chunks]
    else:
        core, z = place_ref[7], place_ref[8]
        chunks = [(z ^ k) * 2 + side for side in (core, 1 - core) for k in block_order(side)]
    fetches = [pltpu.make_async_copy(x_hbm[i], x_ref.at[i], x_sems.at[i]) for i in range(seq_count)]
    stores = [
        pltpu.make_async_copy(normed_ref.at[i], normed_hbm.at[chunks[i]], normed_sems.at[i])
        for i in range(seq_count)
    ]
    for fetch in fetches:
        fetch.start()
    if len(pieces) == 2:
        w_ref[...] = pieces[0][...]
        gains_ref[...] = pieces[1][...]
    else:
        tall = w_ref.shape[0] // len(pieces)
        for key, piece in enumerate(pieces):
            base = pl.multiple_of(place_ref[key] * tall, 128)
            w_ref[pl.ds(base, tall), :] = piece[:tall]
            gains_ref[:, pl.ds(base, tall)] = piece[tall : tall + 2, :tall].astype(F32)
    gain_ref = gains_ref.at[pl.ds(0, 1), :]

    def project(i):
        x = x_ref[i].astype(F32)
        center = x - jnp.mean(x, axis=-1, keepdims=True)
        spread = jnp.mean(center * center, axis=-1, keepdims=True)
        normed = (center * lax.rsqrt(spread + NORM_EPS) * gain_ref[...]).astype(BF16)
        normed_ref[i] = normed
        qkv = nn_dot(normed, w_ref[...]).astype(BF16)
        qkv_t[chunks[i]] = qkv.T

    for i in range(seq_count):
        fetches[i].wait()
        project(i)
        stores[i].start()

    def pack(i, carry):
        at = pl.ds(pl.multiple_of(i * BLOCK, BLOCK), BLOCK)
        order = order_ref[:, at]
        total = jnp.zeros((3 * width, BLOCK), F32)
        for s in range(seq_count):
            here = lax.broadcasted_iota(jnp.int32, (rows, BLOCK), 0) + s * rows
            hot = jnp.where(here == order, 1.0, 0.0).astype(BF16)
            total = total + nn_dot(qkv_t[s], hot)
        cos = cos_ref[:, at]
        sin = sin_ref[:, at]
        half = HD // 2
        for part in range(2):
            for h in range(heads):
                base = part * width + h * HD
                first = total[base : base + half]
                second = total[base + half : base + HD]
                turned = jnp.concatenate(
                    [first * cos - second * sin, second * cos + first * sin], axis=0
                ).astype(BF16)
                packed_ref[base : base + HD, at] = turned
                if part == 1:
                    k_rows[h, at, :] = turned.T
        packed_ref[2 * width :, at] = total[2 * width :].astype(BF16)
        return carry

    lax.fori_loop(0, blocks, pack, 0)
    scale = HD**-0.5 * LOG2E

    def attend(i, carry):
        at = pl.ds(pl.multiple_of(i * WIDE, WIDE), WIDE)
        start = start_ref[:, at]
        end = end_ref[:, at]
        queries = [packed_ref[h * HD : (h + 1) * HD, at] for h in range(heads)]

        low, high = low_ref[i], high_ref[i]

        def score(j, tops):
            there = pl.ds(pl.multiple_of(j * BLOCK, BLOCK), BLOCK)
            where = lax.broadcasted_iota(jnp.int32, (BLOCK, WIDE), 0) + j * BLOCK
            same = jnp.logical_and(where >= start, where < end)
            following = []
            for h in range(heads):
                scores = jnp.where(same, nn_dot(k_rows[h, there, :], queries[h]) * scale, -1e30)
                scores_ref[j, h] = scores
                following.append(jnp.maximum(tops[h], jnp.max(scores.reshape(-1, 8, WIDE), axis=0)))
            return tuple(following)

        tops = lax.fori_loop(low, high, score, tuple(jnp.full((8, WIDE), -1e30, F32) for _ in range(heads)))
        tops = [jnp.max(top, axis=0, keepdims=True) for top in tops]

        def weigh(j, state):
            there = pl.ds(pl.multiple_of(j * BLOCK, BLOCK), BLOCK)
            following = []
            for h in range(heads):
                total, acc = state[h]
                probs = jnp.exp2(scores_ref[j, h] - tops[h])
                total = total + jnp.sum(probs.reshape(-1, 8, WIDE), axis=0)
                base = 2 * width + h * HD
                acc = acc + nn_dot(packed_ref[base : base + HD, there], probs.astype(BF16))
                following.append((total, acc))
            return tuple(following)

        first = tuple((jnp.zeros((8, WIDE), F32), jnp.zeros((HD, WIDE), F32)) for _ in range(heads))
        last = lax.fori_loop(low, high, weigh, first)
        outs = []
        for h in range(heads):
            total, acc = last[h]
            total = jnp.sum(total, axis=0, keepdims=True)
            out = acc / total
            out_ref[h * HD : (h + 1) * HD, at] = out
            lse_ref[h : h + 1, at] = tops[h] + jnp.log2(total)
            outs.append(out)
        o_rows[at, :] = jnp.concatenate(outs, axis=0).astype(BF16).T
        return carry

    lax.fori_loop(0, group // WIDE, attend, 0)

    def arrive(i, carry):
        here = lax.broadcasted_iota(jnp.int32, (rows, group), 0) + i * rows
        hot = jnp.where(here == order_ref[...], 1.0, 0.0).astype(BF16)
        att_ref[i] = nn_dot(hot, o_rows[...]).astype(BF16)
        return carry

    lax.fori_loop(0, seq_count, arrive, 0)
    for store in stores:
        store.wait()


def run_attention_forward(place, chunks, pieces, layout, heads):
    rows, dim = chunks[0].shape[-2:]
    group = layout[2].shape[1]
    seq_count = group // rows
    width = heads * HD
    (low, high), _, order, start, end, cos, sin = layout
    return pl.pallas_call(
        functools.partial(attention_forward, seq_count, heads, group),
        name="attention_forward",
        out_shape=(
            jax.ShapeDtypeStruct((2, dim), F32),
            jax.ShapeDtypeStruct((dim, 3 * width), BF16),
            jax.ShapeDtypeStruct((seq_count, rows, dim), BF16),
            jax.ShapeDtypeStruct((3 * width, group), BF16),
            jax.ShapeDtypeStruct((seq_count, rows, width), BF16),
            jax.ShapeDtypeStruct((width, group), F32),
            jax.ShapeDtypeStruct((heads, group), F32),
        ),
        in_specs=[smem_spec()] * 3 + [vmem_spec()] * 5 + [any_spec()] * len(chunks) + [vmem_spec()] * len(pieces),
        out_specs=[vmem_spec()] * 2 + [any_spec()] + [vmem_spec()] * 4,
        scratch_shapes=[
            pltpu.VMEM((seq_count, rows, dim), BF16),
            pltpu.VMEM((seq_count, rows, dim), BF16),
            pltpu.VMEM((seq_count, 3 * width, rows), BF16),
            pltpu.VMEM((heads, group, HD), BF16),
            pltpu.VMEM((group, width), BF16),
            pltpu.VMEM((group // BLOCK, heads, BLOCK, WIDE), F32),
            pltpu.SemaphoreType.DMA((seq_count,)),
            pltpu.SemaphoreType.DMA((seq_count,)),
        ],
        compiler_params=params(),
        cost_estimate=cost(24e9, 20e6),
    )(low, high, place, order, start, end, cos, sin, *chunks, *pieces)


def attention_backward(
    seq_count, heads, group, low_ref, high_ref, place_ref, dout_ref, packed_ref, out_ref, lse_ref, order_ref,
    start_ref, end_ref, cos_ref, sin_ref, w_ref, grad_ref, *refs,
):
    shares, refs = refs[:-9], refs[-9:]
    dout_t, dpack_t, drows, qrows, krows, vrows, delta_ref, dq_t, grows = refs
    width = heads * HD
    rows = group // seq_count
    blocks = group // BLOCK
    scale = HD**-0.5

    def turn(i, carry):
        dout_t[i] = dout_ref[i].T
        return carry

    lax.fori_loop(0, seq_count, turn, 0)

    def pack(i, carry):
        at = pl.ds(pl.multiple_of(i * BLOCK, BLOCK), BLOCK)
        order = order_ref[:, at]
        total = jnp.zeros((width, BLOCK), F32)
        for s in range(seq_count):
            here = lax.broadcasted_iota(jnp.int32, (rows, BLOCK), 0) + s * rows
            hot = jnp.where(here == order, 1.0, 0.0).astype(BF16)
            total = total + nn_dot(dout_t[s], hot)
        dpack_t[:, at] = total.astype(BF16)
        for h in range(heads):
            mine = total[h * HD : (h + 1) * HD]
            delta_ref[h : h + 1, at] = jnp.sum(
                mine * out_ref[h * HD : (h + 1) * HD, at], axis=0, keepdims=True
            )
            drows[h, at, :] = mine.T.astype(BF16)
            for part, ref in enumerate((qrows, krows, vrows)):
                base = part * width + h * HD
                ref[h, at, :] = packed_ref[base : base + HD, at].T
        dq_t[:, at] = jnp.zeros((width, BLOCK), F32)
        return carry

    lax.fori_loop(0, blocks, pack, 0)

    def keys(j, carry):
        there = pl.ds(pl.multiple_of(j * BLOCK, BLOCK), BLOCK)
        where = lax.broadcasted_iota(jnp.int32, (BLOCK, WIDE), 0) + j * BLOCK

        def queries(i, state):
            at = pl.ds(pl.multiple_of(i * WIDE, WIDE), WIDE)
            same = jnp.logical_and(where >= start_ref[:, at], where < end_ref[:, at])
            following = []
            for h in range(heads):
                dk, dv = state[h]
                base = h * HD
                key_rows = krows[h, there, :]
                query_t = packed_ref[base : base + HD, at]
                scores = nn_dot(key_rows, query_t) * (scale * LOG2E)
                scores = jnp.where(same, scores, -1e30)
                probs = jnp.exp2(scores - lse_ref[h : h + 1, at])
                dprobs = nn_dot(vrows[h, there, :], dpack_t[base : base + HD, at])
                raw = (probs * (dprobs - delta_ref[h : h + 1, at]) * scale).astype(BF16)
                dv = dv + nn_dot(probs.astype(BF16), drows[h, at, :])
                dk = dk + nn_dot(raw, qrows[h, at, :])
                key_t = packed_ref[width + base : width + base + HD, there]
                dq_t[base : base + HD, at] += nn_dot(key_t, raw)
                following.append((dk, dv))
            return tuple(following)

        zero = jnp.zeros((BLOCK, HD), F32)
        last = lax.fori_loop(low_ref[j], high_ref[j], queries, tuple((zero, zero) for _ in range(heads)))
        cos = cos_ref[:, there]
        sin = sin_ref[:, there]
        half = HD // 2
        turned = []
        for h in range(heads):
            dk_t = last[h][0].T
            first, second = dk_t[:half], dk_t[half:]
            turned.append(first * cos + second * sin)
            turned.append(second * cos - first * sin)
        grows[there, width : 2 * width] = jnp.concatenate(turned, axis=0).T.astype(BF16)
        grows[there, 2 * width :] = jnp.concatenate([last[h][1] for h in range(heads)], axis=1).astype(BF16)
        return carry

    lax.fori_loop(0, blocks, keys, 0)

    def finish(i, carry):
        at = pl.ds(pl.multiple_of(i * BLOCK, BLOCK), BLOCK)
        cos = cos_ref[:, at]
        sin = sin_ref[:, at]
        half = HD // 2
        turned = []
        for h in range(heads):
            first = dq_t[h * HD : h * HD + half, at]
            second = dq_t[h * HD + half : (h + 1) * HD, at]
            turned.append(first * cos + second * sin)
            turned.append(second * cos - first * sin)
        grows[at, :width] = jnp.concatenate(turned, axis=0).T.astype(BF16)
        return carry

    lax.fori_loop(0, blocks, finish, 0)

    def arrive(i):
        here = lax.broadcasted_iota(jnp.int32, (rows, group), 0) + i * rows
        hot = jnp.where(here == order_ref[...], 1.0, 0.0).astype(BF16)
        grad = nn_dot(hot, grows[...]).astype(BF16)
        grad_ref[i] = grad
        return nt_dot(grad, w_ref[...]).astype(BF16)

    if len(shares) == 1:

        def each(i, carry):
            shares[0][i] = arrive(i)
            return carry

        lax.fori_loop(0, seq_count, each, 0)
    else:
        for side, share in zip((1 - place_ref[7], place_ref[7]), shares):

            def each(j, carry, side=side, share=share):
                k = jnp.where(j == 1, 2 - side, jnp.where(j == 2, 1 + side, j))
                share[j] = arrive((place_ref[8] ^ k) * 2 + side)
                return carry

            lax.fori_loop(0, seq_count // 2, each, 0)


def run_attention_backward(place, dout, packed, out_t, lse, w_heads, layout, heads, regular):
    seq_count, rows, width = dout.shape
    group = seq_count * rows
    dim = w_heads.shape[0]
    _, (low, high), order, start, end, cos, sin = layout
    shares = [seq_count // 2] * 2 if regular else [seq_count]
    return pl.pallas_call(
        functools.partial(attention_backward, seq_count, heads, group),
        name="attention_backward",
        out_shape=[jax.ShapeDtypeStruct((seq_count, rows, 3 * width), BF16)]
        + [jax.ShapeDtypeStruct((share, rows, dim), BF16) for share in shares],
        in_specs=[smem_spec()] * 3 + [vmem_spec()] * 10,
        out_specs=[vmem_spec()] * (1 + len(shares)),
        scratch_shapes=[
            pltpu.VMEM((seq_count, width, rows), BF16),
            pltpu.VMEM((width, group), BF16),
            pltpu.VMEM((heads, group, HD), BF16),
            pltpu.VMEM((heads, group, HD), BF16),
            pltpu.VMEM((heads, group, HD), BF16),
            pltpu.VMEM((heads, group, HD), BF16),
            pltpu.VMEM((heads, group), F32),
            pltpu.VMEM((width, group), F32),
            pltpu.VMEM((group, 3 * width), BF16),
        ],
        compiler_params=params(),
        cost_estimate=cost(33e9, 15e6),
    )(low, high, place, dout, packed, out_t, lse, order, start, end, cos, sin, w_heads)


def qkv_weight_grad(seq_count, place_ref, normed_ref, grad_ref, *refs):
    outs, (total, turned) = refs[:-2], refs[-2:]
    total[...] = jnp.zeros_like(total)

    def step(i, carry):
        total[...] += nn_dot(grad_ref[i].T, normed_ref[i])
        return carry

    lax.fori_loop(0, seq_count, step, 0)
    if len(outs) == 1:
        outs[0][...] = total[...].T.astype(BF16)
        return
    turned[...] = total[...].T
    rows = outs[0].shape[1]
    for ref, keys in zip(outs, ((2, 3), (1,), (0,))):
        for at, key in enumerate(keys):
            base = pl.multiple_of(place_ref[key] * rows, 16)
            ref[at] = turned[pl.ds(base, rows), :].astype(BF16)


def run_qkv_weight_grad(place, normed, grad, regular):
    seq_count, rows, dim = normed.shape
    width = grad.shape[-1]
    if regular:
        outs = tuple(jax.ShapeDtypeStruct((n, dim // 4, width), BF16) for n in (2, 1, 1))
    else:
        outs = (jax.ShapeDtypeStruct((dim, width), BF16),)
    return pl.pallas_call(
        functools.partial(qkv_weight_grad, seq_count),
        name="qkv_weight_grad",
        out_shape=outs,
        in_specs=[smem_spec()] + [vmem_spec()] * 2,
        out_specs=[vmem_spec()] * len(outs),
        scratch_shapes=[pltpu.VMEM((width, dim), F32), pltpu.VMEM((dim, width), F32)],
        compiler_params=params(),
        cost_estimate=cost(3e9, 6e6),
    )(place, normed, grad)


def padded(hidden):
    return -(-hidden // 128) * 128


def load_down(place_ref, refs, count, hidden, left, full, sems):
    copies = down_copies(place_ref, refs[0], refs[1 : 1 + count], refs[1 + count :], left, full, sems, hidden)
    for copy in copies:
        copy.start()
    tail = padded(hidden) - hidden
    if tail:
        full[pl.ds(hidden, tail), :] = jnp.zeros((tail, full.shape[1]), BF16)
    for copy in copies:
        copy.wait()


def down_semaphores(downs):
    if len(downs) == 1:
        return pltpu.SemaphoreType.DMA((1,))
    blocks = len(down_blocks(downs[0].shape[0], downs[0].shape[1] // 2, downs[1].shape[0]))
    return pltpu.SemaphoreType.DMA((1 + (len(downs) - 1) * blocks,))


def hidden_grad(hidden, left, place_ref, cot_ref, *refs):
    downs, (out_ref, full, sems) = refs[:-3], refs[-3:]
    load_down(place_ref, downs, (len(downs) - 1) // 2, hidden, left, full, sems)
    cot = cot_ref[...]
    tiles = padded(hidden) // 128
    wide = 128 * max(n for n in (1, 2, 3) if tiles % n == 0)

    def step(i, carry):
        at = pl.multiple_of(i * wide, 128)
        out_ref[:, pl.ds(at, wide)] = nt_dot(cot, full[pl.ds(at, wide), :])
        return carry

    lax.fori_loop(0, padded(hidden) // wide, step, 0)


def run_hidden_grad(place, cot, downs, left, hidden):
    rows, dim = cot.shape
    return pl.pallas_call(
        functools.partial(hidden_grad, hidden, left),
        name="hidden_grad",
        out_shape=jax.ShapeDtypeStruct((rows, padded(hidden)), F32),
        in_specs=[smem_spec(), vmem_spec()] + [any_spec()] * len(downs),
        out_specs=vmem_spec(),
        scratch_shapes=[pltpu.VMEM((padded(hidden), dim), BF16), down_semaphores(downs)],
        compiler_params=params(),
        cost_estimate=cost(4e9, 9e6),
    )(place, cot, *downs)


def layer_result(hidden, left, place_ref, mid_ref, keep_ref, *refs):
    downs, (out_ref, full, sems) = refs[:-3], refs[-3:]
    load_down(place_ref, downs, (len(downs) - 1) // 2, hidden, left, full, sems)
    wide = padded(hidden)

    def step(i, carry):
        at = pl.ds(pl.multiple_of(i * 256, 256), 256)
        out_ref[:, at] = (mid_ref[:, at] + nn_dot(keep_ref[:, :wide], full[:, at])).astype(BF16)
        return carry

    lax.fori_loop(0, out_ref.shape[1] // 256, step, 0)


def run_layer_result(place, middle, keep, downs, left, hidden):
    rows, dim = middle.shape
    return pl.pallas_call(
        functools.partial(layer_result, hidden, left),
        name="layer_result",
        out_shape=jax.ShapeDtypeStruct((rows, dim), BF16),
        in_specs=[smem_spec()] + [vmem_spec()] * 2 + [any_spec()] * len(downs),
        out_specs=vmem_spec(),
        scratch_shapes=[pltpu.VMEM((padded(hidden), dim), BF16), down_semaphores(downs)],
        compiler_params=params(),
        cost_estimate=cost(4e9, 9e6),
    )(place, middle, keep, *downs)


def feed_forward(
    count, hidden, heads_width, place_ref, x_ref, att_ref, cot_ref, gain_ref, gh_hbm, *refs
):
    out_own, in_own, refs = refs[0], refs[1], refs[2:]
    first, others, refs = refs[:count], refs[count : 2 * count], refs[2 * count :]
    second, second_others, refs = refs[:count], refs[count : 2 * count], refs[2 * count :]
    mid_ref, gmid_ref, send_hbm, keep_hbm, ga_ref = refs[:5]
    wo, wi, both, early, late, send_ref, keep_ref, gh_ref, sem_o, sem_i, sems = refs[5:]
    fetch = pltpu.make_async_copy(gh_hbm, gh_ref, sems.at[0])
    send_out = pltpu.make_async_copy(send_ref, send_hbm, sems.at[1])
    keep_out = pltpu.make_async_copy(keep_ref, keep_hbm, sems.at[2])
    dim = x_ref.shape[1]
    wide_hidden = padded(hidden)
    nt_ref = send_ref.at[:, pl.ds(2 * hidden, dim)]
    gboth_ref = send_ref
    hid_ref = keep_ref
    gbr_ref = keep_ref.at[:, pl.ds(wide_hidden, dim)]
    att_all_ref = keep_ref.at[:, pl.ds(wide_hidden + dim, dim)]
    keep_ref[:, pl.ds(wide_hidden + 2 * dim, dim)] = cot_ref[...]
    copies_o = row_copies(place_ref, out_own, first, others, 0, wo, sem_o)
    copies_i = row_copies(place_ref, in_own, second, second_others, 0, wi, sem_i)
    for copy in copies_o:
        copy.start()
    for copy in copies_i:
        copy.start()
    fetch.start()
    att = jnp.concatenate([att_ref[s] for s in range(att_ref.shape[0])], axis=1)
    att_all_ref[...] = att
    for copy in copies_o:
        copy.wait()

    def branch(i, carry):
        at = pl.ds(pl.multiple_of(i * 256, 256), 256)
        mid_ref[:, at] = x_ref[:, at].astype(F32) + nn_dot(att_all_ref[...], wo[:, at])
        return carry

    lax.fori_loop(0, dim // 256, branch, 0)
    middle = mid_ref[...]
    center = middle - jnp.mean(middle, axis=-1, keepdims=True)
    spread = jnp.mean(center * center, axis=-1, keepdims=True)
    scale = lax.rsqrt(spread + NORM_EPS)
    nt_ref[...] = (center * scale * gain_ref[...]).astype(BF16)
    for copy in copies_i:
        copy.wait()
    fetch.wait()
    wide = 2 * hidden // 128

    def expand(i, carry):
        at = pl.ds(pl.multiple_of(i * 256, 256), 256)
        both[:, at] = nn_dot(nt_ref[...], wi[:, at])
        return carry

    lax.fori_loop(0, wide // 2, expand, 0)
    if wide % 2:
        both[:, pl.ds(128 * (wide - 1), 128)] = nn_dot(nt_ref[...], wi[:, pl.ds(128 * (wide - 1), 128)])
    both[:, pl.ds(128 * wide, 128)] = jnp.zeros((both.shape[0], 128), F32)
    tiles = padded(hidden) // 128
    whole = hidden // 128
    lanes = lax.broadcasted_iota(jnp.int32, (both.shape[0], 128), 1)
    shift = hidden % 128

    def tile(i):
        return pl.ds(pl.multiple_of(i * 128, 128), 128)

    def gates(i):
        a = both[:, tile(i)]
        if shift:
            left = pltpu.roll(both[:, tile(whole + i)], 128 - shift, 1)
            right = pltpu.roll(both[:, tile(whole + i + 1)], 128 - shift, 1)
            b = jnp.where(lanes < 128 - shift, left, right)
        else:
            b = both[:, tile(whole + i)]
        gh = gh_ref[:, tile(i)]
        phi = 0.5 * (1.0 + lax.erf(a * (0.5**0.5)))
        gelu = a * phi
        slope = phi + a * ((0.5 / math.pi) ** 0.5 * jnp.exp(-0.5 * a * a))
        hid_ref[:, tile(i)] = (gelu * b).astype(BF16)
        return gh * b * slope, gh * gelu

    if shift:
        first_a, first_b = gates(0)
        gboth_ref[:, tile(0)] = first_a.astype(BF16)
        early[...] = pltpu.roll(first_b, shift, 1)
        late[...] = early[...]

        def inner(i, carry):
            ga, gb = gates(i)
            turned = pltpu.roll(gb, shift, 1)
            gboth_ref[:, tile(i)] = ga.astype(BF16)
            gboth_ref[:, tile(whole + i)] = jnp.where(lanes < shift, late[...], turned).astype(BF16)
            late[...] = turned
            return carry

        lax.fori_loop(1, tiles - 1, inner, 0)
        ga, gb = gates(tiles - 1)
        turned = pltpu.roll(gb, shift, 1)
        gboth_ref[:, tile(whole)] = jnp.where(lanes < shift, ga, early[...]).astype(BF16)
        gboth_ref[:, tile(2 * whole)] = jnp.where(lanes < shift, late[...], turned).astype(BF16)
    else:

        def inner(i, carry):
            ga, gb = gates(i)
            gboth_ref[:, tile(i)] = ga.astype(BF16)
            gboth_ref[:, tile(whole + i)] = gb.astype(BF16)
            return carry

        lax.fori_loop(0, tiles, inner, 0)

    send_out.start()

    def back(i, carry):
        at = pl.multiple_of(i * 256, 256)
        both[:, pl.ds(at, 256)] = nt_dot(gboth_ref[:, : 2 * hidden], wi[pl.ds(at, 256), :])
        return carry

    lax.fori_loop(0, dim // 256, back, 0)
    middle = mid_ref[...]
    center = middle - jnp.mean(middle, axis=-1, keepdims=True)
    spread = jnp.mean(center * center, axis=-1, keepdims=True)
    scale = lax.rsqrt(spread + NORM_EPS)
    normal = center * scale
    e = both[:, pl.ds(0, dim)] * gain_ref[...]
    pull = e - jnp.mean(e, axis=-1, keepdims=True) - normal * jnp.mean(e * normal, axis=-1, keepdims=True)
    gmid = cot_ref[...].astype(F32) + scale * pull
    gmid_ref[...] = gmid
    gbr_ref[...] = gmid.astype(BF16)
    keep_out.start()

    def spread_out(i, carry):
        at = pl.multiple_of(i * 256, 256)
        both[:, pl.ds(at, 256)] = nt_dot(gbr_ref[...], wo[pl.ds(at, 256), :])
        return carry

    lax.fori_loop(0, dim // 256, spread_out, 0)
    for s in range(att_ref.shape[0]):
        ga_ref[s] = both[:, s * heads_width : (s + 1) * heads_width].astype(BF16)
    send_out.wait()
    keep_out.wait()


def run_feed_forward(place, x, att, cot, gain, grad_hidden, w_out, w_in, first, second, hidden):
    rows, dim = x.shape
    seq_count, _, heads_width = att.shape
    count = len(first) // 2
    return pl.pallas_call(
        functools.partial(feed_forward, count, hidden, heads_width),
        name="feed_forward",
        out_shape=(
            jax.ShapeDtypeStruct((rows, dim), F32),
            jax.ShapeDtypeStruct((rows, dim), F32),
            jax.ShapeDtypeStruct((rows, 2 * hidden + dim), BF16),
            jax.ShapeDtypeStruct((rows, padded(hidden) + 3 * dim), BF16),
            jax.ShapeDtypeStruct((seq_count, rows, heads_width), BF16),
        ),
        in_specs=[smem_spec()] + [vmem_spec()] * 4 + [any_spec()] * (3 + 4 * count),
        out_specs=[vmem_spec()] * 2 + [any_spec()] * 2 + [vmem_spec()],
        scratch_shapes=[
            pltpu.VMEM((dim, dim), BF16),
            pltpu.VMEM((dim, 2 * hidden), BF16),
            pltpu.VMEM((rows, 2 * hidden + 128), F32),
            pltpu.VMEM((rows, 128), F32),
            pltpu.VMEM((rows, 128), F32),
            pltpu.VMEM((rows, 2 * hidden + dim), BF16),
            pltpu.VMEM((rows, padded(hidden) + 3 * dim), BF16),
            pltpu.VMEM((rows, padded(hidden)), F32),
            pltpu.SemaphoreType.DMA((2 * count + 1,)),
            pltpu.SemaphoreType.DMA((2 * count + 1,)),
            pltpu.SemaphoreType.DMA((3,)),
        ],
        compiler_params=params(),
        cost_estimate=cost(16e9, 24e6),
    )(place, x, att, cot, gain, grad_hidden, w_out, w_in, *first, *second)


def block_order(core):
    return (0, 2 - core, 1 + core, 3)


def in_grad(hidden, wide, place_ref, send_ref, other_ref, a_ref, b_ref, c_ref, turned, picked):
    tokens = send_ref.shape[0]
    rows = turned.shape[0] // 4
    half, short = rows // 2, rows // 8

    @pl.when(pl.program_id(0) == 0)
    def _():
        turned[:, :tokens] = send_ref[:, 2 * hidden :].T
        turned[:, tokens:] = other_ref[:, 2 * hidden :].T
        core, z = place_ref[7], place_ref[8]
        for at, key in enumerate((2, 3, 1, 0)):
            for j, k in enumerate(block_order(core)):
                base = pl.multiple_of(place_ref[key] * rows + core * half + (z ^ k) * short, 16)
                to = at * half + j * short
                picked[to : to + short, :] = turned[pl.ds(base, short), :]

    at = pl.ds(pl.multiple_of(pl.program_id(0) * wide, 128), wide)
    right = jnp.concatenate([send_ref[:, at], other_ref[:, at]], axis=0)
    result = nn_dot(picked[...], right).astype(BF16)
    a_ref[0] = result[:half]
    a_ref[1] = result[half : 2 * half]
    b_ref[0] = result[2 * half : 3 * half]
    c_ref[0] = result[3 * half :]


def run_in_grad(place, send, other, hidden):
    tokens = send.shape[0]
    features = send.shape[1] - 2 * hidden
    columns = 2 * hidden
    half = features // 8
    wide = 896
    whole = pl.BlockSpec(send.shape, lambda i: (0, 0))
    return pl.pallas_call(
        functools.partial(in_grad, hidden, wide),
        name="in_grad",
        out_shape=tuple(jax.ShapeDtypeStruct((n, half, columns), BF16) for n in (2, 1, 1)),
        grid=(pl.cdiv(columns, wide),),
        in_specs=[smem_spec(), whole, whole],
        out_specs=[pl.BlockSpec((n, half, wide), lambda i: (0, 0, i)) for n in (2, 1, 1)],
        scratch_shapes=[
            pltpu.VMEM((features, 2 * tokens), BF16),
            pltpu.VMEM((features // 2, 2 * tokens), BF16),
        ],
        compiler_params=params(),
        cost_estimate=cost(2.0 * 2 * tokens * features * columns, 4 * tokens * columns + features * columns),
    )(place, send, other)


def rest_grad(hidden, place_ref, keep_ref, other_ref, a_ref, b_ref, c_ref, turned, picked):
    tokens = keep_ref.shape[0]
    wide = padded(hidden)
    dim = (keep_ref.shape[1] - wide) // 3
    half = dim // 2
    down_rows = hidden // 4
    short = dim // 32
    core, z = place_ref[7], place_ref[8]
    at = pl.program_id(0)

    @pl.when(at == 0)
    def _():
        turned[:wide, :tokens] = keep_ref[:, :wide].T
        turned[:wide, tokens:] = other_ref[:, :wide].T
        turned[wide:, :tokens] = keep_ref[:, wide + dim : wide + 2 * dim].T
        turned[wide:, tokens:] = other_ref[:, wide + dim : wide + 2 * dim].T
        for j, k in enumerate(block_order(core)):
            left = pl.ds(pl.multiple_of(wide + 2 * dim + core * half + (z ^ k) * 128, 128), 128)
            picked[:tokens, j * 128 : (j + 1) * 128] = keep_ref[:, left]
            picked[tokens:, j * 128 : (j + 1) * 128] = other_ref[:, left]
        picked[:tokens, half:] = keep_ref[:, wide : wide + dim]
        picked[tokens:, half:] = other_ref[:, wide : wide + dim]

    owner = place_ref[jnp.where(at < 2, at + 2, 3 - at)]
    base = pl.multiple_of(owner * down_rows, 16)
    down = nn_dot(turned[pl.ds(base, down_rows), :], picked[:, :half]).astype(BF16)
    left = []
    for k in block_order(core):
        base = pl.multiple_of(wide + owner * 8 * short + core * 4 * short + (z ^ k) * short, 16)
        left.append(turned[pl.ds(base, short), :])
    out = nn_dot(jnp.concatenate(left, axis=0), picked[:, half:]).astype(BF16)
    first = dim // 128 * short

    def store(ref):
        for j in range(4):
            for t in range(dim // 128):
                ref[0, j, t * short : (t + 1) * short, :] = out[
                    j * short : (j + 1) * short, t * 128 : (t + 1) * 128
                ]
            ref[0, j, first:, :] = down[:, j * 128 : (j + 1) * 128]

    pl.when(at < 2)(lambda: store(a_ref))
    pl.when(at == 2)(lambda: store(b_ref))
    pl.when(at == 3)(lambda: store(c_ref))


def run_rest_grad(place, keep, other, hidden):
    tokens = keep.shape[0]
    wide = padded(hidden)
    dim = (keep.shape[1] - wide) // 3
    tall = dim // 128 * (dim // 32) + hidden // 4
    whole = pl.BlockSpec(keep.shape, lambda i: (0, 0))
    return pl.pallas_call(
        functools.partial(rest_grad, hidden),
        name="rest_grad",
        out_shape=tuple(jax.ShapeDtypeStruct((n, 4, tall, 128), BF16) for n in (2, 1, 1)),
        grid=(4,),
        in_specs=[smem_spec(), whole, whole],
        out_specs=[
            pl.BlockSpec((1, 4, tall, 128), lambda i: (jnp.minimum(i, 1), 0, 0, 0)),
            pl.BlockSpec((1, 4, tall, 128), lambda i: (0, 0, 0, 0)),
            pl.BlockSpec((1, 4, tall, 128), lambda i: (0, 0, 0, 0)),
        ],
        scratch_shapes=[
            pltpu.VMEM((wide + dim, 2 * tokens), BF16),
            pltpu.VMEM((2 * tokens, dim + dim // 2), BF16),
        ],
        compiler_params=params(),
        cost_estimate=cost(4e9, 10e6),
    )(place, keep, other)


def unpack_in(place_ref, *refs):
    pieces, w_ref, out_ref, sum_ref = refs[:4], refs[4], refs[5], refs[6]
    at = pl.program_id(0)
    for q, ref in enumerate(pieces):

        @pl.when(at // 2 == q)
        def _(ref=ref):
            value = ref[0].astype(F32)
            out_ref[...] = value
            sum_ref[...] = jnp.sum(value * w_ref[...].astype(F32), axis=1, keepdims=True)


def row_block(i, place_ref):
    side = jnp.where(i < 4, place_ref[7], 1 - place_ref[7])
    order = jnp.where(i % 4 == 1, 2 - side, jnp.where(i % 4 == 2, 1 + side, i % 4))
    return (side * 4 + (place_ref[8] ^ order), 0)


def run_unpack_in(place, pieces, weight):
    rows, columns = weight.shape
    short = rows // 8
    specs = [
        pl.BlockSpec((1, short, columns), lambda i, p, q=q: (jnp.clip(i - 2 * q, 0, 1), 0, 0))
        for q in range(4)
    ]
    block = pl.BlockSpec((short, columns), row_block)
    return pl.pallas_call(
        unpack_in,
        name="unpack_in",
        out_shape=(jax.ShapeDtypeStruct((rows, columns), F32), jax.ShapeDtypeStruct((rows, 1), F32)),
        grid_spec=pltpu.PrefetchScalarGridSpec(
            num_scalar_prefetch=1,
            grid=(8,),
            in_specs=specs + [block],
            out_specs=[block, pl.BlockSpec((short, 1), row_block)],
        ),
        compiler_params=params(),
        cost_estimate=cost(1e7, 11e6),
    )(place, *pieces, weight)


def sources(place_ref, pieces):
    core, z = place_ref[7], place_ref[8]
    for q, ref in enumerate(pieces):
        for at in range(2):
            side = core if q < 2 else 1 - core
            yield ref.at[at], side, z ^ block_order(side)[2 * (q % 2) + at]


def unpack_rest(place_ref, *refs):
    pieces, out_ref, down_ref = refs[:4], refs[4], refs[5]
    dim = out_ref.shape[1]
    short = dim // 32
    first = dim // 128 * short
    for ref, side, z in sources(place_ref, pieces):
        base = pl.multiple_of(side * 4 * short + z * short, 16)
        for t in range(dim // 128):
            out_ref[pl.ds(base, short), t * 128 : (t + 1) * 128] = ref[
                t * short : (t + 1) * short, :
            ].astype(F32)
        left = pl.multiple_of(side * (dim // 2) + z * 128, 128)
        down_ref[:, pl.ds(left, 128)] = ref[first:, :].astype(F32)


def run_unpack_rest(place, pieces, out_shape, down_shape):
    return pl.pallas_call(
        unpack_rest,
        name="unpack_rest",
        out_shape=(jax.ShapeDtypeStruct(out_shape, F32), jax.ShapeDtypeStruct(down_shape, F32)),
        in_specs=[smem_spec()] + [vmem_spec()] * 4,
        out_specs=[vmem_spec()] * 2,
        compiler_params=params(),
        cost_estimate=cost(1e7, 6e6),
    )(place, *pieces)


def unpack_qkv(place_ref, *refs):
    pieces, w_ref, out_ref, sum_ref = refs[:4], refs[4], refs[5], refs[6]
    width = pieces[0].shape[2] // 3
    dim = out_ref.shape[1] // 3
    total = jnp.zeros_like(sum_ref)
    for ref, side, z in sources(place_ref, pieces):
        for part in range(3):
            left = pl.multiple_of(part * dim + (z * 2 + side) * width, 128)
            value = ref[:, part * width : (part + 1) * width].astype(F32)
            out_ref[:, pl.ds(left, width)] = value
            weight = w_ref[:, pl.ds(left, width)].astype(F32)
            total = total + jnp.sum(value * weight, axis=1, keepdims=True)
    sum_ref[...] = total


def run_unpack_qkv(place, pieces, weight):
    return pl.pallas_call(
        unpack_qkv,
        name="unpack_qkv",
        out_shape=(
            jax.ShapeDtypeStruct(weight.shape, F32),
            jax.ShapeDtypeStruct((weight.shape[0], 1), F32),
        ),
        in_specs=[smem_spec()] + [vmem_spec()] * 5,
        out_specs=[vmem_spec()] * 2,
        compiler_params=params(),
        cost_estimate=cost(1e7, 7e6),
    )(place, *pieces, weight)


def input_grad(x_ref, gmid_ref, gain_ref, *refs):
    parts, out_ref = refs[:-1], refs[-1]
    x = x_ref[...].astype(F32)
    center = x - jnp.mean(x, axis=-1, keepdims=True)
    spread = jnp.mean(center * center, axis=-1, keepdims=True)
    scale = lax.rsqrt(spread + NORM_EPS)
    normal = center * scale
    e = sum(part[...].astype(F32) for part in parts) * gain_ref[...]
    pull = e - jnp.mean(e, axis=-1, keepdims=True) - normal * jnp.mean(e * normal, axis=-1, keepdims=True)
    out_ref[...] = (gmid_ref[...] + scale * pull).astype(BF16)


def run_input_grad(x, gmid, gain, parts):
    rows, dim = x.shape
    tall = rows // 4
    block = pl.BlockSpec((tall, dim), lambda i: (i, 0))
    return pl.pallas_call(
        input_grad,
        name="input_grad",
        out_shape=jax.ShapeDtypeStruct((rows, dim), BF16),
        grid=(4,),
        in_specs=[block, block, pl.BlockSpec((1, dim), lambda i: (0, 0))] + [block] * len(parts),
        out_specs=block,
        compiler_params=params(),
        cost_estimate=cost(1e8, 5e6),
    )(x, gmid, gain, *parts)


def sequence_layout(lengths, order, group):
    ends = jnp.cumsum(lengths)
    starts = ends - lengths
    index = jnp.arange(group, dtype=jnp.int32)
    passed = index[:, None] >= ends[None, :]
    start = jnp.sum(jnp.where(passed, lengths[None, :], 0), axis=1).astype(jnp.int32)
    inside = jnp.logical_and(index[:, None] >= starts[None, :], jnp.logical_not(passed))
    end = jnp.sum(jnp.where(inside, ends[None, :], 0), axis=1).astype(jnp.int32)
    places = index - start
    half = HD // 2
    speeds = jnp.power(F32(ROPE_BASE), -2.0 * jnp.arange(half, dtype=F32) / HD)
    angles = speeds[:, None] * places.astype(F32)[None, :]
    keys = (start[::WIDE] // BLOCK, (end[WIDE - 1 :: WIDE] + BLOCK - 1) // BLOCK)
    queries = (start[::BLOCK] // WIDE, (end[BLOCK - 1 :: BLOCK] + WIDE - 1) // WIDE)
    return (keys, queries, order[None, :], start[None, :], end[None, :], jnp.cos(angles), jnp.sin(angles))


def local(tokens, seq_lengths, seq_order, norm_one, w_qkv, w_out, norm_two, w_in, w_down, cotangent):
    seq_count = lax.axis_size("seq")
    fsdp_count = lax.axis_size("fsdp")
    levels = fsdp_count.bit_length() - 1
    count = fsdp_count - 1
    seq_at = lax.axis_index("seq")
    fsdp_at = lax.axis_index("fsdp")
    core = seq_at % 2
    x = tokens[0]
    cot = cotangent[0]
    rows, dim = x.shape
    group = rows * seq_count
    heads = dim // HD // seq_count
    width = heads * HD
    hidden = w_in.shape[1] // 2
    counts = (seq_count, fsdp_count)
    swap = functools.partial(core_swap, seq_count=seq_count)

    keys = [jnp.array([plane_mask(c, key, levels) for key in range(1, fsdp_count)], jnp.int32) for c in (0, 1)]
    mine = fsdp_at ^ jnp.where(core == 0, keys[0], keys[1])
    other = fsdp_at ^ jnp.where(core == 0, keys[1], keys[0])
    place = jnp.stack([fsdp_at, *mine, *other, core, seq_at // 2]).astype(jnp.int32)
    regular = fsdp_count == 4 and seq_count == 8 and w_down.shape[0] % 16 == 0 and dim == 1024

    if regular:
        chunks = [x, line_swap(x, 1, seq_count), line_swap(x, 0, seq_count)]
        chunks.append(line_swap(after(chunks[1], chunks[2]), 0, seq_count))
        chunks += [swap(chunk) for chunk in chunks]
    else:
        chunks = [lax.all_gather(x, "seq", axis=0, tiled=False)]
    own_heads = jnp.concatenate(
        [lax.dynamic_slice_in_dim(w_qkv, part * dim + seq_at * width, width, 1) for part in range(3)], axis=1
    )
    gains = jnp.stack([norm_one, norm_two])
    if regular:
        extra = jnp.pad(gains, ((0, 14), (0, 3 * width - gains.shape[1])))
        own_heads = jnp.concatenate([own_heads, extra], axis=0)
        head_pieces = [own_heads] + [plane_swap(own_heads, phase, *counts) for phase in range(2)]
        head_pieces.append(plane_swap(head_pieces[1], 1, *counts))
    else:
        head_pieces = [
            lax.all_gather(own_heads, "fsdp", axis=0, tiled=True),
            lax.all_gather(gains, "fsdp", axis=1, tiled=True).astype(F32),
        ]
    first_piece, second_piece = run_pack_pieces(place, w_in, w_out, w_down, regular)
    if regular:
        first_piece, second_piece = after(first_piece, *head_pieces[1:3]), after(second_piece, *head_pieces[1:])
    first_a, second_a = plane_swap(first_piece, 0, *counts), plane_swap(second_piece, 0, *counts)
    first = plane_gather_rest(first_piece, first_a, *counts, second_a)
    second = plane_gather_rest(second_piece, second_a, *counts, first_a)
    left = dim

    layout = sequence_layout(seq_lengths[0], seq_order[0], group)
    gains, w_heads, normed, packed, att, out_t, lse = run_attention_forward(place, chunks, head_pieces, layout, heads)
    gain_one, gain_two = gains[:1], gains[1:]
    att_done = lax.all_to_all(att, "seq", split_axis=0, concat_axis=0, tiled=True)
    first = first + [swap(first[0])] + [swap(after(piece, att)) for piece in first[1:]]
    if regular:
        downs = [w_down] + first
    else:
        downs = [lax.all_gather(w_down, "fsdp", axis=0, tiled=True)]
    grad_hidden = run_hidden_grad(place, cot, downs, left, hidden)
    second = second + [swap(second[0])] + [swap(after(piece, att_done, grad_hidden)) for piece in second[1:]]
    att = att_done
    middle, gmid, send, keep, gatt = run_feed_forward(
        place, x, att, cot, gain_two, grad_hidden, w_out, w_in, first, second, hidden
    )
    dout = lax.all_to_all(gatt, "seq", split_axis=0, concat_axis=0, tiled=True)
    reduce = functools.partial(plane_reduce, seq_count=seq_count, fsdp_count=fsdp_count)
    send_other, keep_other = swap(send), swap(keep)
    wide = padded(hidden)
    if regular:
        short = w_in.shape[0] // 8
        in_a, in_b, in_c = run_in_grad(place, send, send_other, hidden)
        in_a = plane_swap(in_a, 1, *counts)
        packed = after(packed, in_b)

    grads, *shares = run_attention_backward(place, dout, packed, out_t, lse, w_heads, layout, heads, regular)
    each = w_qkv.shape[0]
    if regular:
        in_sum = after(added(in_b[0], in_a[1]), grads)
        in_second = plane_swap(in_sum, 0, *counts)
        got, share = swap(shares[0]), shares[1]
        token_sum = added(share[2:], got[2:])
        token_z1 = line_swap(token_sum, 0, seq_count)
        rest_a, rest_b, rest_c = run_rest_grad(place, keep, after(keep_other, in_sum, token_sum), hidden)
        rest_a = plane_swap(rest_a, 1, *counts)
        gw_heads = run_qkv_weight_grad(place, normed, after(grads, rest_b), regular)
        in_parts = [p.reshape(4, short, 2 * hidden) for p in (in_c[0], in_a[0], in_second)]
        in_z1 = line_swap(after(added(*(p[2:] for p in in_parts)), gw_heads[1]), 0, seq_count)
        rest_sum = added(rest_b[0], rest_a[1])
        rest_second = plane_swap(rest_sum, 0, *counts)
        rest_parts = (rest_c[0], rest_a[0], rest_second)
        layer_out = run_layer_result(place, middle, after(keep, rest_sum), downs, left, hidden)
        token_z2 = line_swap(added(share[1], got[1], token_z1[1]), 1, seq_count)
        grad_tokens = run_input_grad(x, gmid, gain_one, [share[0], got[0], token_z1[0], token_z2])
        qkv_a, qkv_b, qkv_c = gw_heads
        qkv_a = plane_swap(after(qkv_a, rest_second), 1, *counts)
        qkv_block = added(*reduce(qkv_a, qkv_b, qkv_c))
        in_z2 = line_swap(added(*(p[1] for p in in_parts), in_z1[1]), 1, seq_count)
        in_block = after(added(*(p[0] for p in in_parts), in_z1[0], in_z2), layer_out)
        rest_z1 = line_swap(after(added(*(p[2:] for p in rest_parts)), token_z2), 0, seq_count)
        rest_z2 = line_swap(after(added(*(p[1] for p in rest_parts), rest_z1[1]), in_z2), 1, seq_count)
        rest_block = added(*(p[0] for p in rest_parts), rest_z1[0], rest_z2)
        in_pieces = line_gather(in_block, seq_count)
        gw_in, sum_in = run_unpack_in(place, in_pieces, w_in)
        rest_pieces = line_gather(rest_block, seq_count, sum_in)
        qkv_pieces = line_gather(after(qkv_block, grad_tokens), seq_count, sum_in)
        gw_qkv, sum_qkv = run_unpack_qkv(place, qkv_pieces, w_qkv)
        gw_out, gw_down = run_unpack_rest(place, rest_pieces, w_out.shape, w_down.shape)
        sum_qkv = sum_qkv[:, 0]
        sum_in = sum_in[:, 0]
    else:
        layer_out = run_layer_result(place, middle, keep, downs, left, hidden)
        gw_heads = run_qkv_weight_grad(place, normed, grads, regular)
        share = lax.psum_scatter(shares[0].astype(F32), "seq", scatter_dimension=0, tiled=False)
        grad_tokens = run_input_grad(x, gmid, gain_one, [share])

        def total(left_rows, right_rows):
            full = lax.dot_general(
                left_rows, right_rows, (((0,), (0,)), ((), ())), preferred_element_type=F32
            )
            return lax.psum(lax.psum_scatter(full, "fsdp", scatter_dimension=0, tiled=True), "seq")

        gw_in = total(send[:, 2 * hidden :], send[:, : 2 * hidden])
        gw_down = total(keep[:, :hidden], cot)
        gw_out = total(keep[:, wide + dim : wide + 2 * dim], keep[:, wide : wide + dim])
        sum_in = jnp.sum(gw_in * w_in.astype(F32), axis=1)
        gw_heads = lax.all_to_all(gw_heads[0].reshape(fsdp_count, each, -1), "fsdp", 0, 0, tiled=True)
        gw_heads = jnp.sum(gw_heads.astype(F32), axis=0).astype(BF16)
        gw_qkv = lax.all_gather(gw_heads, "seq", axis=0, tiled=False).reshape(seq_count, each, 3, width)
        gw_qkv = gw_qkv.transpose(1, 2, 0, 3).reshape(each, 3 * dim).astype(F32)
        sum_qkv = jnp.sum(gw_qkv * w_qkv.astype(F32), axis=1)

    grad_one = sum_qkv / norm_one.astype(F32)
    grad_two = sum_in / norm_two.astype(F32)
    return (layer_out[None], grad_tokens[None], grad_one, gw_qkv, gw_out, grad_two, gw_in, gw_down)


def solution(mesh):
    tokens = P("fsdp", "seq", None)
    rows = P("fsdp", None)
    return jax.shard_map(
        local,
        mesh=mesh,
        in_specs=(tokens, rows, rows, P("fsdp"), rows, rows, P("fsdp"), rows, rows, tokens),
        out_specs=(tokens, tokens, P("fsdp"), rows, rows, P("fsdp"), rows, rows),
        check_vma=False,
    )
```

```python
import functools
import math

import jax
import jax.numpy as jnp
from jax import lax
from jax.experimental import pallas as pl
from jax.experimental.pallas import tpu as pltpu
from jax.sharding import PartitionSpec as P

HD = 64
NORM_EPS = 1e-05
ROPE_BASE = 160000.0
BLOCK = 256
WIDE = 512
LOG2E = math.log2(math.e)
AXES = ("seq", "fsdp")
F32 = jnp.float32
BF16 = jnp.bfloat16
VMEM_LIMIT = 60 * 1024 * 1024


def core_swap(value, seq_count):
    return lax.ppermute(value, "seq", [(i, i ^ 1) for i in range(seq_count)])


def plane_bit(core, phase, levels):
    return (phase + core * (levels // 2)) % levels


def plane_mask(core, key, levels):
    mask = 0
    for phase in range(levels):
        if key >> phase & 1:
            mask |= 1 << plane_bit(core, phase, levels)
    return mask


def plane_swap(value, phase, seq_count, fsdp_count):
    levels = fsdp_count.bit_length() - 1
    pairs = []
    for s in range(seq_count):
        step = 1 << plane_bit(s & 1, phase, levels)
        for f in range(fsdp_count):
            pairs.append((s * fsdp_count + f, s * fsdp_count + (f ^ step)))
    return lax.ppermute(value, AXES, pairs)


def after(value, *others):
    return lax.optimization_barrier((value, *others))[0]


def plane_gather_rest(piece, first, seq_count, fsdp_count, *others):
    pieces = [after(piece, first, *others), after(first, *others)]
    for phase in range(1, fsdp_count.bit_length() - 1):
        pieces = pieces + [plane_swap(p, phase, seq_count, fsdp_count) for p in pieces]
    return [first] + pieces[2:]


def added(*values):
    return sum(v.astype(F32) for v in values).astype(BF16)


def plane_reduce(first, b, c, seq_count, fsdp_count):
    second = plane_swap(added(b[0], first[1]), 0, seq_count, fsdp_count)
    return c[0], first[0], second


def line_swap(value, level, seq_count):
    return lax.ppermute(value, "seq", [(i, i ^ (2 << level)) for i in range(seq_count)])


def mixed_swap(value, level, seq_count):
    return lax.ppermute(value, "seq", [(i, i ^ (2 << (level ^ (i & 1)))) for i in range(seq_count)])


def line_reduce(parts, seq_count):
    got = line_swap(added(*(p[2:] for p in parts)), 0, seq_count)
    last = line_swap(added(*(p[1] for p in parts), got[1]), 1, seq_count)
    return added(*(p[0] for p in parts), got[0], last)


def line_gather(block, seq_count, *others):
    pair = jnp.stack([block, line_swap(block, 1, seq_count)])
    rest = line_swap(pair, 0, seq_count)
    return [pair, rest, core_swap(pair, seq_count), core_swap(after(rest, *others), seq_count)]


def any_spec():
    return pl.BlockSpec(memory_space=pl.ANY)


def vmem_spec():
    return pl.BlockSpec(memory_space=pltpu.VMEM)


def smem_spec():
    return pl.BlockSpec(memory_space=pltpu.SMEM)


def params():
    return pltpu.CompilerParams(vmem_limit_bytes=VMEM_LIMIT)


def cost(flops, moved):
    return pl.CostEstimate(flops=int(flops), bytes_accessed=int(moved), transcendentals=0)


def nt_dot(a, b):
    return lax.dot_general(a, b, (((1,), (1,)), ((), ())), preferred_element_type=F32)


def nn_dot(a, b):
    return jnp.dot(a, b, preferred_element_type=F32)


def own_copy(place_ref, own, full, sems, rows):
    base = pl.multiple_of(place_ref[0] * rows, 16)
    return pltpu.make_async_copy(own, full.at[pl.ds(base, rows), :], sems.at[0])


def row_copies(place_ref, own, mine, others, left, full, sems):
    count = len(mine)
    rows = own.shape[0]
    half = rows // 2
    core = place_ref[2 * count + 1]
    copies = [own_copy(place_ref, own, full, sems, rows)]
    for which, (refs, side) in enumerate(((mine, core), (others, 1 - core))):
        for i, ref in enumerate(refs):
            at = 1 + which * count + i
            base = pl.multiple_of(place_ref[at] * rows + side * half, 16)
            copies.append(
                pltpu.make_async_copy(
                    ref.at[:, pl.ds(left, full.shape[1])], full.at[pl.ds(base, half), :], sems.at[at]
                )
            )
    return copies


def down_blocks(rows, columns, tall):
    whole = rows // tall
    blocks = [(k * tall, 0, tall, columns, 0, k * columns) for k in range(whole)]
    left = rows - whole * tall
    if left:
        blocks += [
            (whole * tall, 128 * q, left, 128, q * left, whole * columns) for q in range(columns // 128)
        ]
    return blocks


def down_width(rows, columns, tall):
    return rows // tall * columns + (128 if rows % tall else 0)


def down_copies(place_ref, own, mine, others, left, full, sems, hidden):
    if not mine:
        return [pltpu.make_async_copy(own, full.at[pl.ds(0, hidden), :], sems.at[0])]
    count = len(mine)
    rows = own.shape[0]
    half = own.shape[1] // 2
    core = place_ref[2 * count + 1]
    blocks = down_blocks(rows, half, mine[0].shape[0])
    copies = [own_copy(place_ref, own, full, sems, rows)]
    for which, (refs, side) in enumerate(((mine, core), (others, 1 - core))):
        for i, ref in enumerate(refs):
            at = 1 + which * count + i
            side_at = pl.multiple_of(side * half, 128)
            for k, (row, column, tall, wide, packed_row, packed_column) in enumerate(blocks):
                base = pl.multiple_of(place_ref[at] * rows + row, 16)
                copies.append(
                    pltpu.make_async_copy(
                        ref.at[pl.ds(packed_row, tall), pl.ds(left + packed_column, wide)],
                        full.at[pl.ds(base, tall), pl.ds(pl.multiple_of(side_at + column, 128), wide)],
                        sems.at[1 + (at - 1) * len(blocks) + k],
                    )
                )
    return copies


def pack_pieces(place_ref, in_ref, out_ref, down_ref, first_ref, second_ref, sems):
    half = in_ref.shape[0] // 2
    core = place_ref[place_ref.shape[0] - 2]
    base = pl.multiple_of(core * half, 16)
    also = out_ref.shape[1]
    copies = [
        pltpu.make_async_copy(
            out_ref.at[pl.ds(base, half), :], first_ref.at[:, pl.ds(0, also)], sems.at[0]
        ),
        pltpu.make_async_copy(in_ref.at[pl.ds(base, half), :], second_ref, sems.at[1]),
    ]
    if first_ref.shape[1] > also:
        columns = down_ref.shape[1] // 2
        side = pl.multiple_of(core * columns, 128)
        blocks = down_blocks(down_ref.shape[0], columns, half)
        for k, (row, column, tall, part, packed_row, packed_column) in enumerate(blocks):
            copies.append(
                pltpu.make_async_copy(
                    down_ref.at[pl.ds(row, tall), pl.ds(pl.multiple_of(side + column, 128), part)],
                    first_ref.at[pl.ds(packed_row, tall), pl.ds(also + packed_column, part)],
                    sems.at[2 + k],
                )
            )
    for copy in copies:
        copy.start()
    for copy in copies:
        copy.wait()


def run_pack_pieces(place, w_in, w_out, w_down, regular):
    half = w_in.shape[0] // 2
    down = (w_down.shape[0], w_down.shape[1] // 2, half)
    blocks = len(down_blocks(*down)) if regular else 0
    wide = w_out.shape[1] + (down_width(*down) if regular else 0)
    return pl.pallas_call(
        pack_pieces,
        name="pack_pieces",
        out_shape=(
            jax.ShapeDtypeStruct((half, wide), BF16),
            jax.ShapeDtypeStruct((half, w_in.shape[1]), BF16),
        ),
        in_specs=[smem_spec()] + [any_spec()] * 3,
        out_specs=[vmem_spec()] * 2,
        scratch_shapes=[pltpu.SemaphoreType.DMA((2 + blocks,))],
        compiler_params=params(),
        cost_estimate=cost(1e6, 5e6),
    )(place, w_in, w_out, w_down)


def attention_forward(
    seq_count, heads, group, low_ref, high_ref, place_ref, order_ref, start_ref, end_ref,
    cos_ref, sin_ref, *refs,
):
    x_hbm, refs = (refs[:1], refs[1:]) if len(refs[0].shape) == 3 else (refs[:seq_count], refs[seq_count:])
    pieces, refs = refs[:-15], refs[-15:]
    gains_ref, w_ref, normed_hbm, packed_ref, att_ref, out_ref, lse_ref = refs[:7]
    x_ref, normed_ref, qkv_t, k_rows, o_rows, scores_ref, x_sems, normed_sems = refs[7:]
    width = heads * HD
    rows = group // seq_count
    blocks = group // BLOCK
    if len(x_hbm) == 1:
        chunks = list(range(seq_count))
        x_hbm = [x_hbm[0].at[i] for i in chunks]
    else:
        core, z = place_ref[7], place_ref[8]
        chunks = [(z ^ k) * 2 + side for side in (core, 1 - core) for k in block_order(side)]
    fetches = [pltpu.make_async_copy(x_hbm[i], x_ref.at[i], x_sems.at[i]) for i in range(seq_count)]
    stores = [
        pltpu.make_async_copy(normed_ref.at[i], normed_hbm.at[chunks[i]], normed_sems.at[i])
        for i in range(seq_count)
    ]
    for fetch in fetches:
        fetch.start()
    if len(pieces) == 2:
        w_ref[...] = pieces[0][...]
        gains_ref[...] = pieces[1][...]
    else:
        tall = w_ref.shape[0] // len(pieces)
        for key, piece in enumerate(pieces):
            base = pl.multiple_of(place_ref[key] * tall, 128)
            w_ref[pl.ds(base, tall), :] = piece[:tall]
            gains_ref[:, pl.ds(base, tall)] = piece[tall : tall + 2, :tall].astype(F32)
    gain_ref = gains_ref.at[pl.ds(0, 1), :]

    def project(i):
        x = x_ref[i].astype(F32)
        center = x - jnp.mean(x, axis=-1, keepdims=True)
        spread = jnp.mean(center * center, axis=-1, keepdims=True)
        normed = (center * lax.rsqrt(spread + NORM_EPS) * gain_ref[...]).astype(BF16)
        normed_ref[i] = normed
        qkv = nn_dot(normed, w_ref[...]).astype(BF16)
        qkv_t[chunks[i]] = qkv.T

    for i in range(seq_count):
        fetches[i].wait()
        project(i)
        stores[i].start()

    def pack(i, carry):
        at = pl.ds(pl.multiple_of(i * BLOCK, BLOCK), BLOCK)
        order = order_ref[:, at]
        total = jnp.zeros((3 * width, BLOCK), F32)
        for s in range(seq_count):
            here = lax.broadcasted_iota(jnp.int32, (rows, BLOCK), 0) + s * rows
            hot = jnp.where(here == order, 1.0, 0.0).astype(BF16)
            total = total + nn_dot(qkv_t[s], hot)
        cos = cos_ref[:, at]
        sin = sin_ref[:, at]
        half = HD // 2
        for part in range(2):
            for h in range(heads):
                base = part * width + h * HD
                first = total[base : base + half]
                second = total[base + half : base + HD]
                turned = jnp.concatenate(
                    [first * cos - second * sin, second * cos + first * sin], axis=0
                ).astype(BF16)
                packed_ref[base : base + HD, at] = turned
                if part == 1:
                    k_rows[h, at, :] = turned.T
        packed_ref[2 * width :, at] = total[2 * width :].astype(BF16)
        return carry

    lax.fori_loop(0, blocks, pack, 0)
    scale = HD**-0.5 * LOG2E

    def attend(i, carry):
        at = pl.ds(pl.multiple_of(i * WIDE, WIDE), WIDE)
        start = start_ref[:, at]
        end = end_ref[:, at]
        queries = [packed_ref[h * HD : (h + 1) * HD, at] for h in range(heads)]

        low, high = low_ref[i], high_ref[i]

        def score(j, tops):
            there = pl.ds(pl.multiple_of(j * BLOCK, BLOCK), BLOCK)
            where = lax.broadcasted_iota(jnp.int32, (BLOCK, WIDE), 0) + j * BLOCK
            same = jnp.logical_and(where >= start, where < end)
            following = []
            for h in range(heads):
                scores = jnp.where(same, nn_dot(k_rows[h, there, :], queries[h]) * scale, -1e30)
                scores_ref[j, h] = scores
                following.append(jnp.maximum(tops[h], jnp.max(scores.reshape(-1, 8, WIDE), axis=0)))
            return tuple(following)

        tops = lax.fori_loop(low, high, score, tuple(jnp.full((8, WIDE), -1e30, F32) for _ in range(heads)))
        tops = [jnp.max(top, axis=0, keepdims=True) for top in tops]

        def weigh(j, state):
            there = pl.ds(pl.multiple_of(j * BLOCK, BLOCK), BLOCK)
            following = []
            for h in range(heads):
                total, acc = state[h]
                probs = jnp.exp2(scores_ref[j, h] - tops[h])
                total = total + jnp.sum(probs.reshape(-1, 8, WIDE), axis=0)
                base = 2 * width + h * HD
                acc = acc + nn_dot(packed_ref[base : base + HD, there], probs.astype(BF16))
                following.append((total, acc))
            return tuple(following)

        first = tuple((jnp.zeros((8, WIDE), F32), jnp.zeros((HD, WIDE), F32)) for _ in range(heads))
        last = lax.fori_loop(low, high, weigh, first)
        outs = []
        for h in range(heads):
            total, acc = last[h]
            total = jnp.sum(total, axis=0, keepdims=True)
            out = acc / total
            out_ref[h * HD : (h + 1) * HD, at] = out
            lse_ref[h : h + 1, at] = tops[h] + jnp.log2(total)
            outs.append(out)
        o_rows[at, :] = jnp.concatenate(outs, axis=0).astype(BF16).T
        return carry

    lax.fori_loop(0, group // WIDE, attend, 0)

    def arrive(i, carry):
        here = lax.broadcasted_iota(jnp.int32, (rows, group), 0) + i * rows
        hot = jnp.where(here == order_ref[...], 1.0, 0.0).astype(BF16)
        att_ref[i] = nn_dot(hot, o_rows[...]).astype(BF16)
        return carry

    lax.fori_loop(0, seq_count, arrive, 0)
    for store in stores:
        store.wait()


def run_attention_forward(place, chunks, pieces, layout, heads):
    rows, dim = chunks[0].shape[-2:]
    group = layout[2].shape[1]
    seq_count = group // rows
    width = heads * HD
    (low, high), _, order, start, end, cos, sin = layout
    return pl.pallas_call(
        functools.partial(attention_forward, seq_count, heads, group),
        name="attention_forward",
        out_shape=(
            jax.ShapeDtypeStruct((2, dim), F32),
            jax.ShapeDtypeStruct((dim, 3 * width), BF16),
            jax.ShapeDtypeStruct((seq_count, rows, dim), BF16),
            jax.ShapeDtypeStruct((3 * width, group), BF16),
            jax.ShapeDtypeStruct((seq_count, rows, width), BF16),
            jax.ShapeDtypeStruct((width, group), F32),
            jax.ShapeDtypeStruct((heads, group), F32),
        ),
        in_specs=[smem_spec()] * 3 + [vmem_spec()] * 5 + [any_spec()] * len(chunks) + [vmem_spec()] * len(pieces),
        out_specs=[vmem_spec()] * 2 + [any_spec()] + [vmem_spec()] * 4,
        scratch_shapes=[
            pltpu.VMEM((seq_count, rows, dim), BF16),
            pltpu.VMEM((seq_count, rows, dim), BF16),
            pltpu.VMEM((seq_count, 3 * width, rows), BF16),
            pltpu.VMEM((heads, group, HD), BF16),
            pltpu.VMEM((group, width), BF16),
            pltpu.VMEM((group // BLOCK, heads, BLOCK, WIDE), F32),
            pltpu.SemaphoreType.DMA((seq_count,)),
            pltpu.SemaphoreType.DMA((seq_count,)),
        ],
        compiler_params=params(),
        cost_estimate=cost(24e9, 20e6),
    )(low, high, place, order, start, end, cos, sin, *chunks, *pieces)


def attention_backward(
    seq_count, heads, group, low_ref, high_ref, place_ref, dout_ref, packed_ref, out_ref, lse_ref, order_ref,
    start_ref, end_ref, cos_ref, sin_ref, w_ref, grad_hbm, *refs,
):
    results, refs = refs[:-13], refs[-13:]
    dout_t, dpack_t, drows, qrows, krows, vrows, delta_ref, dq_t, grows = refs[:9]
    grad_ref, share_ref, grad_sems, share_sems = refs[9:]
    width = heads * HD
    rows = group // seq_count
    blocks = group // BLOCK
    scale = HD**-0.5

    def turn(i, carry):
        dout_t[i] = dout_ref[i].T
        return carry

    lax.fori_loop(0, seq_count, turn, 0)

    def pack(i, carry):
        at = pl.ds(pl.multiple_of(i * BLOCK, BLOCK), BLOCK)
        order = order_ref[:, at]
        total = jnp.zeros((width, BLOCK), F32)
        for s in range(seq_count):
            here = lax.broadcasted_iota(jnp.int32, (rows, BLOCK), 0) + s * rows
            hot = jnp.where(here == order, 1.0, 0.0).astype(BF16)
            total = total + nn_dot(dout_t[s], hot)
        dpack_t[:, at] = total.astype(BF16)
        for h in range(heads):
            mine = total[h * HD : (h + 1) * HD]
            delta_ref[h : h + 1, at] = jnp.sum(
                mine * out_ref[h * HD : (h + 1) * HD, at], axis=0, keepdims=True
            )
            drows[h, at, :] = mine.T.astype(BF16)
            for part, ref in enumerate((qrows, krows, vrows)):
                base = part * width + h * HD
                ref[h, at, :] = packed_ref[base : base + HD, at].T
        dq_t[:, at] = jnp.zeros((width, BLOCK), F32)
        return carry

    lax.fori_loop(0, blocks, pack, 0)

    def keys(j, carry):
        there = pl.ds(pl.multiple_of(j * BLOCK, BLOCK), BLOCK)
        where = lax.broadcasted_iota(jnp.int32, (BLOCK, WIDE), 0) + j * BLOCK

        def queries(i, state):
            at = pl.ds(pl.multiple_of(i * WIDE, WIDE), WIDE)
            same = jnp.logical_and(where >= start_ref[:, at], where < end_ref[:, at])
            following = []
            for h in range(heads):
                dk, dv = state[h]
                base = h * HD
                key_rows = krows[h, there, :]
                query_t = packed_ref[base : base + HD, at]
                scores = nn_dot(key_rows, query_t) * (scale * LOG2E)
                scores = jnp.where(same, scores, -1e30)
                probs = jnp.exp2(scores - lse_ref[h : h + 1, at])
                dprobs = nn_dot(vrows[h, there, :], dpack_t[base : base + HD, at])
                raw = (probs * (dprobs - delta_ref[h : h + 1, at]) * scale).astype(BF16)
                dv = dv + nn_dot(probs.astype(BF16), drows[h, at, :])
                dk = dk + nn_dot(raw, qrows[h, at, :])
                key_t = packed_ref[width + base : width + base + HD, there]
                dq_t[base : base + HD, at] += nn_dot(key_t, raw)
                following.append((dk, dv))
            return tuple(following)

        zero = jnp.zeros((BLOCK, HD), F32)
        last = lax.fori_loop(low_ref[j], high_ref[j], queries, tuple((zero, zero) for _ in range(heads)))
        cos = cos_ref[:, there]
        sin = sin_ref[:, there]
        half = HD // 2
        turned = []
        for h in range(heads):
            dk_t = last[h][0].T
            first, second = dk_t[:half], dk_t[half:]
            turned.append(first * cos + second * sin)
            turned.append(second * cos - first * sin)
        grows[there, width : 2 * width] = jnp.concatenate(turned, axis=0).T.astype(BF16)
        grows[there, 2 * width :] = jnp.concatenate([last[h][1] for h in range(heads)], axis=1).astype(BF16)
        return carry

    lax.fori_loop(0, blocks, keys, 0)

    def finish(i, carry):
        at = pl.ds(pl.multiple_of(i * BLOCK, BLOCK), BLOCK)
        cos = cos_ref[:, at]
        sin = sin_ref[:, at]
        half = HD // 2
        turned = []
        for h in range(heads):
            first = dq_t[h * HD : h * HD + half, at]
            second = dq_t[h * HD + half : (h + 1) * HD, at]
            turned.append(first * cos + second * sin)
            turned.append(second * cos - first * sin)
        grows[at, :width] = jnp.concatenate(turned, axis=0).T.astype(BF16)
        return carry

    lax.fori_loop(0, blocks, finish, 0)

    def arrive(i):
        here = lax.broadcasted_iota(jnp.int32, (rows, group), 0) + i * rows
        hot = jnp.where(here == order_ref[...], 1.0, 0.0).astype(BF16)
        grad = nn_dot(hot, grows[...]).astype(BF16)
        grad_ref[i] = grad
        grad_out(i).start()
        return nt_dot(grad, w_ref[...]).astype(BF16)

    def grad_out(i):
        return pltpu.make_async_copy(grad_ref.at[i], grad_hbm.at[i], grad_sems.at[i])

    def share_out(result, first, j):
        return pltpu.make_async_copy(share_ref.at[first + j], result.at[j], share_sems.at[first + j])

    sides = [0] if len(results) == 1 else [1 - place_ref[7], place_ref[7]]
    count = seq_count // len(results)
    for which, (side, result) in enumerate(zip(sides, results)):
        first = which * count

        def each(j, carry, side=side, result=result, first=first):
            if len(results) == 1:
                source = j
            else:
                k = jnp.where(j == 1, 2 - side, jnp.where(j == 2, 1 + side, j))
                source = (place_ref[8] ^ k) * 2 + side
            share_ref[first + j] = arrive(source)
            share_out(result, first, j).start()
            return carry

        lax.fori_loop(0, count, each, 0)
    for i in range(seq_count):
        grad_out(i).wait()
    for which, result in enumerate(results):
        for j in range(count):
            share_out(result, which * count, j).wait()


def run_attention_backward(place, dout, packed, out_t, lse, w_heads, layout, heads, regular):
    seq_count, rows, width = dout.shape
    group = seq_count * rows
    dim = w_heads.shape[0]
    _, (low, high), order, start, end, cos, sin = layout
    shares = [seq_count // 2] * 2 if regular else [seq_count]
    return pl.pallas_call(
        functools.partial(attention_backward, seq_count, heads, group),
        name="attention_backward",
        out_shape=[jax.ShapeDtypeStruct((seq_count, rows, 3 * width), BF16)]
        + [jax.ShapeDtypeStruct((share, rows, dim), BF16) for share in shares],
        in_specs=[smem_spec()] * 3 + [vmem_spec()] * 10,
        out_specs=[any_spec()] * (1 + len(shares)),
        scratch_shapes=[
            pltpu.VMEM((seq_count, width, rows), BF16),
            pltpu.VMEM((width, group), BF16),
            pltpu.VMEM((heads, group, HD), BF16),
            pltpu.VMEM((heads, group, HD), BF16),
            pltpu.VMEM((heads, group, HD), BF16),
            pltpu.VMEM((heads, group, HD), BF16),
            pltpu.VMEM((heads, group), F32),
            pltpu.VMEM((width, group), F32),
            pltpu.VMEM((group, 3 * width), BF16),
            pltpu.VMEM((seq_count, rows, 3 * width), BF16),
            pltpu.VMEM((seq_count, rows, dim), BF16),
            pltpu.SemaphoreType.DMA((seq_count,)),
            pltpu.SemaphoreType.DMA((seq_count,)),
        ],
        compiler_params=params(),
        cost_estimate=cost(33e9, 15e6),
    )(low, high, place, dout, packed, out_t, lse, order, start, end, cos, sin, w_heads)


def qkv_weight_grad(seq_count, place_ref, normed_ref, grad_ref, *refs):
    outs, (total, turned) = refs[:-2], refs[-2:]
    total[...] = jnp.zeros_like(total)

    def step(i, carry):
        total[...] += nn_dot(grad_ref[i].T, normed_ref[i])
        return carry

    lax.fori_loop(0, seq_count, step, 0)
    if len(outs) == 1:
        outs[0][...] = total[...].T.astype(BF16)
        return
    turned[...] = total[...].T
    rows = outs[0].shape[1]
    for ref, keys in zip(outs, ((2, 3), (1,), (0,))):
        for at, key in enumerate(keys):
            base = pl.multiple_of(place_ref[key] * rows, 16)
            ref[at] = turned[pl.ds(base, rows), :].astype(BF16)


def run_qkv_weight_grad(place, normed, grad, regular):
    seq_count, rows, dim = normed.shape
    width = grad.shape[-1]
    if regular:
        outs = tuple(jax.ShapeDtypeStruct((n, dim // 4, width), BF16) for n in (2, 1, 1))
    else:
        outs = (jax.ShapeDtypeStruct((dim, width), BF16),)
    return pl.pallas_call(
        functools.partial(qkv_weight_grad, seq_count),
        name="qkv_weight_grad",
        out_shape=outs,
        in_specs=[smem_spec()] + [vmem_spec()] * 2,
        out_specs=[vmem_spec()] * len(outs),
        scratch_shapes=[pltpu.VMEM((width, dim), F32), pltpu.VMEM((dim, width), F32)],
        compiler_params=params(),
        cost_estimate=cost(3e9, 6e6),
    )(place, normed, grad)


def padded(hidden):
    return -(-hidden // 128) * 128


def load_down(place_ref, refs, count, hidden, left, full, sems):
    copies = down_copies(place_ref, refs[0], refs[1 : 1 + count], refs[1 + count :], left, full, sems, hidden)
    for copy in copies:
        copy.start()
    tail = padded(hidden) - hidden
    if tail:
        full[pl.ds(hidden, tail), :] = jnp.zeros((tail, full.shape[1]), BF16)
    for copy in copies:
        copy.wait()


def down_semaphores(downs):
    if len(downs) == 1:
        return pltpu.SemaphoreType.DMA((1,))
    blocks = len(down_blocks(downs[0].shape[0], downs[0].shape[1] // 2, downs[1].shape[0]))
    return pltpu.SemaphoreType.DMA((1 + (len(downs) - 1) * blocks,))


def hidden_grad(hidden, left, place_ref, cot_ref, *refs):
    downs, (out_ref, full, sems) = refs[:-3], refs[-3:]
    load_down(place_ref, downs, (len(downs) - 1) // 2, hidden, left, full, sems)
    cot = cot_ref[...]
    tiles = padded(hidden) // 128
    wide = 128 * max(n for n in (1, 2, 3) if tiles % n == 0)

    def step(i, carry):
        at = pl.multiple_of(i * wide, 128)
        out_ref[:, pl.ds(at, wide)] = nt_dot(cot, full[pl.ds(at, wide), :])
        return carry

    lax.fori_loop(0, padded(hidden) // wide, step, 0)


def run_hidden_grad(place, cot, downs, left, hidden):
    rows, dim = cot.shape
    return pl.pallas_call(
        functools.partial(hidden_grad, hidden, left),
        name="hidden_grad",
        out_shape=jax.ShapeDtypeStruct((rows, padded(hidden)), F32),
        in_specs=[smem_spec(), vmem_spec()] + [any_spec()] * len(downs),
        out_specs=vmem_spec(),
        scratch_shapes=[pltpu.VMEM((padded(hidden), dim), BF16), down_semaphores(downs)],
        compiler_params=params(),
        cost_estimate=cost(4e9, 9e6),
    )(place, cot, *downs)


def layer_result(hidden, left, place_ref, mid_ref, keep_ref, *refs):
    downs, (out_ref, full, sems) = refs[:-3], refs[-3:]
    load_down(place_ref, downs, (len(downs) - 1) // 2, hidden, left, full, sems)
    wide = padded(hidden)

    def step(i, carry):
        at = pl.ds(pl.multiple_of(i * 256, 256), 256)
        out_ref[:, at] = (mid_ref[:, at] + nn_dot(keep_ref[:, :wide], full[:, at])).astype(BF16)
        return carry

    lax.fori_loop(0, out_ref.shape[1] // 256, step, 0)


def run_layer_result(place, middle, keep, downs, left, hidden):
    rows, dim = middle.shape
    return pl.pallas_call(
        functools.partial(layer_result, hidden, left),
        name="layer_result",
        out_shape=jax.ShapeDtypeStruct((rows, dim), BF16),
        in_specs=[smem_spec()] + [vmem_spec()] * 2 + [any_spec()] * len(downs),
        out_specs=vmem_spec(),
        scratch_shapes=[pltpu.VMEM((padded(hidden), dim), BF16), down_semaphores(downs)],
        compiler_params=params(),
        cost_estimate=cost(4e9, 9e6),
    )(place, middle, keep, *downs)


def feed_forward(
    count, hidden, heads_width, place_ref, x_ref, att_ref, cot_ref, gain_ref, gh_hbm, *refs
):
    out_own, in_own, refs = refs[0], refs[1], refs[2:]
    first, others, refs = refs[:count], refs[count : 2 * count], refs[2 * count :]
    second, second_others, refs = refs[:count], refs[count : 2 * count], refs[2 * count :]
    mid_ref, gmid_ref, send_hbm, keep_hbm, ga_ref = refs[:5]
    wo, wi, both, early, late, send_ref, keep_ref, gh_ref, sem_o, sem_i, sems = refs[5:]
    fetch = pltpu.make_async_copy(gh_hbm, gh_ref, sems.at[0])
    send_out = pltpu.make_async_copy(send_ref, send_hbm, sems.at[1])
    keep_out = pltpu.make_async_copy(keep_ref, keep_hbm, sems.at[2])
    dim = x_ref.shape[1]
    wide_hidden = padded(hidden)
    nt_ref = send_ref.at[:, pl.ds(2 * hidden, dim)]
    gboth_ref = send_ref
    hid_ref = keep_ref
    gbr_ref = keep_ref.at[:, pl.ds(wide_hidden, dim)]
    att_all_ref = keep_ref.at[:, pl.ds(wide_hidden + dim, dim)]
    keep_ref[:, pl.ds(wide_hidden + 2 * dim, dim)] = cot_ref[...]
    copies_o = row_copies(place_ref, out_own, first, others, 0, wo, sem_o)
    copies_i = row_copies(place_ref, in_own, second, second_others, 0, wi, sem_i)
    for copy in copies_o:
        copy.start()
    for copy in copies_i:
        copy.start()
    fetch.start()
    att = jnp.concatenate([att_ref[s] for s in range(att_ref.shape[0])], axis=1)
    att_all_ref[...] = att
    for copy in copies_o:
        copy.wait()

    def branch(i, carry):
        at = pl.ds(pl.multiple_of(i * 256, 256), 256)
        mid_ref[:, at] = x_ref[:, at].astype(F32) + nn_dot(att_all_ref[...], wo[:, at])
        return carry

    lax.fori_loop(0, dim // 256, branch, 0)
    middle = mid_ref[...]
    center = middle - jnp.mean(middle, axis=-1, keepdims=True)
    spread = jnp.mean(center * center, axis=-1, keepdims=True)
    scale = lax.rsqrt(spread + NORM_EPS)
    nt_ref[...] = (center * scale * gain_ref[...]).astype(BF16)
    for copy in copies_i:
        copy.wait()
    fetch.wait()
    wide = 2 * hidden // 128

    def expand(i, carry):
        at = pl.ds(pl.multiple_of(i * 256, 256), 256)
        both[:, at] = nn_dot(nt_ref[...], wi[:, at])
        return carry

    lax.fori_loop(0, wide // 2, expand, 0)
    if wide % 2:
        both[:, pl.ds(128 * (wide - 1), 128)] = nn_dot(nt_ref[...], wi[:, pl.ds(128 * (wide - 1), 128)])
    both[:, pl.ds(128 * wide, 128)] = jnp.zeros((both.shape[0], 128), F32)
    tiles = padded(hidden) // 128
    whole = hidden // 128
    lanes = lax.broadcasted_iota(jnp.int32, (both.shape[0], 128), 1)
    shift = hidden % 128

    def tile(i):
        return pl.ds(pl.multiple_of(i * 128, 128), 128)

    def gates(i):
        a = both[:, tile(i)]
        if shift:
            left = pltpu.roll(both[:, tile(whole + i)], 128 - shift, 1)
            right = pltpu.roll(both[:, tile(whole + i + 1)], 128 - shift, 1)
            b = jnp.where(lanes < 128 - shift, left, right)
        else:
            b = both[:, tile(whole + i)]
        gh = gh_ref[:, tile(i)]
        phi = 0.5 * (1.0 + lax.erf(a * (0.5**0.5)))
        gelu = a * phi
        slope = phi + a * ((0.5 / math.pi) ** 0.5 * jnp.exp(-0.5 * a * a))
        hid_ref[:, tile(i)] = (gelu * b).astype(BF16)
        return gh * b * slope, gh * gelu

    if shift:
        first_a, first_b = gates(0)
        gboth_ref[:, tile(0)] = first_a.astype(BF16)
        early[...] = pltpu.roll(first_b, shift, 1)
        late[...] = early[...]

        def inner(i, carry):
            ga, gb = gates(i)
            turned = pltpu.roll(gb, shift, 1)
            gboth_ref[:, tile(i)] = ga.astype(BF16)
            gboth_ref[:, tile(whole + i)] = jnp.where(lanes < shift, late[...], turned).astype(BF16)
            late[...] = turned
            return carry

        lax.fori_loop(1, tiles - 1, inner, 0)
        ga, gb = gates(tiles - 1)
        turned = pltpu.roll(gb, shift, 1)
        gboth_ref[:, tile(whole)] = jnp.where(lanes < shift, ga, early[...]).astype(BF16)
        gboth_ref[:, tile(2 * whole)] = jnp.where(lanes < shift, late[...], turned).astype(BF16)
    else:

        def inner(i, carry):
            ga, gb = gates(i)
            gboth_ref[:, tile(i)] = ga.astype(BF16)
            gboth_ref[:, tile(whole + i)] = gb.astype(BF16)
            return carry

        lax.fori_loop(0, tiles, inner, 0)

    send_out.start()

    def back(i, carry):
        at = pl.multiple_of(i * 256, 256)
        both[:, pl.ds(at, 256)] = nt_dot(gboth_ref[:, : 2 * hidden], wi[pl.ds(at, 256), :])
        return carry

    lax.fori_loop(0, dim // 256, back, 0)
    middle = mid_ref[...]
    center = middle - jnp.mean(middle, axis=-1, keepdims=True)
    spread = jnp.mean(center * center, axis=-1, keepdims=True)
    scale = lax.rsqrt(spread + NORM_EPS)
    normal = center * scale
    e = both[:, pl.ds(0, dim)] * gain_ref[...]
    pull = e - jnp.mean(e, axis=-1, keepdims=True) - normal * jnp.mean(e * normal, axis=-1, keepdims=True)
    gmid = cot_ref[...].astype(F32) + scale * pull
    gmid_ref[...] = gmid
    gbr_ref[...] = gmid.astype(BF16)
    keep_out.start()

    def spread_out(i, carry):
        at = pl.multiple_of(i * 256, 256)
        both[:, pl.ds(at, 256)] = nt_dot(gbr_ref[...], wo[pl.ds(at, 256), :])
        return carry

    lax.fori_loop(0, dim // 256, spread_out, 0)
    for s in range(att_ref.shape[0]):
        ga_ref[s] = both[:, s * heads_width : (s + 1) * heads_width].astype(BF16)
    send_out.wait()
    keep_out.wait()


def run_feed_forward(place, x, att, cot, gain, grad_hidden, w_out, w_in, first, second, hidden):
    rows, dim = x.shape
    seq_count, _, heads_width = att.shape
    count = len(first) // 2
    return pl.pallas_call(
        functools.partial(feed_forward, count, hidden, heads_width),
        name="feed_forward",
        out_shape=(
            jax.ShapeDtypeStruct((rows, dim), F32),
            jax.ShapeDtypeStruct((rows, dim), F32),
            jax.ShapeDtypeStruct((rows, 2 * hidden + dim), BF16),
            jax.ShapeDtypeStruct((rows, padded(hidden) + 3 * dim), BF16),
            jax.ShapeDtypeStruct((seq_count, rows, heads_width), BF16),
        ),
        in_specs=[smem_spec()] + [vmem_spec()] * 4 + [any_spec()] * (3 + 4 * count),
        out_specs=[vmem_spec()] * 2 + [any_spec()] * 2 + [vmem_spec()],
        scratch_shapes=[
            pltpu.VMEM((dim, dim), BF16),
            pltpu.VMEM((dim, 2 * hidden), BF16),
            pltpu.VMEM((rows, 2 * hidden + 128), F32),
            pltpu.VMEM((rows, 128), F32),
            pltpu.VMEM((rows, 128), F32),
            pltpu.VMEM((rows, 2 * hidden + dim), BF16),
            pltpu.VMEM((rows, padded(hidden) + 3 * dim), BF16),
            pltpu.VMEM((rows, padded(hidden)), F32),
            pltpu.SemaphoreType.DMA((2 * count + 1,)),
            pltpu.SemaphoreType.DMA((2 * count + 1,)),
            pltpu.SemaphoreType.DMA((3,)),
        ],
        compiler_params=params(),
        cost_estimate=cost(16e9, 24e6),
    )(place, x, att, cot, gain, grad_hidden, w_out, w_in, *first, *second)


ORDER = (0, 2, 1, 3)


def block_order(core):
    return (0, 2 - core, 1 + core, 3)


def in_grad(hidden, wide, place_ref, send_ref, other_ref, a_ref, b_ref, c_ref, turned, picked):
    tokens = send_ref.shape[0]
    rows = turned.shape[0] // 4
    half, short = rows // 2, rows // 8

    @pl.when(pl.program_id(0) == 0)
    def _():
        turned[:, :tokens] = send_ref[:, 2 * hidden :].T
        turned[:, tokens:] = other_ref[:, 2 * hidden :].T
        core, z = place_ref[7], place_ref[8]
        for at, key in enumerate((2, 3, 1, 0)):
            for j, k in enumerate(ORDER):
                base = pl.multiple_of(place_ref[key] * rows + core * half + (z ^ k) * short, 16)
                to = at * half + j * short
                picked[to : to + short, :] = turned[pl.ds(base, short), :]

    at = pl.ds(pl.multiple_of(pl.program_id(0) * wide, 128), wide)
    right = jnp.concatenate([send_ref[:, at], other_ref[:, at]], axis=0)
    result = nn_dot(picked[...], right).astype(BF16)
    a_ref[0] = result[:half]
    a_ref[1] = result[half : 2 * half]
    b_ref[0] = result[2 * half : 3 * half]
    c_ref[0] = result[3 * half :]


def run_in_grad(place, send, other, hidden):
    tokens = send.shape[0]
    features = send.shape[1] - 2 * hidden
    columns = 2 * hidden
    half = features // 8
    wide = 896
    whole = pl.BlockSpec(send.shape, lambda i: (0, 0))
    return pl.pallas_call(
        functools.partial(in_grad, hidden, wide),
        name="in_grad",
        out_shape=tuple(jax.ShapeDtypeStruct((n, half, columns), BF16) for n in (2, 1, 1)),
        grid=(pl.cdiv(columns, wide),),
        in_specs=[smem_spec(), whole, whole],
        out_specs=[pl.BlockSpec((n, half, wide), lambda i: (0, 0, i)) for n in (2, 1, 1)],
        scratch_shapes=[
            pltpu.VMEM((features, 2 * tokens), BF16),
            pltpu.VMEM((features // 2, 2 * tokens), BF16),
        ],
        compiler_params=params(),
        cost_estimate=cost(2.0 * 2 * tokens * features * columns, 4 * tokens * columns + features * columns),
    )(place, send, other)


def rest_grad(hidden, place_ref, keep_ref, other_ref, a_ref, b_ref, c_ref, turned, picked):
    tokens = keep_ref.shape[0]
    wide = padded(hidden)
    dim = (keep_ref.shape[1] - wide) // 3
    half = dim // 2
    down_rows = hidden // 4
    short = dim // 32
    core, z = place_ref[7], place_ref[8]
    at = pl.program_id(0)

    @pl.when(at == 0)
    def _():
        turned[:wide, :tokens] = keep_ref[:, :wide].T
        turned[:wide, tokens:] = other_ref[:, :wide].T
        turned[wide:, :tokens] = keep_ref[:, wide + dim : wide + 2 * dim].T
        turned[wide:, tokens:] = other_ref[:, wide + dim : wide + 2 * dim].T
        for j, k in enumerate(ORDER):
            left = pl.ds(pl.multiple_of(wide + 2 * dim + core * half + (z ^ k) * 128, 128), 128)
            picked[:tokens, j * 128 : (j + 1) * 128] = keep_ref[:, left]
            picked[tokens:, j * 128 : (j + 1) * 128] = other_ref[:, left]
        picked[:tokens, half:] = keep_ref[:, wide : wide + dim]
        picked[tokens:, half:] = other_ref[:, wide : wide + dim]

    owner = place_ref[jnp.where(at < 2, at + 2, 3 - at)]
    base = pl.multiple_of(owner * down_rows, 16)
    down = nn_dot(turned[pl.ds(base, down_rows), :], picked[:, :half]).astype(BF16)
    left = []
    for k in ORDER:
        base = pl.multiple_of(wide + owner * 8 * short + core * 4 * short + (z ^ k) * short, 16)
        left.append(turned[pl.ds(base, short), :])
    out = nn_dot(jnp.concatenate(left, axis=0), picked[:, half:]).astype(BF16)
    first = dim // 128 * short

    def store(ref):
        for j in range(4):
            for t in range(dim // 128):
                ref[0, j, t * short : (t + 1) * short, :] = out[
                    j * short : (j + 1) * short, t * 128 : (t + 1) * 128
                ]
            ref[0, j, first:, :] = down[:, j * 128 : (j + 1) * 128]

    pl.when(at < 2)(lambda: store(a_ref))
    pl.when(at == 2)(lambda: store(b_ref))
    pl.when(at == 3)(lambda: store(c_ref))


def run_rest_grad(place, keep, other, hidden):
    tokens = keep.shape[0]
    wide = padded(hidden)
    dim = (keep.shape[1] - wide) // 3
    tall = dim // 128 * (dim // 32) + hidden // 4
    whole = pl.BlockSpec(keep.shape, lambda i: (0, 0))
    return pl.pallas_call(
        functools.partial(rest_grad, hidden),
        name="rest_grad",
        out_shape=tuple(jax.ShapeDtypeStruct((n, 4, tall, 128), BF16) for n in (2, 1, 1)),
        grid=(4,),
        in_specs=[smem_spec(), whole, whole],
        out_specs=[
            pl.BlockSpec((1, 4, tall, 128), lambda i: (jnp.minimum(i, 1), 0, 0, 0)),
            pl.BlockSpec((1, 4, tall, 128), lambda i: (0, 0, 0, 0)),
            pl.BlockSpec((1, 4, tall, 128), lambda i: (0, 0, 0, 0)),
        ],
        scratch_shapes=[
            pltpu.VMEM((wide + dim, 2 * tokens), BF16),
            pltpu.VMEM((2 * tokens, dim + dim // 2), BF16),
        ],
        compiler_params=params(),
        cost_estimate=cost(4e9, 10e6),
    )(place, keep, other)


def unpack_in(place_ref, *refs):
    pieces, w_ref, out_ref, sum_ref = refs[:4], refs[4], refs[5], refs[6]
    at = pl.program_id(0)
    for q, ref in enumerate(pieces):

        @pl.when(at // 2 == q)
        def _(ref=ref):
            value = ref[0].astype(F32)
            out_ref[...] = value
            sum_ref[...] = jnp.sum(value * w_ref[...].astype(F32), axis=1, keepdims=True)


def row_block(i, place_ref):
    side = jnp.where(i < 4, place_ref[7], 1 - place_ref[7])
    order = jnp.where(i % 4 == 1, 2, jnp.where(i % 4 == 2, 1, i % 4))
    return (side * 4 + (place_ref[8] ^ order), 0)


def run_unpack_in(place, pieces, weight):
    rows, columns = weight.shape
    short = rows // 8
    specs = [
        pl.BlockSpec((1, short, columns), lambda i, p, q=q: (jnp.clip(i - 2 * q, 0, 1), 0, 0))
        for q in range(4)
    ]
    block = pl.BlockSpec((short, columns), row_block)
    return pl.pallas_call(
        unpack_in,
        name="unpack_in",
        out_shape=(jax.ShapeDtypeStruct((rows, columns), F32), jax.ShapeDtypeStruct((rows, 1), F32)),
        grid_spec=pltpu.PrefetchScalarGridSpec(
            num_scalar_prefetch=1,
            grid=(8,),
            in_specs=specs + [block],
            out_specs=[block, pl.BlockSpec((short, 1), row_block)],
        ),
        compiler_params=params(),
        cost_estimate=cost(1e7, 11e6),
    )(place, *pieces, weight)


def sources(place_ref, pieces):
    core, z = place_ref[7], place_ref[8]
    for q, ref in enumerate(pieces):
        for at in range(2):
            side = core if q < 2 else 1 - core
            yield ref.at[at], side, z ^ ORDER[2 * (q % 2) + at]


def unpack_rest(place_ref, *refs):
    pieces, out_ref, down_ref = refs[:4], refs[4], refs[5]
    dim = out_ref.shape[1]
    short = dim // 32
    first = dim // 128 * short
    for ref, side, z in sources(place_ref, pieces):
        base = pl.multiple_of(side * 4 * short + z * short, 16)
        for t in range(dim // 128):
            out_ref[pl.ds(base, short), t * 128 : (t + 1) * 128] = ref[
                t * short : (t + 1) * short, :
            ].astype(F32)
        left = pl.multiple_of(side * (dim // 2) + z * 128, 128)
        down_ref[:, pl.ds(left, 128)] = ref[first:, :].astype(F32)


def run_unpack_rest(place, pieces, out_shape, down_shape):
    return pl.pallas_call(
        unpack_rest,
        name="unpack_rest",
        out_shape=(jax.ShapeDtypeStruct(out_shape, F32), jax.ShapeDtypeStruct(down_shape, F32)),
        in_specs=[smem_spec()] + [vmem_spec()] * 4,
        out_specs=[vmem_spec()] * 2,
        compiler_params=params(),
        cost_estimate=cost(1e7, 6e6),
    )(place, *pieces)


def unpack_qkv(place_ref, *refs):
    pieces, w_ref, out_ref, sum_ref = refs[:4], refs[4], refs[5], refs[6]
    width = pieces[0].shape[2] // 3
    dim = out_ref.shape[1] // 3
    total = jnp.zeros_like(sum_ref)
    for ref, side, z in sources(place_ref, pieces):
        for part in range(3):
            left = pl.multiple_of(part * dim + (z * 2 + side) * width, 128)
            value = ref[:, part * width : (part + 1) * width].astype(F32)
            out_ref[:, pl.ds(left, width)] = value
            weight = w_ref[:, pl.ds(left, width)].astype(F32)
            total = total + jnp.sum(value * weight, axis=1, keepdims=True)
    sum_ref[...] = total


def run_unpack_qkv(place, pieces, weight):
    return pl.pallas_call(
        unpack_qkv,
        name="unpack_qkv",
        out_shape=(
            jax.ShapeDtypeStruct(weight.shape, F32),
            jax.ShapeDtypeStruct((weight.shape[0], 1), F32),
        ),
        in_specs=[smem_spec()] + [vmem_spec()] * 5,
        out_specs=[vmem_spec()] * 2,
        compiler_params=params(),
        cost_estimate=cost(1e7, 7e6),
    )(place, *pieces, weight)


def input_grad(x_ref, gmid_ref, gain_ref, *refs):
    parts, out_ref = refs[:-1], refs[-1]
    x = x_ref[...].astype(F32)
    center = x - jnp.mean(x, axis=-1, keepdims=True)
    spread = jnp.mean(center * center, axis=-1, keepdims=True)
    scale = lax.rsqrt(spread + NORM_EPS)
    normal = center * scale
    e = sum(part[...].astype(F32) for part in parts) * gain_ref[...]
    pull = e - jnp.mean(e, axis=-1, keepdims=True) - normal * jnp.mean(e * normal, axis=-1, keepdims=True)
    out_ref[...] = (gmid_ref[...] + scale * pull).astype(BF16)


def run_input_grad(x, gmid, gain, parts):
    rows, dim = x.shape
    tall = rows // 4
    block = pl.BlockSpec((tall, dim), lambda i: (i, 0))
    return pl.pallas_call(
        input_grad,
        name="input_grad",
        out_shape=jax.ShapeDtypeStruct((rows, dim), BF16),
        grid=(4,),
        in_specs=[block, block, pl.BlockSpec((1, dim), lambda i: (0, 0))] + [block] * len(parts),
        out_specs=block,
        compiler_params=params(),
        cost_estimate=cost(1e8, 5e6),
    )(x, gmid, gain, *parts)


def sequence_layout(lengths, order, group):
    ends = jnp.cumsum(lengths)
    starts = ends - lengths
    index = jnp.arange(group, dtype=jnp.int32)
    passed = index[:, None] >= ends[None, :]
    start = jnp.sum(jnp.where(passed, lengths[None, :], 0), axis=1).astype(jnp.int32)
    inside = jnp.logical_and(index[:, None] >= starts[None, :], jnp.logical_not(passed))
    end = jnp.sum(jnp.where(inside, ends[None, :], 0), axis=1).astype(jnp.int32)
    places = index - start
    half = HD // 2
    speeds = jnp.power(F32(ROPE_BASE), -2.0 * jnp.arange(half, dtype=F32) / HD)
    angles = speeds[:, None] * places.astype(F32)[None, :]
    keys = (start[::WIDE] // BLOCK, (end[WIDE - 1 :: WIDE] + BLOCK - 1) // BLOCK)
    queries = (start[::BLOCK] // WIDE, (end[BLOCK - 1 :: BLOCK] + WIDE - 1) // WIDE)
    return (keys, queries, order[None, :], start[None, :], end[None, :], jnp.cos(angles), jnp.sin(angles))


def local(tokens, seq_lengths, seq_order, norm_one, w_qkv, w_out, norm_two, w_in, w_down, cotangent):
    seq_count = lax.axis_size("seq")
    fsdp_count = lax.axis_size("fsdp")
    levels = fsdp_count.bit_length() - 1
    count = fsdp_count - 1
    seq_at = lax.axis_index("seq")
    fsdp_at = lax.axis_index("fsdp")
    core = seq_at % 2
    x = tokens[0]
    cot = cotangent[0]
    rows, dim = x.shape
    group = rows * seq_count
    heads = dim // HD // seq_count
    width = heads * HD
    hidden = w_in.shape[1] // 2
    counts = (seq_count, fsdp_count)
    swap = functools.partial(core_swap, seq_count=seq_count)

    keys = [jnp.array([plane_mask(c, key, levels) for key in range(1, fsdp_count)], jnp.int32) for c in (0, 1)]
    mine = fsdp_at ^ jnp.where(core == 0, keys[0], keys[1])
    other = fsdp_at ^ jnp.where(core == 0, keys[1], keys[0])
    place = jnp.stack([fsdp_at, *mine, *other, core, seq_at // 2]).astype(jnp.int32)
    regular = fsdp_count == 4 and seq_count == 8 and w_down.shape[0] % 16 == 0 and dim == 1024

    layout = sequence_layout(seq_lengths[0], seq_order[0], group)
    if regular:
        chunks = [x, mixed_swap(x, 1, seq_count), mixed_swap(x, 0, seq_count)]
        chunks.append(mixed_swap(after(chunks[1], chunks[2], layout[5], layout[6]), 0, seq_count))
        chunks += [swap(chunk) for chunk in chunks]
    else:
        chunks = [lax.all_gather(x, "seq", axis=0, tiled=False)]
    own_heads = jnp.concatenate(
        [lax.dynamic_slice_in_dim(w_qkv, part * dim + seq_at * width, width, 1) for part in range(3)], axis=1
    )
    gains = jnp.stack([norm_one, norm_two])
    if regular:
        extra = jnp.pad(gains, ((0, 14), (0, 3 * width - gains.shape[1])))
        own_heads = jnp.concatenate([own_heads, extra], axis=0)
        head_pieces = [own_heads] + [plane_swap(own_heads, phase, *counts) for phase in range(2)]
        head_pieces.append(plane_swap(head_pieces[1], 1, *counts))
    else:
        head_pieces = [
            lax.all_gather(own_heads, "fsdp", axis=0, tiled=True),
            lax.all_gather(gains, "fsdp", axis=1, tiled=True).astype(F32),
        ]
    first_piece, second_piece = run_pack_pieces(place, w_in, w_out, w_down, regular)
    if regular:
        first_piece, second_piece = after(first_piece, *head_pieces[1:3]), after(second_piece, *head_pieces[1:])
    first_a, second_a = plane_swap(first_piece, 0, *counts), plane_swap(second_piece, 0, *counts)
    first = plane_gather_rest(first_piece, first_a, *counts, second_a)
    second = plane_gather_rest(second_piece, second_a, *counts, first_a)
    left = dim

    gains, w_heads, normed, packed, att, out_t, lse = run_attention_forward(place, chunks, head_pieces, layout, heads)
    gain_one, gain_two = gains[:1], gains[1:]
    att_done = lax.all_to_all(att, "seq", split_axis=0, concat_axis=0, tiled=True)
    first = first + [swap(first[0])] + [swap(after(piece, att)) for piece in first[1:]]
    if regular:
        downs = [w_down] + first
    else:
        downs = [lax.all_gather(w_down, "fsdp", axis=0, tiled=True)]
    grad_hidden = run_hidden_grad(place, cot, downs, left, hidden)
    second = second + [swap(second[0])] + [swap(after(piece, att_done, grad_hidden)) for piece in second[1:]]
    att = att_done
    middle, gmid, send, keep, gatt = run_feed_forward(
        place, x, att, cot, gain_two, grad_hidden, w_out, w_in, first, second, hidden
    )
    dout = lax.all_to_all(gatt, "seq", split_axis=0, concat_axis=0, tiled=True)
    reduce = functools.partial(plane_reduce, seq_count=seq_count, fsdp_count=fsdp_count)
    send_other, keep_other = swap(send), swap(keep)
    wide = padded(hidden)
    if regular:
        short = w_in.shape[0] // 8
        in_a, in_b, in_c = run_in_grad(place, send, send_other, hidden)
        in_a = plane_swap(in_a, 1, *counts)
        packed = after(packed, in_b)

    grads, *shares = run_attention_backward(place, dout, packed, out_t, lse, w_heads, layout, heads, regular)
    each = w_qkv.shape[0]
    if regular:
        in_sum = after(added(in_b[0], in_a[1]), grads)
        in_second = plane_swap(in_sum, 0, *counts)
        got, share = swap(shares[0]), shares[1]
        token_sum = added(share[2:], got[2:])
        token_z1 = mixed_swap(token_sum, 0, seq_count)
        rest_a, rest_b, rest_c = run_rest_grad(place, keep, after(keep_other, in_sum, token_sum), hidden)
        rest_a = plane_swap(rest_a, 1, *counts)
        gw_heads = run_qkv_weight_grad(place, normed, after(grads, rest_b), regular)
        in_parts = [p.reshape(4, short, 2 * hidden) for p in (in_c[0], in_a[0], in_second)]
        in_z1 = line_swap(after(added(*(p[2:] for p in in_parts)), gw_heads[1]), 0, seq_count)
        rest_sum = added(rest_b[0], rest_a[1])
        rest_second = plane_swap(rest_sum, 0, *counts)
        rest_parts = (rest_c[0], rest_a[0], rest_second)
        layer_out = run_layer_result(place, middle, after(keep, rest_sum), downs, left, hidden)
        token_z2 = mixed_swap(added(share[1], got[1], token_z1[1]), 1, seq_count)
        grad_tokens = run_input_grad(x, gmid, gain_one, [share[0], got[0], token_z1[0], token_z2])
        qkv_a, qkv_b, qkv_c = gw_heads
        qkv_a = plane_swap(after(qkv_a, rest_second), 1, *counts)
        qkv_block = added(*reduce(qkv_a, qkv_b, qkv_c))
        in_z2 = line_swap(added(*(p[1] for p in in_parts), in_z1[1]), 1, seq_count)
        in_block = after(added(*(p[0] for p in in_parts), in_z1[0], in_z2), layer_out)
        rest_z1 = line_swap(after(added(*(p[2:] for p in rest_parts)), token_z2), 0, seq_count)
        rest_z2 = line_swap(after(added(*(p[1] for p in rest_parts), rest_z1[1]), in_z2), 1, seq_count)
        rest_block = added(*(p[0] for p in rest_parts), rest_z1[0], rest_z2)
        in_pieces = line_gather(in_block, seq_count)
        gw_in, sum_in = run_unpack_in(place, in_pieces, w_in)
        rest_pieces = line_gather(rest_block, seq_count, sum_in)
        qkv_pieces = line_gather(after(qkv_block, grad_tokens), seq_count, sum_in)
        gw_qkv, sum_qkv = run_unpack_qkv(place, qkv_pieces, w_qkv)
        gw_out, gw_down = run_unpack_rest(place, rest_pieces, w_out.shape, w_down.shape)
        sum_qkv = sum_qkv[:, 0]
        sum_in = sum_in[:, 0]
    else:
        layer_out = run_layer_result(place, middle, keep, downs, left, hidden)
        gw_heads = run_qkv_weight_grad(place, normed, grads, regular)
        share = lax.psum_scatter(shares[0].astype(F32), "seq", scatter_dimension=0, tiled=False)
        grad_tokens = run_input_grad(x, gmid, gain_one, [share])

        def total(left_rows, right_rows):
            full = lax.dot_general(
                left_rows, right_rows, (((0,), (0,)), ((), ())), preferred_element_type=F32
            )
            return lax.psum(lax.psum_scatter(full, "fsdp", scatter_dimension=0, tiled=True), "seq")

        gw_in = total(send[:, 2 * hidden :], send[:, : 2 * hidden])
        gw_down = total(keep[:, :hidden], cot)
        gw_out = total(keep[:, wide + dim : wide + 2 * dim], keep[:, wide : wide + dim])
        sum_in = jnp.sum(gw_in * w_in.astype(F32), axis=1)
        gw_heads = lax.all_to_all(gw_heads[0].reshape(fsdp_count, each, -1), "fsdp", 0, 0, tiled=True)
        gw_heads = jnp.sum(gw_heads.astype(F32), axis=0).astype(BF16)
        gw_qkv = lax.all_gather(gw_heads, "seq", axis=0, tiled=False).reshape(seq_count, each, 3, width)
        gw_qkv = gw_qkv.transpose(1, 2, 0, 3).reshape(each, 3 * dim).astype(F32)
        sum_qkv = jnp.sum(gw_qkv * w_qkv.astype(F32), axis=1)

    grad_one = sum_qkv / norm_one.astype(F32)
    grad_two = sum_in / norm_two.astype(F32)
    return (layer_out[None], grad_tokens[None], grad_one, gw_qkv, gw_out, grad_two, gw_in, gw_down)


def solution(mesh):
    tokens = P("fsdp", "seq", None)
    rows = P("fsdp", None)
    return jax.shard_map(
        local,
        mesh=mesh,
        in_specs=(tokens, rows, rows, P("fsdp"), rows, rows, P("fsdp"), rows, rows, tokens),
        out_specs=(tokens, tokens, P("fsdp"), rows, rows, P("fsdp"), rows, rows),
        check_vma=False,
    )
```

```python
import functools
import math

import jax
import jax.numpy as jnp
from jax import lax
from jax.experimental import pallas as pl
from jax.experimental.pallas import tpu as pltpu
from jax.sharding import PartitionSpec as P

HD = 64
NORM_EPS = 1e-05
ROPE_BASE = 160000.0
BLOCK = 256
WIDE = 512
LOG2E = math.log2(math.e)
AXES = ("seq", "fsdp")
F32 = jnp.float32
BF16 = jnp.bfloat16
VMEM_LIMIT = 60 * 1024 * 1024


def core_swap(value, seq_count):
    return lax.ppermute(value, "seq", [(i, i ^ 1) for i in range(seq_count)])


def plane_bit(core, phase, levels):
    return (phase + core * (levels // 2)) % levels


def plane_mask(core, key, levels):
    mask = 0
    for phase in range(levels):
        if key >> phase & 1:
            mask |= 1 << plane_bit(core, phase, levels)
    return mask


def plane_swap(value, phase, seq_count, fsdp_count):
    levels = fsdp_count.bit_length() - 1
    pairs = []
    for s in range(seq_count):
        step = 1 << plane_bit(s & 1, phase, levels)
        for f in range(fsdp_count):
            pairs.append((s * fsdp_count + f, s * fsdp_count + (f ^ step)))
    return lax.ppermute(value, AXES, pairs)


def after(value, *others):
    return lax.optimization_barrier((value, *others))[0]


def plane_gather_rest(piece, first, seq_count, fsdp_count, *others):
    pieces = [after(piece, first, *others), after(first, *others)]
    for phase in range(1, fsdp_count.bit_length() - 1):
        pieces = pieces + [plane_swap(p, phase, seq_count, fsdp_count) for p in pieces]
    return [first] + pieces[2:]


def added(*values):
    return sum(v.astype(F32) for v in values).astype(BF16)


def plane_reduce(first, b, c, seq_count, fsdp_count):
    second = plane_swap(added(b[0], first[1]), 0, seq_count, fsdp_count)
    return c[0], first[0], second


def line_swap(value, level, seq_count):
    return lax.ppermute(value, "seq", [(i, i ^ (2 << level)) for i in range(seq_count)])


def mixed_swap(value, level, seq_count):
    return lax.ppermute(value, "seq", [(i, i ^ (2 << (level ^ (i & 1)))) for i in range(seq_count)])


def line_reduce(parts, seq_count):
    got = line_swap(added(*(p[2:] for p in parts)), 0, seq_count)
    last = line_swap(added(*(p[1] for p in parts), got[1]), 1, seq_count)
    return added(*(p[0] for p in parts), got[0], last)


def line_gather(block, seq_count, *others):
    pair = jnp.stack([block, line_swap(block, 1, seq_count)])
    rest = line_swap(pair, 0, seq_count)
    return [pair, rest, core_swap(pair, seq_count), core_swap(after(rest, *others), seq_count)]


def any_spec():
    return pl.BlockSpec(memory_space=pl.ANY)


def vmem_spec():
    return pl.BlockSpec(memory_space=pltpu.VMEM)


def smem_spec():
    return pl.BlockSpec(memory_space=pltpu.SMEM)


def params():
    return pltpu.CompilerParams(vmem_limit_bytes=VMEM_LIMIT)


def cost(flops, moved):
    return pl.CostEstimate(flops=int(flops), bytes_accessed=int(moved), transcendentals=0)


def nt_dot(a, b):
    return lax.dot_general(a, b, (((1,), (1,)), ((), ())), preferred_element_type=F32)


def nn_dot(a, b):
    return jnp.dot(a, b, preferred_element_type=F32)


def own_copy(place_ref, own, full, sems, rows):
    base = pl.multiple_of(place_ref[0] * rows, 16)
    return pltpu.make_async_copy(own, full.at[pl.ds(base, rows), :], sems.at[0])


def row_copies(place_ref, own, mine, others, left, full, sems):
    count = len(mine)
    rows = own.shape[0]
    half = rows // 2
    core = place_ref[2 * count + 1]
    copies = [own_copy(place_ref, own, full, sems, rows)]
    for which, (refs, side) in enumerate(((mine, core), (others, 1 - core))):
        for i, ref in enumerate(refs):
            at = 1 + which * count + i
            base = pl.multiple_of(place_ref[at] * rows + side * half, 16)
            copies.append(
                pltpu.make_async_copy(
                    ref.at[:, pl.ds(left, full.shape[1])], full.at[pl.ds(base, half), :], sems.at[at]
                )
            )
    return copies


def down_blocks(rows, columns, tall):
    whole = rows // tall
    blocks = [(k * tall, 0, tall, columns, 0, k * columns) for k in range(whole)]
    left = rows - whole * tall
    if left:
        blocks += [
            (whole * tall, 128 * q, left, 128, q * left, whole * columns) for q in range(columns // 128)
        ]
    return blocks


def down_width(rows, columns, tall):
    return rows // tall * columns + (128 if rows % tall else 0)


def down_copies(place_ref, own, mine, others, left, full, sems, hidden):
    if not mine:
        return [pltpu.make_async_copy(own, full.at[pl.ds(0, hidden), :], sems.at[0])]
    count = len(mine)
    rows = own.shape[0]
    half = own.shape[1] // 2
    core = place_ref[2 * count + 1]
    blocks = down_blocks(rows, half, mine[0].shape[0])
    copies = [own_copy(place_ref, own, full, sems, rows)]
    for which, (refs, side) in enumerate(((mine, core), (others, 1 - core))):
        for i, ref in enumerate(refs):
            at = 1 + which * count + i
            side_at = pl.multiple_of(side * half, 128)
            for k, (row, column, tall, wide, packed_row, packed_column) in enumerate(blocks):
                base = pl.multiple_of(place_ref[at] * rows + row, 16)
                copies.append(
                    pltpu.make_async_copy(
                        ref.at[pl.ds(packed_row, tall), pl.ds(left + packed_column, wide)],
                        full.at[pl.ds(base, tall), pl.ds(pl.multiple_of(side_at + column, 128), wide)],
                        sems.at[1 + (at - 1) * len(blocks) + k],
                    )
                )
    return copies


def pack_pieces(place_ref, in_ref, out_ref, down_ref, first_ref, second_ref, sems):
    half = in_ref.shape[0] // 2
    core = place_ref[place_ref.shape[0] - 2]
    base = pl.multiple_of(core * half, 16)
    also = out_ref.shape[1]
    copies = [
        pltpu.make_async_copy(
            out_ref.at[pl.ds(base, half), :], first_ref.at[:, pl.ds(0, also)], sems.at[0]
        ),
        pltpu.make_async_copy(in_ref.at[pl.ds(base, half), :], second_ref, sems.at[1]),
    ]
    if first_ref.shape[1] > also:
        columns = down_ref.shape[1] // 2
        side = pl.multiple_of(core * columns, 128)
        blocks = down_blocks(down_ref.shape[0], columns, half)
        for k, (row, column, tall, part, packed_row, packed_column) in enumerate(blocks):
            copies.append(
                pltpu.make_async_copy(
                    down_ref.at[pl.ds(row, tall), pl.ds(pl.multiple_of(side + column, 128), part)],
                    first_ref.at[pl.ds(packed_row, tall), pl.ds(also + packed_column, part)],
                    sems.at[2 + k],
                )
            )
    for copy in copies:
        copy.start()
    for copy in copies:
        copy.wait()


def run_pack_pieces(place, w_in, w_out, w_down, regular):
    half = w_in.shape[0] // 2
    down = (w_down.shape[0], w_down.shape[1] // 2, half)
    blocks = len(down_blocks(*down)) if regular else 0
    wide = w_out.shape[1] + (down_width(*down) if regular else 0)
    return pl.pallas_call(
        pack_pieces,
        name="pack_pieces",
        out_shape=(
            jax.ShapeDtypeStruct((half, wide), BF16),
            jax.ShapeDtypeStruct((half, w_in.shape[1]), BF16),
        ),
        in_specs=[smem_spec()] + [any_spec()] * 3,
        out_specs=[vmem_spec()] * 2,
        scratch_shapes=[pltpu.SemaphoreType.DMA((2 + blocks,))],
        compiler_params=params(),
        cost_estimate=cost(1e6, 5e6),
    )(place, w_in, w_out, w_down)


def attention_forward(
    seq_count, heads, group, low_ref, high_ref, place_ref, order_ref, start_ref, end_ref,
    cos_ref, sin_ref, *refs,
):
    x_hbm, refs = (refs[:1], refs[1:]) if len(refs[0].shape) == 3 else (refs[:seq_count], refs[seq_count:])
    pieces, refs = refs[:-15], refs[-15:]
    gains_ref, w_ref, normed_hbm, packed_ref, att_ref, out_ref, lse_ref = refs[:7]
    x_ref, normed_ref, qkv_t, k_rows, o_rows, scores_ref, x_sems, normed_sems = refs[7:]
    width = heads * HD
    rows = group // seq_count
    blocks = group // BLOCK
    if len(x_hbm) == 1:
        chunks = list(range(seq_count))
        x_hbm = [x_hbm[0].at[i] for i in chunks]
    else:
        core, z = place_ref[7], place_ref[8]
        chunks = [(z ^ k) * 2 + side for side in (core, 1 - core) for k in block_order(side)]
    fetches = [pltpu.make_async_copy(x_hbm[i], x_ref.at[i], x_sems.at[i]) for i in range(seq_count)]
    stores = [
        pltpu.make_async_copy(normed_ref.at[i], normed_hbm.at[chunks[i]], normed_sems.at[i])
        for i in range(seq_count)
    ]
    for fetch in fetches:
        fetch.start()
    if len(pieces) == 2:
        w_ref[...] = pieces[0][...]
        gains_ref[...] = pieces[1][...]
    else:
        tall = w_ref.shape[0] // len(pieces)
        for key, piece in enumerate(pieces):
            base = pl.multiple_of(place_ref[key] * tall, 128)
            w_ref[pl.ds(base, tall), :] = piece[:tall]
            gains_ref[:, pl.ds(base, tall)] = piece[tall : tall + 2, :tall].astype(F32)
    gain_ref = gains_ref.at[pl.ds(0, 1), :]

    def project(i):
        x = x_ref[i].astype(F32)
        center = x - jnp.mean(x, axis=-1, keepdims=True)
        spread = jnp.mean(center * center, axis=-1, keepdims=True)
        normed = (center * lax.rsqrt(spread + NORM_EPS) * gain_ref[...]).astype(BF16)
        normed_ref[i] = normed
        qkv = nn_dot(normed, w_ref[...]).astype(BF16)
        qkv_t[chunks[i]] = qkv.T

    for i in range(seq_count):
        fetches[i].wait()
        project(i)
        stores[i].start()

    def pack(i, carry):
        at = pl.ds(pl.multiple_of(i * BLOCK, BLOCK), BLOCK)
        order = order_ref[:, at]
        total = jnp.zeros((3 * width, BLOCK), F32)
        for s in range(seq_count):
            here = lax.broadcasted_iota(jnp.int32, (rows, BLOCK), 0) + s * rows
            hot = jnp.where(here == order, 1.0, 0.0).astype(BF16)
            total = total + nn_dot(qkv_t[s], hot)
        cos = cos_ref[:, at]
        sin = sin_ref[:, at]
        half = HD // 2
        for part in range(2):
            for h in range(heads):
                base = part * width + h * HD
                first = total[base : base + half]
                second = total[base + half : base + HD]
                turned = jnp.concatenate(
                    [first * cos - second * sin, second * cos + first * sin], axis=0
                ).astype(BF16)
                packed_ref[base : base + HD, at] = turned
                if part == 1:
                    k_rows[h, at, :] = turned.T
        packed_ref[2 * width :, at] = total[2 * width :].astype(BF16)
        return carry

    lax.fori_loop(0, blocks, pack, 0)
    scale = HD**-0.5 * LOG2E

    def attend(i, carry):
        at = pl.ds(pl.multiple_of(i * WIDE, WIDE), WIDE)
        start = start_ref[:, at]
        end = end_ref[:, at]
        queries = [packed_ref[h * HD : (h + 1) * HD, at] for h in range(heads)]

        low, high = low_ref[i], high_ref[i]

        def score(j, tops):
            there = pl.ds(pl.multiple_of(j * BLOCK, BLOCK), BLOCK)
            where = lax.broadcasted_iota(jnp.int32, (BLOCK, WIDE), 0) + j * BLOCK
            same = jnp.logical_and(where >= start, where < end)
            following = []
            for h in range(heads):
                scores = jnp.where(same, nn_dot(k_rows[h, there, :], queries[h]) * scale, -1e30)
                scores_ref[j, h] = scores
                following.append(jnp.maximum(tops[h], jnp.max(scores.reshape(-1, 8, WIDE), axis=0)))
            return tuple(following)

        tops = lax.fori_loop(low, high, score, tuple(jnp.full((8, WIDE), -1e30, F32) for _ in range(heads)))
        tops = [jnp.max(top, axis=0, keepdims=True) for top in tops]

        def weigh(j, state):
            there = pl.ds(pl.multiple_of(j * BLOCK, BLOCK), BLOCK)
            following = []
            for h in range(heads):
                total, acc = state[h]
                probs = jnp.exp2(scores_ref[j, h] - tops[h])
                total = total + jnp.sum(probs.reshape(-1, 8, WIDE), axis=0)
                base = 2 * width + h * HD
                acc = acc + nn_dot(packed_ref[base : base + HD, there], probs.astype(BF16))
                following.append((total, acc))
            return tuple(following)

        first = tuple((jnp.zeros((8, WIDE), F32), jnp.zeros((HD, WIDE), F32)) for _ in range(heads))
        last = lax.fori_loop(low, high, weigh, first)
        outs = []
        for h in range(heads):
            total, acc = last[h]
            total = jnp.sum(total, axis=0, keepdims=True)
            out = acc / total
            out_ref[h * HD : (h + 1) * HD, at] = out
            lse_ref[h : h + 1, at] = tops[h] + jnp.log2(total)
            outs.append(out)
        o_rows[at, :] = jnp.concatenate(outs, axis=0).astype(BF16).T
        return carry

    lax.fori_loop(0, group // WIDE, attend, 0)

    def arrive(i, carry):
        here = lax.broadcasted_iota(jnp.int32, (rows, group), 0) + i * rows
        hot = jnp.where(here == order_ref[...], 1.0, 0.0).astype(BF16)
        att_ref[i] = nn_dot(hot, o_rows[...]).astype(BF16)
        return carry

    lax.fori_loop(0, seq_count, arrive, 0)
    for store in stores:
        store.wait()


def run_attention_forward(place, chunks, pieces, layout, heads):
    rows, dim = chunks[0].shape[-2:]
    group = layout[2].shape[1]
    seq_count = group // rows
    width = heads * HD
    (low, high), _, order, start, end, cos, sin = layout
    return pl.pallas_call(
        functools.partial(attention_forward, seq_count, heads, group),
        name="attention_forward",
        out_shape=(
            jax.ShapeDtypeStruct((2, dim), F32),
            jax.ShapeDtypeStruct((dim, 3 * width), BF16),
            jax.ShapeDtypeStruct((seq_count, rows, dim), BF16),
            jax.ShapeDtypeStruct((3 * width, group), BF16),
            jax.ShapeDtypeStruct((seq_count, rows, width), BF16),
            jax.ShapeDtypeStruct((width, group), F32),
            jax.ShapeDtypeStruct((heads, group), F32),
        ),
        in_specs=[smem_spec()] * 3 + [vmem_spec()] * 5 + [any_spec()] * len(chunks) + [vmem_spec()] * len(pieces),
        out_specs=[vmem_spec()] * 2 + [any_spec()] + [vmem_spec()] * 4,
        scratch_shapes=[
            pltpu.VMEM((seq_count, rows, dim), BF16),
            pltpu.VMEM((seq_count, rows, dim), BF16),
            pltpu.VMEM((seq_count, 3 * width, rows), BF16),
            pltpu.VMEM((heads, group, HD), BF16),
            pltpu.VMEM((group, width), BF16),
            pltpu.VMEM((group // BLOCK, heads, BLOCK, WIDE), F32),
            pltpu.SemaphoreType.DMA((seq_count,)),
            pltpu.SemaphoreType.DMA((seq_count,)),
        ],
        compiler_params=params(),
        cost_estimate=cost(24e9, 20e6),
    )(low, high, place, order, start, end, cos, sin, *chunks, *pieces)


def attention_backward(
    seq_count, heads, group, low_ref, high_ref, place_ref, dout_ref, packed_ref, out_ref, lse_ref, order_ref,
    start_ref, end_ref, cos_ref, sin_ref, w_ref, grad_hbm, *refs,
):
    results, refs = refs[:-13], refs[-13:]
    dout_t, dpack_t, drows, qrows, krows, vrows, delta_ref, dq_t, grows = refs[:9]
    grad_ref, share_ref, grad_sems, share_sems = refs[9:]
    width = heads * HD
    rows = group // seq_count
    blocks = group // BLOCK
    scale = HD**-0.5

    def turn(i, carry):
        dout_t[i] = dout_ref[i].T
        return carry

    lax.fori_loop(0, seq_count, turn, 0)

    def pack(i, carry):
        at = pl.ds(pl.multiple_of(i * BLOCK, BLOCK), BLOCK)
        order = order_ref[:, at]
        total = jnp.zeros((width, BLOCK), F32)
        for s in range(seq_count):
            here = lax.broadcasted_iota(jnp.int32, (rows, BLOCK), 0) + s * rows
            hot = jnp.where(here == order, 1.0, 0.0).astype(BF16)
            total = total + nn_dot(dout_t[s], hot)
        dpack_t[:, at] = total.astype(BF16)
        for h in range(heads):
            mine = total[h * HD : (h + 1) * HD]
            delta_ref[h : h + 1, at] = jnp.sum(
                mine * out_ref[h * HD : (h + 1) * HD, at], axis=0, keepdims=True
            )
            drows[h, at, :] = mine.T.astype(BF16)
            for part, ref in enumerate((qrows, krows, vrows)):
                base = part * width + h * HD
                ref[h, at, :] = packed_ref[base : base + HD, at].T
        dq_t[:, at] = jnp.zeros((width, BLOCK), F32)
        return carry

    lax.fori_loop(0, blocks, pack, 0)

    def keys(j, carry):
        there = pl.ds(pl.multiple_of(j * BLOCK, BLOCK), BLOCK)
        where = lax.broadcasted_iota(jnp.int32, (BLOCK, WIDE), 0) + j * BLOCK

        def queries(i, state):
            at = pl.ds(pl.multiple_of(i * WIDE, WIDE), WIDE)
            same = jnp.logical_and(where >= start_ref[:, at], where < end_ref[:, at])
            following = []
            for h in range(heads):
                dk, dv = state[h]
                base = h * HD
                key_rows = krows[h, there, :]
                query_t = packed_ref[base : base + HD, at]
                scores = nn_dot(key_rows, query_t) * (scale * LOG2E)
                scores = jnp.where(same, scores, -1e30)
                probs = jnp.exp2(scores - lse_ref[h : h + 1, at])
                dprobs = nn_dot(vrows[h, there, :], dpack_t[base : base + HD, at])
                raw = (probs * (dprobs - delta_ref[h : h + 1, at]) * scale).astype(BF16)
                dv = dv + nn_dot(probs.astype(BF16), drows[h, at, :])
                dk = dk + nn_dot(raw, qrows[h, at, :])
                key_t = packed_ref[width + base : width + base + HD, there]
                dq_t[base : base + HD, at] += nn_dot(key_t, raw)
                following.append((dk, dv))
            return tuple(following)

        zero = jnp.zeros((BLOCK, HD), F32)
        last = lax.fori_loop(low_ref[j], high_ref[j], queries, tuple((zero, zero) for _ in range(heads)))
        cos = cos_ref[:, there]
        sin = sin_ref[:, there]
        half = HD // 2
        turned = []
        for h in range(heads):
            dk_t = last[h][0].T
            first, second = dk_t[:half], dk_t[half:]
            turned.append(first * cos + second * sin)
            turned.append(second * cos - first * sin)
        grows[there, width : 2 * width] = jnp.concatenate(turned, axis=0).T.astype(BF16)
        grows[there, 2 * width :] = jnp.concatenate([last[h][1] for h in range(heads)], axis=1).astype(BF16)
        return carry

    lax.fori_loop(0, blocks, keys, 0)

    def finish(i, carry):
        at = pl.ds(pl.multiple_of(i * BLOCK, BLOCK), BLOCK)
        cos = cos_ref[:, at]
        sin = sin_ref[:, at]
        half = HD // 2
        turned = []
        for h in range(heads):
            first = dq_t[h * HD : h * HD + half, at]
            second = dq_t[h * HD + half : (h + 1) * HD, at]
            turned.append(first * cos + second * sin)
            turned.append(second * cos - first * sin)
        grows[at, :width] = jnp.concatenate(turned, axis=0).T.astype(BF16)
        return carry

    lax.fori_loop(0, blocks, finish, 0)

    def arrive(i):
        here = lax.broadcasted_iota(jnp.int32, (rows, group), 0) + i * rows
        hot = jnp.where(here == order_ref[...], 1.0, 0.0).astype(BF16)
        grad = nn_dot(hot, grows[...]).astype(BF16)
        grad_ref[i] = grad
        grad_out(i).start()
        return nt_dot(grad, w_ref[...]).astype(BF16)

    def grad_out(i):
        return pltpu.make_async_copy(grad_ref.at[i], grad_hbm.at[i], grad_sems.at[i])

    def share_out(result, first, j):
        return pltpu.make_async_copy(share_ref.at[first + j], result.at[j], share_sems.at[first + j])

    sides = [0] if len(results) == 1 else [1 - place_ref[7], place_ref[7]]
    count = seq_count // len(results)
    for which, (side, result) in enumerate(zip(sides, results)):
        first = which * count

        def each(j, carry, side=side, result=result, first=first):
            if len(results) == 1:
                source = j
            else:
                k = jnp.where(j == 1, 2 - side, jnp.where(j == 2, 1 + side, j))
                source = (place_ref[8] ^ k) * 2 + side
            share_ref[first + j] = arrive(source)
            share_out(result, first, j).start()
            return carry

        lax.fori_loop(0, count, each, 0)
    for i in range(seq_count):
        grad_out(i).wait()
    for which, result in enumerate(results):
        for j in range(count):
            share_out(result, which * count, j).wait()


def run_attention_backward(place, dout, packed, out_t, lse, w_heads, layout, heads, regular):
    seq_count, rows, width = dout.shape
    group = seq_count * rows
    dim = w_heads.shape[0]
    _, (low, high), order, start, end, cos, sin = layout
    shares = [seq_count // 2] * 2 if regular else [seq_count]
    return pl.pallas_call(
        functools.partial(attention_backward, seq_count, heads, group),
        name="attention_backward",
        out_shape=[jax.ShapeDtypeStruct((seq_count, rows, 3 * width), BF16)]
        + [jax.ShapeDtypeStruct((share, rows, dim), BF16) for share in shares],
        in_specs=[smem_spec()] * 3 + [vmem_spec()] * 10,
        out_specs=[any_spec()] * (1 + len(shares)),
        scratch_shapes=[
            pltpu.VMEM((seq_count, width, rows), BF16),
            pltpu.VMEM((width, group), BF16),
            pltpu.VMEM((heads, group, HD), BF16),
            pltpu.VMEM((heads, group, HD), BF16),
            pltpu.VMEM((heads, group, HD), BF16),
            pltpu.VMEM((heads, group, HD), BF16),
            pltpu.VMEM((heads, group), F32),
            pltpu.VMEM((width, group), F32),
            pltpu.VMEM((group, 3 * width), BF16),
            pltpu.VMEM((seq_count, rows, 3 * width), BF16),
            pltpu.VMEM((seq_count, rows, dim), BF16),
            pltpu.SemaphoreType.DMA((seq_count,)),
            pltpu.SemaphoreType.DMA((seq_count,)),
        ],
        compiler_params=params(),
        cost_estimate=cost(33e9, 15e6),
    )(low, high, place, dout, packed, out_t, lse, order, start, end, cos, sin, w_heads)


def qkv_weight_grad(seq_count, place_ref, normed_ref, grad_ref, *refs):
    outs, (total, turned) = refs[:-2], refs[-2:]
    total[...] = jnp.zeros_like(total)

    def step(i, carry):
        total[...] += nn_dot(grad_ref[i].T, normed_ref[i])
        return carry

    lax.fori_loop(0, seq_count, step, 0)
    if len(outs) == 1:
        outs[0][...] = total[...].T.astype(BF16)
        return
    turned[...] = total[...].T
    rows = outs[0].shape[1]
    for ref, keys in zip(outs, ((2, 3), (1,), (0,))):
        for at, key in enumerate(keys):
            base = pl.multiple_of(place_ref[key] * rows, 16)
            ref[at] = turned[pl.ds(base, rows), :].astype(BF16)


def run_qkv_weight_grad(place, normed, grad, regular):
    seq_count, rows, dim = normed.shape
    width = grad.shape[-1]
    if regular:
        outs = tuple(jax.ShapeDtypeStruct((n, dim // 4, width), BF16) for n in (2, 1, 1))
    else:
        outs = (jax.ShapeDtypeStruct((dim, width), BF16),)
    return pl.pallas_call(
        functools.partial(qkv_weight_grad, seq_count),
        name="qkv_weight_grad",
        out_shape=outs,
        in_specs=[smem_spec()] + [vmem_spec()] * 2,
        out_specs=[vmem_spec()] * len(outs),
        scratch_shapes=[pltpu.VMEM((width, dim), F32), pltpu.VMEM((dim, width), F32)],
        compiler_params=params(),
        cost_estimate=cost(3e9, 6e6),
    )(place, normed, grad)


def padded(hidden):
    return -(-hidden // 128) * 128


def load_down(place_ref, refs, count, hidden, left, full, sems):
    copies = down_copies(place_ref, refs[0], refs[1 : 1 + count], refs[1 + count :], left, full, sems, hidden)
    for copy in copies:
        copy.start()
    tail = padded(hidden) - hidden
    if tail:
        full[pl.ds(hidden, tail), :] = jnp.zeros((tail, full.shape[1]), BF16)
    for copy in copies:
        copy.wait()


def down_semaphores(downs):
    if len(downs) == 1:
        return pltpu.SemaphoreType.DMA((1,))
    blocks = len(down_blocks(downs[0].shape[0], downs[0].shape[1] // 2, downs[1].shape[0]))
    return pltpu.SemaphoreType.DMA((1 + (len(downs) - 1) * blocks,))


def hidden_grad(hidden, left, place_ref, cot_ref, *refs):
    downs, (out_ref, full, sems) = refs[:-3], refs[-3:]
    load_down(place_ref, downs, (len(downs) - 1) // 2, hidden, left, full, sems)
    cot = cot_ref[...]
    tiles = padded(hidden) // 128
    wide = 128 * max(n for n in (1, 2, 3) if tiles % n == 0)

    def step(i, carry):
        at = pl.multiple_of(i * wide, 128)
        out_ref[:, pl.ds(at, wide)] = nt_dot(cot, full[pl.ds(at, wide), :])
        return carry

    lax.fori_loop(0, padded(hidden) // wide, step, 0)


def run_hidden_grad(place, cot, downs, left, hidden):
    rows, dim = cot.shape
    return pl.pallas_call(
        functools.partial(hidden_grad, hidden, left),
        name="hidden_grad",
        out_shape=jax.ShapeDtypeStruct((rows, padded(hidden)), F32),
        in_specs=[smem_spec(), vmem_spec()] + [any_spec()] * len(downs),
        out_specs=vmem_spec(),
        scratch_shapes=[pltpu.VMEM((padded(hidden), dim), BF16), down_semaphores(downs)],
        compiler_params=params(),
        cost_estimate=cost(4e9, 9e6),
    )(place, cot, *downs)


def layer_result(hidden, left, place_ref, mid_ref, keep_ref, *refs):
    downs, (out_ref, full, sems) = refs[:-3], refs[-3:]
    load_down(place_ref, downs, (len(downs) - 1) // 2, hidden, left, full, sems)
    wide = padded(hidden)

    def step(i, carry):
        at = pl.ds(pl.multiple_of(i * 256, 256), 256)
        out_ref[:, at] = (mid_ref[:, at] + nn_dot(keep_ref[:, :wide], full[:, at])).astype(BF16)
        return carry

    lax.fori_loop(0, out_ref.shape[1] // 256, step, 0)


def run_layer_result(place, middle, keep, downs, left, hidden):
    rows, dim = middle.shape
    return pl.pallas_call(
        functools.partial(layer_result, hidden, left),
        name="layer_result",
        out_shape=jax.ShapeDtypeStruct((rows, dim), BF16),
        in_specs=[smem_spec()] + [vmem_spec()] * 2 + [any_spec()] * len(downs),
        out_specs=vmem_spec(),
        scratch_shapes=[pltpu.VMEM((padded(hidden), dim), BF16), down_semaphores(downs)],
        compiler_params=params(),
        cost_estimate=cost(4e9, 9e6),
    )(place, middle, keep, *downs)


def feed_forward(
    count, hidden, heads_width, place_ref, x_ref, att_ref, cot_ref, gain_ref, gh_hbm, *refs
):
    out_own, in_own, refs = refs[0], refs[1], refs[2:]
    first, others, refs = refs[:count], refs[count : 2 * count], refs[2 * count :]
    second, second_others, refs = refs[:count], refs[count : 2 * count], refs[2 * count :]
    mid_ref, gmid_ref, send_hbm, keep_hbm, ga_ref = refs[:5]
    wo, wi, both, early, late, send_ref, keep_ref, gh_ref, sem_o, sem_i, sems = refs[5:]
    fetch = pltpu.make_async_copy(gh_hbm, gh_ref, sems.at[0])
    send_out = pltpu.make_async_copy(send_ref, send_hbm, sems.at[1])
    keep_out = pltpu.make_async_copy(keep_ref, keep_hbm, sems.at[2])
    dim = x_ref.shape[1]
    wide_hidden = padded(hidden)
    nt_ref = send_ref.at[:, pl.ds(2 * hidden, dim)]
    gboth_ref = send_ref
    hid_ref = keep_ref
    gbr_ref = keep_ref.at[:, pl.ds(wide_hidden, dim)]
    att_all_ref = keep_ref.at[:, pl.ds(wide_hidden + dim, dim)]
    keep_ref[:, pl.ds(wide_hidden + 2 * dim, dim)] = cot_ref[...]
    copies_o = row_copies(place_ref, out_own, first, others, 0, wo, sem_o)
    copies_i = row_copies(place_ref, in_own, second, second_others, 0, wi, sem_i)
    for copy in copies_o:
        copy.start()
    for copy in copies_i:
        copy.start()
    fetch.start()
    att = jnp.concatenate([att_ref[s] for s in range(att_ref.shape[0])], axis=1)
    att_all_ref[...] = att
    for copy in copies_o:
        copy.wait()

    def branch(i, carry):
        at = pl.ds(pl.multiple_of(i * 256, 256), 256)
        mid_ref[:, at] = x_ref[:, at].astype(F32) + nn_dot(att_all_ref[...], wo[:, at])
        return carry

    lax.fori_loop(0, dim // 256, branch, 0)
    middle = mid_ref[...]
    center = middle - jnp.mean(middle, axis=-1, keepdims=True)
    spread = jnp.mean(center * center, axis=-1, keepdims=True)
    scale = lax.rsqrt(spread + NORM_EPS)
    nt_ref[...] = (center * scale * gain_ref[...]).astype(BF16)
    for copy in copies_i:
        copy.wait()
    fetch.wait()
    wide = 2 * hidden // 128

    def expand(i, carry):
        at = pl.ds(pl.multiple_of(i * 512, 512), 512)
        both[:, at] = nn_dot(nt_ref[...], wi[:, at])
        return carry

    lax.fori_loop(0, wide // 4, expand, 0)
    if wide % 4:
        at = pl.ds(128 * (wide - wide % 4), 128 * (wide % 4))
        both[:, at] = nn_dot(nt_ref[...], wi[:, at])
    both[:, pl.ds(128 * wide, 128)] = jnp.zeros((both.shape[0], 128), F32)
    tiles = padded(hidden) // 128
    whole = hidden // 128
    lanes = lax.broadcasted_iota(jnp.int32, (both.shape[0], 128), 1)
    shift = hidden % 128

    def tile(i):
        return pl.ds(pl.multiple_of(i * 128, 128), 128)

    def gates(i):
        a = both[:, tile(i)]
        if shift:
            left = pltpu.roll(both[:, tile(whole + i)], 128 - shift, 1)
            right = pltpu.roll(both[:, tile(whole + i + 1)], 128 - shift, 1)
            b = jnp.where(lanes < 128 - shift, left, right)
        else:
            b = both[:, tile(whole + i)]
        gh = gh_ref[:, tile(i)]
        phi = 0.5 * (1.0 + lax.erf(a * (0.5**0.5)))
        gelu = a * phi
        slope = phi + a * ((0.5 / math.pi) ** 0.5 * jnp.exp(-0.5 * a * a))
        hid_ref[:, tile(i)] = (gelu * b).astype(BF16)
        return gh * b * slope, gh * gelu

    if shift:
        first_a, first_b = gates(0)
        gboth_ref[:, tile(0)] = first_a.astype(BF16)
        early[...] = pltpu.roll(first_b, shift, 1)
        late[...] = early[...]

        def inner(i, carry):
            ga, gb = gates(i)
            turned = pltpu.roll(gb, shift, 1)
            gboth_ref[:, tile(i)] = ga.astype(BF16)
            gboth_ref[:, tile(whole + i)] = jnp.where(lanes < shift, late[...], turned).astype(BF16)
            late[...] = turned
            return carry

        lax.fori_loop(1, tiles - 1, inner, 0)
        ga, gb = gates(tiles - 1)
        turned = pltpu.roll(gb, shift, 1)
        gboth_ref[:, tile(whole)] = jnp.where(lanes < shift, ga, early[...]).astype(BF16)
        gboth_ref[:, tile(2 * whole)] = jnp.where(lanes < shift, late[...], turned).astype(BF16)
    else:

        def inner(i, carry):
            ga, gb = gates(i)
            gboth_ref[:, tile(i)] = ga.astype(BF16)
            gboth_ref[:, tile(whole + i)] = gb.astype(BF16)
            return carry

        lax.fori_loop(0, tiles, inner, 0)

    send_out.start()

    def back(i, carry):
        at = pl.multiple_of(i * 512, 512)
        both[:, pl.ds(at, 512)] = nt_dot(gboth_ref[:, : 2 * hidden], wi[pl.ds(at, 512), :])
        return carry

    lax.fori_loop(0, dim // 512, back, 0)
    middle = mid_ref[...]
    center = middle - jnp.mean(middle, axis=-1, keepdims=True)
    spread = jnp.mean(center * center, axis=-1, keepdims=True)
    scale = lax.rsqrt(spread + NORM_EPS)
    normal = center * scale
    e = both[:, pl.ds(0, dim)] * gain_ref[...]
    pull = e - jnp.mean(e, axis=-1, keepdims=True) - normal * jnp.mean(e * normal, axis=-1, keepdims=True)
    gmid = cot_ref[...].astype(F32) + scale * pull
    gmid_ref[...] = gmid
    gbr_ref[...] = gmid.astype(BF16)
    keep_out.start()

    def spread_out(i, carry):
        at = pl.multiple_of(i * 512, 512)
        both[:, pl.ds(at, 512)] = nt_dot(gbr_ref[...], wo[pl.ds(at, 512), :])
        return carry

    lax.fori_loop(0, dim // 512, spread_out, 0)
    for s in range(att_ref.shape[0]):
        ga_ref[s] = both[:, s * heads_width : (s + 1) * heads_width].astype(BF16)
    send_out.wait()
    keep_out.wait()


def run_feed_forward(place, x, att, cot, gain, grad_hidden, w_out, w_in, first, second, hidden):
    rows, dim = x.shape
    seq_count, _, heads_width = att.shape
    count = len(first) // 2
    return pl.pallas_call(
        functools.partial(feed_forward, count, hidden, heads_width),
        name="feed_forward",
        out_shape=(
            jax.ShapeDtypeStruct((rows, dim), F32),
            jax.ShapeDtypeStruct((rows, dim), F32),
            jax.ShapeDtypeStruct((rows, 2 * hidden + dim), BF16),
            jax.ShapeDtypeStruct((rows, padded(hidden) + 3 * dim), BF16),
            jax.ShapeDtypeStruct((seq_count, rows, heads_width), BF16),
        ),
        in_specs=[smem_spec()] + [vmem_spec()] * 4 + [any_spec()] * (3 + 4 * count),
        out_specs=[vmem_spec()] * 2 + [any_spec()] * 2 + [vmem_spec()],
        scratch_shapes=[
            pltpu.VMEM((dim, dim), BF16),
            pltpu.VMEM((dim, 2 * hidden), BF16),
            pltpu.VMEM((rows, 2 * hidden + 128), F32),
            pltpu.VMEM((rows, 128), F32),
            pltpu.VMEM((rows, 128), F32),
            pltpu.VMEM((rows, 2 * hidden + dim), BF16),
            pltpu.VMEM((rows, padded(hidden) + 3 * dim), BF16),
            pltpu.VMEM((rows, padded(hidden)), F32),
            pltpu.SemaphoreType.DMA((2 * count + 1,)),
            pltpu.SemaphoreType.DMA((2 * count + 1,)),
            pltpu.SemaphoreType.DMA((3,)),
        ],
        compiler_params=params(),
        cost_estimate=cost(16e9, 24e6),
    )(place, x, att, cot, gain, grad_hidden, w_out, w_in, *first, *second)


ORDER = (0, 2, 1, 3)


def block_order(core):
    return (0, 2 - core, 1 + core, 3)


def in_grad(hidden, wide, place_ref, send_ref, other_ref, a_ref, b_ref, c_ref, turned, picked):
    tokens = send_ref.shape[0]
    rows = turned.shape[0] // 4
    half, short = rows // 2, rows // 8

    @pl.when(pl.program_id(0) == 0)
    def _():
        turned[:, :tokens] = send_ref[:, 2 * hidden :].T
        turned[:, tokens:] = other_ref[:, 2 * hidden :].T
        core, z = place_ref[7], place_ref[8]
        for at, key in enumerate((2, 3, 1, 0)):
            for j, k in enumerate(ORDER):
                base = pl.multiple_of(place_ref[key] * rows + core * half + (z ^ k) * short, 16)
                to = at * half + j * short
                picked[to : to + short, :] = turned[pl.ds(base, short), :]

    at = pl.ds(pl.multiple_of(pl.program_id(0) * wide, 128), wide)
    right = jnp.concatenate([send_ref[:, at], other_ref[:, at]], axis=0)
    result = nn_dot(picked[...], right).astype(BF16)
    a_ref[0] = result[:half]
    a_ref[1] = result[half : 2 * half]
    b_ref[0] = result[2 * half : 3 * half]
    c_ref[0] = result[3 * half :]


def run_in_grad(place, send, other, hidden):
    tokens = send.shape[0]
    features = send.shape[1] - 2 * hidden
    columns = 2 * hidden
    half = features // 8
    wide = 896
    whole = pl.BlockSpec(send.shape, lambda i: (0, 0))
    return pl.pallas_call(
        functools.partial(in_grad, hidden, wide),
        name="in_grad",
        out_shape=tuple(jax.ShapeDtypeStruct((n, half, columns), BF16) for n in (2, 1, 1)),
        grid=(pl.cdiv(columns, wide),),
        in_specs=[smem_spec(), whole, whole],
        out_specs=[pl.BlockSpec((n, half, wide), lambda i: (0, 0, i)) for n in (2, 1, 1)],
        scratch_shapes=[
            pltpu.VMEM((features, 2 * tokens), BF16),
            pltpu.VMEM((features // 2, 2 * tokens), BF16),
        ],
        compiler_params=params(),
        cost_estimate=cost(2.0 * 2 * tokens * features * columns, 4 * tokens * columns + features * columns),
    )(place, send, other)


def rest_grad(hidden, place_ref, keep_ref, other_ref, a_ref, b_ref, c_ref, turned, picked):
    tokens = keep_ref.shape[0]
    wide = padded(hidden)
    dim = (keep_ref.shape[1] - wide) // 3
    half = dim // 2
    down_rows = hidden // 4
    short = dim // 32
    core, z = place_ref[7], place_ref[8]
    at = pl.program_id(0)

    @pl.when(at == 0)
    def _():
        turned[:wide, :tokens] = keep_ref[:, :wide].T
        turned[:wide, tokens:] = other_ref[:, :wide].T
        turned[wide:, :tokens] = keep_ref[:, wide + dim : wide + 2 * dim].T
        turned[wide:, tokens:] = other_ref[:, wide + dim : wide + 2 * dim].T
        for j, k in enumerate(ORDER):
            left = pl.ds(pl.multiple_of(wide + 2 * dim + core * half + (z ^ k) * 128, 128), 128)
            picked[:tokens, j * 128 : (j + 1) * 128] = keep_ref[:, left]
            picked[tokens:, j * 128 : (j + 1) * 128] = other_ref[:, left]
        picked[:tokens, half:] = keep_ref[:, wide : wide + dim]
        picked[tokens:, half:] = other_ref[:, wide : wide + dim]

    owner = place_ref[jnp.where(at < 2, at + 2, 3 - at)]
    base = pl.multiple_of(owner * down_rows, 16)
    down = nn_dot(turned[pl.ds(base, down_rows), :], picked[:, :half]).astype(BF16)
    left = []
    for k in ORDER:
        base = pl.multiple_of(wide + owner * 8 * short + core * 4 * short + (z ^ k) * short, 16)
        left.append(turned[pl.ds(base, short), :])
    out = nn_dot(jnp.concatenate(left, axis=0), picked[:, half:]).astype(BF16)
    first = dim // 128 * short

    def store(ref):
        for j in range(4):
            for t in range(dim // 128):
                ref[0, j, t * short : (t + 1) * short, :] = out[
                    j * short : (j + 1) * short, t * 128 : (t + 1) * 128
                ]
            ref[0, j, first:, :] = down[:, j * 128 : (j + 1) * 128]

    pl.when(at < 2)(lambda: store(a_ref))
    pl.when(at == 2)(lambda: store(b_ref))
    pl.when(at == 3)(lambda: store(c_ref))


def run_rest_grad(place, keep, other, hidden):
    tokens = keep.shape[0]
    wide = padded(hidden)
    dim = (keep.shape[1] - wide) // 3
    tall = dim // 128 * (dim // 32) + hidden // 4
    whole = pl.BlockSpec(keep.shape, lambda i: (0, 0))
    return pl.pallas_call(
        functools.partial(rest_grad, hidden),
        name="rest_grad",
        out_shape=tuple(jax.ShapeDtypeStruct((n, 4, tall, 128), BF16) for n in (2, 1, 1)),
        grid=(4,),
        in_specs=[smem_spec(), whole, whole],
        out_specs=[
            pl.BlockSpec((1, 4, tall, 128), lambda i: (jnp.minimum(i, 1), 0, 0, 0)),
            pl.BlockSpec((1, 4, tall, 128), lambda i: (0, 0, 0, 0)),
            pl.BlockSpec((1, 4, tall, 128), lambda i: (0, 0, 0, 0)),
        ],
        scratch_shapes=[
            pltpu.VMEM((wide + dim, 2 * tokens), BF16),
            pltpu.VMEM((2 * tokens, dim + dim // 2), BF16),
        ],
        compiler_params=params(),
        cost_estimate=cost(4e9, 10e6),
    )(place, keep, other)


def unpack_in(place_ref, *refs):
    pieces, w_ref, out_ref, sum_ref = refs[:4], refs[4], refs[5], refs[6]
    at = pl.program_id(0)
    for q, ref in enumerate(pieces):

        @pl.when(at // 2 == q)
        def _(ref=ref):
            value = ref[0].astype(F32)
            out_ref[...] = value
            sum_ref[...] = jnp.sum(value * w_ref[...].astype(F32), axis=1, keepdims=True)


def row_block(i, place_ref):
    side = jnp.where(i < 4, place_ref[7], 1 - place_ref[7])
    order = jnp.where(i % 4 == 1, 2, jnp.where(i % 4 == 2, 1, i % 4))
    return (side * 4 + (place_ref[8] ^ order), 0)


def run_unpack_in(place, pieces, weight):
    rows, columns = weight.shape
    short = rows // 8
    specs = [
        pl.BlockSpec((1, short, columns), lambda i, p, q=q: (jnp.clip(i - 2 * q, 0, 1), 0, 0))
        for q in range(4)
    ]
    block = pl.BlockSpec((short, columns), row_block)
    return pl.pallas_call(
        unpack_in,
        name="unpack_in",
        out_shape=(jax.ShapeDtypeStruct((rows, columns), F32), jax.ShapeDtypeStruct((rows, 1), F32)),
        grid_spec=pltpu.PrefetchScalarGridSpec(
            num_scalar_prefetch=1,
            grid=(8,),
            in_specs=specs + [block],
            out_specs=[block, pl.BlockSpec((short, 1), row_block)],
        ),
        compiler_params=params(),
        cost_estimate=cost(1e7, 11e6),
    )(place, *pieces, weight)


def sources(place_ref, pieces):
    core, z = place_ref[7], place_ref[8]
    for q, ref in enumerate(pieces):
        for at in range(2):
            side = core if q < 2 else 1 - core
            yield ref.at[at], side, z ^ ORDER[2 * (q % 2) + at]


def unpack_rest(place_ref, *refs):
    pieces, out_ref, down_ref = refs[:4], refs[4], refs[5]
    dim = out_ref.shape[1]
    short = dim // 32
    first = dim // 128 * short
    for ref, side, z in sources(place_ref, pieces):
        base = pl.multiple_of(side * 4 * short + z * short, 16)
        for t in range(dim // 128):
            out_ref[pl.ds(base, short), t * 128 : (t + 1) * 128] = ref[
                t * short : (t + 1) * short, :
            ].astype(F32)
        left = pl.multiple_of(side * (dim // 2) + z * 128, 128)
        down_ref[:, pl.ds(left, 128)] = ref[first:, :].astype(F32)


def run_unpack_rest(place, pieces, out_shape, down_shape):
    return pl.pallas_call(
        unpack_rest,
        name="unpack_rest",
        out_shape=(jax.ShapeDtypeStruct(out_shape, F32), jax.ShapeDtypeStruct(down_shape, F32)),
        in_specs=[smem_spec()] + [vmem_spec()] * 4,
        out_specs=[vmem_spec()] * 2,
        compiler_params=params(),
        cost_estimate=cost(1e7, 6e6),
    )(place, *pieces)


def unpack_qkv(place_ref, *refs):
    pieces, w_ref, out_ref, sum_ref = refs[:4], refs[4], refs[5], refs[6]
    width = pieces[0].shape[2] // 3
    dim = out_ref.shape[1] // 3
    total = jnp.zeros_like(sum_ref)
    for ref, side, z in sources(place_ref, pieces):
        for part in range(3):
            left = pl.multiple_of(part * dim + (z * 2 + side) * width, 128)
            value = ref[:, part * width : (part + 1) * width].astype(F32)
            out_ref[:, pl.ds(left, width)] = value
            weight = w_ref[:, pl.ds(left, width)].astype(F32)
            total = total + jnp.sum(value * weight, axis=1, keepdims=True)
    sum_ref[...] = total


def run_unpack_qkv(place, pieces, weight):
    return pl.pallas_call(
        unpack_qkv,
        name="unpack_qkv",
        out_shape=(
            jax.ShapeDtypeStruct(weight.shape, F32),
            jax.ShapeDtypeStruct((weight.shape[0], 1), F32),
        ),
        in_specs=[smem_spec()] + [vmem_spec()] * 5,
        out_specs=[vmem_spec()] * 2,
        compiler_params=params(),
        cost_estimate=cost(1e7, 7e6),
    )(place, *pieces, weight)


def input_grad(x_ref, gmid_ref, gain_ref, *refs):
    parts, out_ref = refs[:-1], refs[-1]
    x = x_ref[...].astype(F32)
    center = x - jnp.mean(x, axis=-1, keepdims=True)
    spread = jnp.mean(center * center, axis=-1, keepdims=True)
    scale = lax.rsqrt(spread + NORM_EPS)
    normal = center * scale
    e = sum(part[...].astype(F32) for part in parts) * gain_ref[...]
    pull = e - jnp.mean(e, axis=-1, keepdims=True) - normal * jnp.mean(e * normal, axis=-1, keepdims=True)
    out_ref[...] = (gmid_ref[...] + scale * pull).astype(BF16)


def run_input_grad(x, gmid, gain, parts):
    rows, dim = x.shape
    tall = rows // 4
    block = pl.BlockSpec((tall, dim), lambda i: (i, 0))
    return pl.pallas_call(
        input_grad,
        name="input_grad",
        out_shape=jax.ShapeDtypeStruct((rows, dim), BF16),
        grid=(4,),
        in_specs=[block, block, pl.BlockSpec((1, dim), lambda i: (0, 0))] + [block] * len(parts),
        out_specs=block,
        compiler_params=params(),
        cost_estimate=cost(1e8, 5e6),
    )(x, gmid, gain, *parts)


def sequence_layout(lengths, order, group):
    ends = jnp.cumsum(lengths)
    starts = ends - lengths
    index = jnp.arange(group, dtype=jnp.int32)
    passed = index[:, None] >= ends[None, :]
    start = jnp.sum(jnp.where(passed, lengths[None, :], 0), axis=1).astype(jnp.int32)
    inside = jnp.logical_and(index[:, None] >= starts[None, :], jnp.logical_not(passed))
    end = jnp.sum(jnp.where(inside, ends[None, :], 0), axis=1).astype(jnp.int32)
    places = index - start
    half = HD // 2
    speeds = jnp.power(F32(ROPE_BASE), -2.0 * jnp.arange(half, dtype=F32) / HD)
    angles = speeds[:, None] * places.astype(F32)[None, :]
    keys = (start[::WIDE] // BLOCK, (end[WIDE - 1 :: WIDE] + BLOCK - 1) // BLOCK)
    queries = (start[::BLOCK] // WIDE, (end[BLOCK - 1 :: BLOCK] + WIDE - 1) // WIDE)
    return (keys, queries, order[None, :], start[None, :], end[None, :], jnp.cos(angles), jnp.sin(angles))


def local(tokens, seq_lengths, seq_order, norm_one, w_qkv, w_out, norm_two, w_in, w_down, cotangent):
    seq_count = lax.axis_size("seq")
    fsdp_count = lax.axis_size("fsdp")
    levels = fsdp_count.bit_length() - 1
    count = fsdp_count - 1
    seq_at = lax.axis_index("seq")
    fsdp_at = lax.axis_index("fsdp")
    core = seq_at % 2
    x = tokens[0]
    cot = cotangent[0]
    rows, dim = x.shape
    group = rows * seq_count
    heads = dim // HD // seq_count
    width = heads * HD
    hidden = w_in.shape[1] // 2
    counts = (seq_count, fsdp_count)
    swap = functools.partial(core_swap, seq_count=seq_count)

    keys = [jnp.array([plane_mask(c, key, levels) for key in range(1, fsdp_count)], jnp.int32) for c in (0, 1)]
    mine = fsdp_at ^ jnp.where(core == 0, keys[0], keys[1])
    other = fsdp_at ^ jnp.where(core == 0, keys[1], keys[0])
    place = jnp.stack([fsdp_at, *mine, *other, core, seq_at // 2]).astype(jnp.int32)
    regular = fsdp_count == 4 and seq_count == 8 and w_down.shape[0] % 16 == 0 and dim == 1024

    layout = sequence_layout(seq_lengths[0], seq_order[0], group)
    if regular:
        chunks = [x, mixed_swap(x, 1, seq_count), mixed_swap(x, 0, seq_count)]
        chunks.append(mixed_swap(after(chunks[1], chunks[2], layout[5], layout[6]), 0, seq_count))
        chunks += [swap(chunk) for chunk in chunks]
    else:
        chunks = [lax.all_gather(x, "seq", axis=0, tiled=False)]
    own_heads = jnp.concatenate(
        [lax.dynamic_slice_in_dim(w_qkv, part * dim + seq_at * width, width, 1) for part in range(3)], axis=1
    )
    gains = jnp.stack([norm_one, norm_two])
    if regular:
        extra = jnp.pad(gains, ((0, 14), (0, 3 * width - gains.shape[1])))
        own_heads = jnp.concatenate([own_heads, extra], axis=0)
        head_pieces = [own_heads] + [plane_swap(own_heads, phase, *counts) for phase in range(2)]
        head_pieces.append(plane_swap(head_pieces[1], 1, *counts))
    else:
        head_pieces = [
            lax.all_gather(own_heads, "fsdp", axis=0, tiled=True),
            lax.all_gather(gains, "fsdp", axis=1, tiled=True).astype(F32),
        ]
    first_piece, second_piece = run_pack_pieces(place, w_in, w_out, w_down, regular)
    if regular:
        first_piece, second_piece = after(first_piece, *head_pieces[1:3]), after(second_piece, *head_pieces[1:])
    first_a, second_a = plane_swap(first_piece, 0, *counts), plane_swap(second_piece, 0, *counts)
    first = plane_gather_rest(first_piece, first_a, *counts, second_a)
    second = plane_gather_rest(second_piece, second_a, *counts, first_a)
    left = dim

    gains, w_heads, normed, packed, att, out_t, lse = run_attention_forward(place, chunks, head_pieces, layout, heads)
    gain_one, gain_two = gains[:1], gains[1:]
    att_done = lax.all_to_all(att, "seq", split_axis=0, concat_axis=0, tiled=True)
    first = first + [swap(first[0])] + [swap(after(piece, att)) for piece in first[1:]]
    if regular:
        downs = [w_down] + first
    else:
        downs = [lax.all_gather(w_down, "fsdp", axis=0, tiled=True)]
    grad_hidden = run_hidden_grad(place, cot, downs, left, hidden)
    second = second + [swap(second[0])] + [swap(after(piece, att_done, grad_hidden)) for piece in second[1:]]
    att = att_done
    middle, gmid, send, keep, gatt = run_feed_forward(
        place, x, att, cot, gain_two, grad_hidden, w_out, w_in, first, second, hidden
    )
    dout = lax.all_to_all(gatt, "seq", split_axis=0, concat_axis=0, tiled=True)
    reduce = functools.partial(plane_reduce, seq_count=seq_count, fsdp_count=fsdp_count)
    send_other, keep_other = swap(send), swap(keep)
    wide = padded(hidden)
    if regular:
        short = w_in.shape[0] // 8
        in_a, in_b, in_c = run_in_grad(place, send, send_other, hidden)
        in_a = plane_swap(in_a, 1, *counts)
        packed = after(packed, in_b)

    grads, *shares = run_attention_backward(place, dout, packed, out_t, lse, w_heads, layout, heads, regular)
    each = w_qkv.shape[0]
    if regular:
        in_sum = after(added(in_b[0], in_a[1]), grads)
        in_second = plane_swap(in_sum, 0, *counts)
        got, share = swap(shares[0]), shares[1]
        token_sum = added(share[2:], got[2:])
        token_z1 = mixed_swap(token_sum, 0, seq_count)
        rest_a, rest_b, rest_c = run_rest_grad(place, keep, after(keep_other, in_sum, token_sum), hidden)
        rest_a = plane_swap(rest_a, 1, *counts)
        gw_heads = run_qkv_weight_grad(place, normed, after(grads, rest_b), regular)
        in_parts = [p.reshape(4, short, 2 * hidden) for p in (in_c[0], in_a[0], in_second)]
        in_z1 = line_swap(after(added(*(p[2:] for p in in_parts)), gw_heads[1]), 0, seq_count)
        rest_sum = added(rest_b[0], rest_a[1])
        rest_second = plane_swap(rest_sum, 0, *counts)
        rest_parts = (rest_c[0], rest_a[0], rest_second)
        layer_out = run_layer_result(place, middle, after(keep, rest_sum), downs, left, hidden)
        token_z2 = mixed_swap(added(share[1], got[1], token_z1[1]), 1, seq_count)
        grad_tokens = run_input_grad(x, gmid, gain_one, [share[0], got[0], token_z1[0], token_z2])
        qkv_a, qkv_b, qkv_c = gw_heads
        qkv_a = plane_swap(after(qkv_a, rest_second), 1, *counts)
        qkv_block = added(*reduce(qkv_a, qkv_b, qkv_c))
        in_z2 = line_swap(added(*(p[1] for p in in_parts), in_z1[1]), 1, seq_count)
        in_block = after(added(*(p[0] for p in in_parts), in_z1[0], in_z2), layer_out)
        rest_z1 = line_swap(after(added(*(p[2:] for p in rest_parts)), token_z2), 0, seq_count)
        rest_z2 = line_swap(after(added(*(p[1] for p in rest_parts), rest_z1[1]), in_z2), 1, seq_count)
        rest_block = added(*(p[0] for p in rest_parts), rest_z1[0], rest_z2)
        in_pieces = line_gather(in_block, seq_count)
        gw_in, sum_in = run_unpack_in(place, in_pieces, w_in)
        rest_pieces = line_gather(rest_block, seq_count, sum_in)
        qkv_pieces = line_gather(after(qkv_block, grad_tokens), seq_count, sum_in)
        gw_qkv, sum_qkv = run_unpack_qkv(place, qkv_pieces, w_qkv)
        gw_out, gw_down = run_unpack_rest(place, rest_pieces, w_out.shape, w_down.shape)
        sum_qkv = sum_qkv[:, 0]
        sum_in = sum_in[:, 0]
    else:
        layer_out = run_layer_result(place, middle, keep, downs, left, hidden)
        gw_heads = run_qkv_weight_grad(place, normed, grads, regular)
        share = lax.psum_scatter(shares[0].astype(F32), "seq", scatter_dimension=0, tiled=False)
        grad_tokens = run_input_grad(x, gmid, gain_one, [share])

        def total(left_rows, right_rows):
            full = lax.dot_general(
                left_rows, right_rows, (((0,), (0,)), ((), ())), preferred_element_type=F32
            )
            return lax.psum(lax.psum_scatter(full, "fsdp", scatter_dimension=0, tiled=True), "seq")

        gw_in = total(send[:, 2 * hidden :], send[:, : 2 * hidden])
        gw_down = total(keep[:, :hidden], cot)
        gw_out = total(keep[:, wide + dim : wide + 2 * dim], keep[:, wide : wide + dim])
        sum_in = jnp.sum(gw_in * w_in.astype(F32), axis=1)
        gw_heads = lax.all_to_all(gw_heads[0].reshape(fsdp_count, each, -1), "fsdp", 0, 0, tiled=True)
        gw_heads = jnp.sum(gw_heads.astype(F32), axis=0).astype(BF16)
        gw_qkv = lax.all_gather(gw_heads, "seq", axis=0, tiled=False).reshape(seq_count, each, 3, width)
        gw_qkv = gw_qkv.transpose(1, 2, 0, 3).reshape(each, 3 * dim).astype(F32)
        sum_qkv = jnp.sum(gw_qkv * w_qkv.astype(F32), axis=1)

    grad_one = sum_qkv / norm_one.astype(F32)
    grad_two = sum_in / norm_two.astype(F32)
    return (layer_out[None], grad_tokens[None], grad_one, gw_qkv, gw_out, grad_two, gw_in, gw_down)


def solution(mesh):
    tokens = P("fsdp", "seq", None)
    rows = P("fsdp", None)
    return jax.shard_map(
        local,
        mesh=mesh,
        in_specs=(tokens, rows, rows, P("fsdp"), rows, rows, P("fsdp"), rows, rows, tokens),
        out_specs=(tokens, tokens, P("fsdp"), rows, rows, P("fsdp"), rows, rows),
        check_vma=False,
    )
```
